32 devices in a mesh: groups: 2 (over y), rows: 4 (over z), cols: 2 (over x), sub: 2 (over core).
Axes of the slice: x: 2, y: 2, z: 4, core: 2. Of those that a mesh axis runs over, the one named last changes fastest.
Arguments:
- tile_index: int32 [64, 2], P(('groups', 'rows', 'cols', 'sub')), parts along dimension 0, may hold values from 0 to 7, as said below
- tile_values: bfloat16 [64, 256, 256], P(('groups', 'rows', 'cols', 'sub')), parts along dimension 0, may hold values from -0.125 to 0.125
- onsite_energy: float32 [4096], P(('groups', 'rows', 'cols')), parts along dimension 0, may hold values from 0.5 to 4
- start_block: float32 [4096, 64], P(('groups', 'rows', 'cols')), parts along dimension 0, may hold values from -6 to 6
- previous_block: float32 [4096, 64], P(('groups', 'rows', 'cols')), parts along dimension 0, may hold values from -6 to 6
- previous_coupling: float32 [128, 64], P('groups'), parts along dimension 0, may hold values from -0.6 to 0.6
- stored_basis: float32 [8, 4096, 64], P('sub', ('groups', 'rows', 'cols')), parts along dimension 1, may hold values from -6 to 6
Outputs:
- new_blocks: float32 [1, 4096, 64], P(None, ('groups', 'rows', 'cols')), parts along dimension 1
- diagonal_blocks: float32 [1, 128, 64], P(None, 'groups'), parts along dimension 1
- coupling_blocks: float32 [1, 128, 64], P(None, 'groups'), parts along dimension 1
The draws below stay inside these ranges and needn't reach their ends.
There are 2 independent parts, one for each index of `groups`. The reference program is written for one: setup_inputs(seed, part) draws one part's arguments, and reference() takes and returns one part's arrays. A program takes and returns all parts, laid end to end along the dimension named above; each array names one. Nothing has to cross between parts.
Inputs may be any that keep to these rules, and one draw needn't show every extreme that they name: `tile_index`: tile rows of a device's tiles lie in the rows of the operator that the device's index of rows and cols holds; tile columns lie in the rows held by some index of rows with the same index of cols. Tiles may repeat.
All inputs are finite; a program needn't handle non-finite values.
Results may differ from the reference program's by a relative error of at most 0.0019.
Values may be sent and summed in bfloat16 or wider, within the bound.
No kernel may reach another device: no remote copies, remote signals or barrier semaphores. Data moves between devices by JAX's collectives and lax.ppermute only.
A program may use at most 64 MiB of HBM per device.

```python
import math
import jax
import jax.numpy as jnp
from jax import lax

BLOCK = 64
TILE = 256
STORED = 8
ITERS = 1
TROWS_DEV = 1
TILES_DEV = 2
ORDER = 2048
TILES = 32
N_ROWS = 4
N_COLS = 2
N_SUB = 2


def draw_tile_index(key, part):
    count = TILES_DEV * N_ROWS * N_COLS * N_SUB
    device = jnp.arange(count, dtype=jnp.int32) // TILES_DEV
    own_slice = device // N_SUB
    own_column = own_slice % N_COLS
    first_key, second_key, third_key = jax.random.split(jax.random.fold_in(key, 17), 3)
    local_row = jax.random.randint(first_key, (count,), 0, TROWS_DEV)
    source_band = jax.random.randint(second_key, (count,), 0, N_ROWS)
    source_row = jax.random.randint(third_key, (count,), 0, TROWS_DEV)
    tile_row = own_slice * TROWS_DEV + local_row
    tile_column = (source_band * N_COLS + own_column) * TROWS_DEV + source_row
    return jnp.stack([tile_row, tile_column], axis=1).astype(jnp.int32)


def draw_stored_basis(key, part):
    subkeys = jax.random.split(jax.random.fold_in(key, 29), 3)
    private = jax.random.normal(subkeys[0], (STORED, ORDER, BLOCK), jnp.float32)
    common = jax.random.normal(subkeys[1], (ORDER, BLOCK), jnp.float32)
    mixing = jnp.eye(BLOCK, dtype=jnp.float32)[None] + 0.6 * jax.random.normal(subkeys[2], (STORED, BLOCK, BLOCK), jnp.float32) / jnp.sqrt(jnp.float32(BLOCK))
    blended = jnp.einsum('kib,kbc->kic', private, mixing, precision=lax.Precision.HIGHEST) * 0.857493
    values = 0.5 * blended + 0.866 * common[None]
    return jnp.clip(values, -6.0, 6.0).astype(jnp.float32)


def level_of(key, shape, cuts, low, largest):
    gain, own = 1.0, jax.random.fold_in(key, 6)
    for axis_at, shards_of in cuts:
        heights = jnp.exp(jax.random.uniform(jax.random.fold_in(own, axis_at), (shards_of,), jnp.float32, low / len(cuts), largest / len(cuts)))
        gain = gain * jnp.repeat(heights, shape[axis_at] // shards_of).reshape([-1 if axis == axis_at else 1 for axis in range(len(shape))])
    return gain


def gaussian(key, dims, deviation, limit, cuts=(), kind=jnp.bfloat16):
    loudness = level_of(key, dims, cuts, -0.22, 0.18) if cuts else 1.0
    result = jax.random.normal(key, dims, jnp.float32) * deviation * loudness
    return jnp.minimum(jnp.maximum(result, -limit), limit).astype(kind)


def setup_inputs(seed: int = 0, part: int = 0) -> dict:
    streams_of = jax.random.split(jax.random.key(seed), 8)
    own_keys = jax.random.split(jax.random.fold_in(streams_of[7], part), 8)
    tile_index = draw_tile_index(jax.random.fold_in(jax.random.fold_in(streams_of[7], part), 71), part)
    tile_values = gaussian(own_keys[1], (TILES, TILE, TILE), (4 * TILES_DEV * TILE // TROWS_DEV) ** -0.5, 0.125, ((0, 16),))
    onsite_energy = jnp.clip(jnp.exp(math.log(4.0) - 2.0794415 * jax.random.uniform(own_keys[2], (ORDER,), jnp.float32) ** level_of(own_keys[2], (ORDER,), ((0, 8),), -0.2, 0.2)), 0.5, 4.0)
    start_block = gaussian(own_keys[3], (ORDER, BLOCK), 1.0, 6.0, ((0, 8),), jnp.float32)
    previous_block = gaussian(own_keys[4], (ORDER, BLOCK), 1.0, 6.0, ((0, 8),), jnp.float32)
    previous_coupling = gaussian(own_keys[5], (BLOCK, BLOCK), 0.1, 0.6, (), jnp.float32)
    stored_basis = draw_stored_basis(jax.random.fold_in(jax.random.fold_in(streams_of[7], part), 71), part)
    return {"tile_index": tile_index, "tile_values": tile_values, "onsite_energy": onsite_energy, "start_block": start_block, "previous_block": previous_block, "previous_coupling": previous_coupling, "stored_basis": stored_basis}


highest = lax.Precision.HIGHEST

def apply_operator(tile_index, tile_values, onsite_energy, current):
    tile_rows = ORDER // TILE
    narrow = lax.optimization_barrier(current.astype(jnp.bfloat16))
    rounded = narrow.astype(jnp.float32).reshape(tile_rows, TILE, BLOCK)
    grouped_index = tile_index.reshape(-1, TILES_DEV, 2)
    grouped_values = tile_values.reshape(-1, TILES_DEV, TILE, TILE)

    def accumulate(total, item):
        indices, values = item
        values = values.astype(jnp.float32)
        pulled = jnp.einsum('kab,kbn->kan', values, rounded[indices[:, 1]], precision=highest)
        pushed = jnp.einsum('kab,kan->kbn', values, rounded[indices[:, 0]], precision=highest)
        total = total.at[indices[:, 0]].add(pulled)
        total = total.at[indices[:, 1]].add(pushed)
        return (total, None)
    initial = jnp.zeros((tile_rows, TILE, BLOCK), jnp.float32)
    total, unused = lax.scan(accumulate, initial, (grouped_index, grouped_values))
    return total.reshape(ORDER, BLOCK) + onsite_energy[:, None] * current

def reference(tile_index, tile_values, onsite_energy, start_block, previous_block, previous_coupling, stored_basis):
    current = start_block
    earlier = previous_block
    coupling = jnp.triu(previous_coupling)
    new_list = []
    diagonal_list = []
    coupling_list = []
    for iteration in range(ITERS):
        images = apply_operator(tile_index, tile_values, onsite_energy, current)
        images = images - jnp.dot(earlier, coupling.T, precision=highest)
        diagonal = jnp.dot(current.T, images, precision=highest) / ORDER
        images = images - jnp.dot(current, diagonal, precision=highest)
        projection = jnp.einsum('kib,ic->kbc', stored_basis, images, precision=highest) / ORDER
        images = images - jnp.einsum('kib,kbc->ic', stored_basis, projection, precision=highest)
        gram = jnp.dot(images.T, images, precision=highest) / ORDER
        lower_factor = jnp.linalg.cholesky(gram)
        following = lax.linalg.triangular_solve(lower_factor, images, left_side=False, lower=True, transpose_a=True)
        new_list.append(following)
        diagonal_list.append(diagonal)
        coupling_list.append(lower_factor.T)
        earlier = current
        coupling = lower_factor.T
        current = following
    return (jnp.stack(new_list), jnp.stack(diagonal_list), jnp.stack(coupling_list))
```

```python
import functools

import jax
import jax.numpy as jnp
from jax import lax
from jax.experimental import pallas as pl
from jax.experimental.pallas import tpu as pltpu
from jax.sharding import PartitionSpec as P

f32 = jnp.float32
bf16 = jnp.bfloat16
GROUP = 16
HIGHEST = lax.Precision.HIGHEST
GRANT = 16 * 1024 * 1024
NN = (((1,), (0,)), ((), ()))
NT = (((1,), (1,)), ((), ()))


def split(x):
    high = x.astype(bf16)
    return high, (x - high.astype(f32)).astype(bf16)


def dot_bf16(a, b, dims):
    return lax.dot_general(a, b, dims, preferred_element_type=f32)


def dot_split(a, b, dims):
    (ah, al), (bh, bl) = a, b
    return dot_bf16(ah, bh, dims) + dot_bf16(ah, bl, dims) + dot_bf16(al, bh, dims)


def dot_exact(a, b, dims):
    return lax.dot_general(a, b, dims, precision=HIGHEST, preferred_element_type=f32)


def fold(x, parts):
    rows = x.shape[0] // parts
    return jnp.concatenate([x[i * rows : (i + 1) * rows] for i in range(parts)], axis=1)


def unfold(x, parts):
    lanes = x.shape[1] // parts
    return jnp.concatenate([x[:, i * lanes : (i + 1) * lanes] for i in range(parts)], axis=0)


def call(kernel, outs, ins, scratch=(), work=40000000):
    spaces = {"v": pltpu.VMEM, "h": pltpu.HBM}
    return pl.pallas_call(
        kernel,
        out_shape=[jax.ShapeDtypeStruct(s, d) for s, d in outs],
        in_specs=[pl.BlockSpec(memory_space=spaces[c]) for c in ins],
        out_specs=[pl.BlockSpec(memory_space=pltpu.VMEM)] * len(outs),
        scratch_shapes=list(scratch),
        cost_estimate=pl.CostEstimate(flops=work, bytes_accessed=1000000, transcendentals=0),
        compiler_params=pltpu.CompilerParams(vmem_limit_bytes=GRANT),
    )


def prepare_kernel(
    x_hbm, e_hbm, p_hbm, c_hbm, s_hbm, t_hbm, i_hbm,
    base_ref, corr_ref, x_ref, xs_ref, ss_ref, t_ref, i_ref,
    e_ref, p_ref, c_ref, s_ref, sems,
):
    pairs = (
        (s_hbm, s_ref), (x_hbm, x_ref), (p_hbm, p_ref), (c_hbm, c_ref),
        (e_hbm, e_ref), (t_hbm, t_ref), (i_hbm, i_ref),
    )
    copies = [pltpu.make_async_copy(a, b, sems.at[k]) for k, (a, b) in enumerate(pairs)]
    for copy in copies:
        copy.start()
    for copy in copies[:5]:
        copy.wait()
    block = x_ref.shape[0]
    row = lax.broadcasted_iota(jnp.int32, (block, block), 0)
    column = lax.broadcasted_iota(jnp.int32, (block, block), 1)
    coupling = jnp.where(row <= column, c_ref[...], 0.0)
    x = x_ref[...]
    xs = split(x)
    ss = split(s_ref[...])
    for half in range(2):
        xs_ref[half] = xs[half]
        ss_ref[half] = ss[half]
    base_ref[...] = e_ref[...] * x - dot_split(split(coupling), split(p_ref[...]), NN)
    corr = dot_split(xs, ss, NT)
    chunk = corr_ref.shape[1]
    for band in range(corr_ref.shape[0]):
        corr_ref[band] = corr[band * chunk : (band + 1) * chunk]
    for copy in copies[5:]:
        copy.wait()


def tile_columns(index_refs, shape):
    found = []
    for ref in index_refs:
        index = ref[...]
        for k in range(ref.shape[0]):
            found.append(jnp.broadcast_to(index[k : k + 1, 1:2], shape))
    return found


def target_band(me, core, pair):
    return jnp.bitwise_xor(me, jnp.where(core == 0, pair[0], pair[1]))


def push_kernel(pairs, columns, i_ref, j_ref, xs_ref, corr_ref, t_ref, u_ref, *outs):
    block, rows = xs_ref.shape[1:]
    x = xs_ref[0]
    me, core = lax.axis_index("rows"), lax.axis_index("sub")
    targets = tile_columns((i_ref, j_ref), (block, rows))
    products = [dot_bf16(x, ref[k], NN) for ref in (t_ref, u_ref) for k in range(ref.shape[0])]

    def pushed(band):
        first = band * columns
        total = jnp.zeros((block, rows), f32)
        for target, product in zip(targets, products):
            inside = (target >= first) & (target < first + columns)
            total = total + jnp.where(inside, product, 0.0)
        return total

    parity = jnp.bitwise_and(me, 1)
    outs[0][...] = jnp.concatenate([pushed(me), corr_ref[parity]], axis=0)
    for ref, pair in zip(outs[1:], pairs):
        message = jnp.concatenate([x.astype(f32), pushed(target_band(me, core, pair))], axis=0)
        if pair[0] != pair[1]:
            ref[...] = message.astype(bf16)
        else:
            message = jnp.where(core == 0, message[:, : rows // 2], message[:, rows // 2 :])
            halves = [unfold(h.astype(f32), 2) for h in split(corr_ref[1 - parity])]
            ref[...] = jnp.concatenate([message, *halves], axis=0).astype(bf16)


def image_kernel(pairs, columns, parts, i_ref, j_ref, base_ref, xs_ref, ss_ref, t_ref, u_ref, own_ref, *refs):
    received, (y_ref, send_ref) = refs[:-2], refs[-2:]
    block, rows = base_ref.shape
    xs = (xs_ref[0], xs_ref[1])
    me, core = lax.axis_index("rows"), lax.axis_index("sub")
    y = base_ref[...] + own_ref[0:block]
    corr = own_ref[block:]
    blocks = [(me, xs[0].astype(f32))]
    for k, pair in enumerate(pairs):
        mine, other = received[2 * k][...].astype(f32), received[2 * k + 1][...].astype(f32)
        if pair[0] != pair[1]:
            found = [(target_band(me, core, pair), mine), (target_band(me, core, pair[::-1]), other)]
        else:
            parts_of = mine[2 * block :]
            count = parts_of.shape[0] // 2
            corr = corr + fold(parts_of[:count] + parts_of[count:], 2)
            mine, other = mine[: 2 * block], other[: 2 * block]
            first, second = jnp.where(core == 0, mine, other), jnp.where(core == 0, other, mine)
            found = [(jnp.bitwise_xor(me, pair[0]), jnp.concatenate([first, second], axis=1))]
        for band, message in found:
            blocks.append((band, message[0:block]))
            y = y + message[block:]
    tiles = [ref[k] for ref in (t_ref, u_ref) for k in range(ref.shape[0])]
    for target, tile in zip(tile_columns((i_ref, j_ref), (block, rows)), tiles):
        source = jnp.zeros((block, rows), f32)
        for band, held in blocks:
            first = band * columns
            inside = (target >= first) & (target < first + columns)
            source = jnp.where(inside, held, source)
        y = y + dot_bf16(source.astype(bf16), tile, NT)
    y_ref[...] = y
    halves = split(y)
    stored = dot_split(halves, (ss_ref[0], ss_ref[1]), NT)
    diagonal = fold(dot_split(halves, xs, NT), parts)
    middle = diagonal.shape[0] // 2
    diagonal = jnp.where(core == 0, diagonal[:middle], diagonal[middle:])
    send_ref[...] = jnp.concatenate([stored, diagonal, corr], axis=0)


def combine_kernel(block, small, mine_ref, other_ref, total_ref, send_ref):
    total = mine_ref[...] + other_ref[...]
    total_ref[...] = total
    high, low = split(total[block : block + small])
    message = [total[0:block], high.astype(f32), low.astype(f32), total[block + small :]]
    send_ref[...] = jnp.concatenate(message, axis=0).astype(bf16)


def project_kernel(steps, block, small, total_rows, total_ref, ss_ref, *refs):
    received, out_ref = refs[:-1], refs[-1]
    me, core = lax.axis_index("rows"), lax.axis_index("sub")
    total = total_ref[...]
    stored, diagonal = total[0:block], total[block : block + small]
    same, other = total[block + small :], jnp.zeros((block // 2, total.shape[1]), f32)
    for step, ref in zip(steps, received):
        message = ref[...].astype(f32)
        stored = stored + message[0:block]
        diagonal = diagonal + message[block : block + small]
        diagonal = diagonal + message[block + small : block + 2 * small]
        part = message[block + 2 * small :]
        if step % 2:
            other = other + part
        else:
            same = same + part
    even = jnp.bitwise_and(me, 1) == 0
    first, second = jnp.where(even, same, other), jnp.where(even, other, same)
    scale = 1.0 / total_rows
    weights = jnp.concatenate([stored, first, second], axis=0) * scale
    out_ref[0 : 2 * block, :] = dot_split(split(weights), (ss_ref[0], ss_ref[1]), NN)
    out_ref[2 * block : 2 * block + small, :] = jnp.where(core == 0, diagonal * scale, 0.0)
    out_ref[2 * block + small :, :] = jnp.where(core == 0, 0.0, diagonal * scale)


def gram_kernel(parts, mine_ref, other_ref, x_ref, y_ref, images_ref, send_ref, diagonal_ref):
    block = x_ref.shape[0]
    both = mine_ref[...] + other_ref[...]
    diagonal = unfold(both[2 * block :], parts)
    reduced = x_ref[...] - both[block : 2 * block]
    images = y_ref[...] - both[0:block] - dot_split(split(diagonal), split(reduced), NN)
    images_ref[...] = images
    diagonal_ref[...] = diagonal
    message = fold(dot_exact(images, images, NT), 2)
    for device in range(send_ref.shape[0]):
        send_ref[device] = message


def factor_kernel(total_rows, got_ref, images_ref, d_ref, following_ref, coupling_ref, diagonal_ref):
    block = images_ref.shape[0]
    half, lanes = block // 2, 2 * block
    gram = got_ref[0]
    for device in range(1, got_ref.shape[0]):
        gram = gram + got_ref[device]
    gram = gram * (1.0 / total_rows)
    row = lax.broadcasted_iota(jnp.int32, (block, lanes), 0)
    column = lax.broadcasted_iota(jnp.int32, (block, lanes), 1)
    left = column < block
    m = jnp.concatenate([gram, pltpu.roll(gram, block, 1)], axis=0)
    m = jnp.where(left, m, jnp.where(column == row + block, 1.0, 0.0))
    finished = []
    for start in range(0, block, GROUP):
        spread = [
            jnp.broadcast_to(m[:, start + p : start + p + 1], m.shape) for p in range(GROUP)
        ]
        for p in range(GROUP):
            at = p % 8
            root = lax.rsqrt(spread[p][at : at + 1])
            lower = spread[p] * root
            done = m[at : at + 1] * root
            finished.append(done)
            for q in range(p + 1, GROUP):
                pivot = q - p + at
                spread[q] = spread[q] - lower * lower[pivot : pivot + 1]
            m = m - lower * done
            if at == 7:
                m = m[8:]
                spread = [column[8:] for column in spread]
    done = jnp.concatenate(finished, axis=0)
    coupling_ref[...] = jnp.where((row <= column) & left, done, 0.0)[:, 0:block]
    inverse = jnp.where((row + block >= column) & ~left, done, 0.0)
    images = images_ref[...]
    following_ref[...] = dot_exact(inverse, jnp.concatenate([images, images], axis=0), NN)
    diagonal_ref[...] = d_ref[...].T


def exchange(x, axis, distance):
    return lax.ppermute(x, axis, [(i, i ^ distance) for i in range(lax.axis_size(axis))])


def local(
    tile_index,
    tile_values,
    onsite_energy,
    start_block,
    previous_block,
    previous_coupling,
    stored_basis,
):
    rows, block = start_block.shape
    bands, columns = lax.axis_size("rows"), lax.axis_size("cols")
    cores = lax.axis_size("sub")
    stored = stored_basis.shape[0]
    width = stored * block
    total_rows = rows * bands * columns
    peers = bands * columns
    parts = width // block
    chunk = block // 2
    assert rows == tile_values.shape[1] and cores == 2 and width == rows
    assert bands > 1 and columns > 1 and bands & (bands - 1) == 0 and columns & (columns - 1) == 0
    half = (block, rows)
    swap = [(0, 1), (1, 0)]
    other_tiles = lax.ppermute(tile_values, "sub", swap)
    other_index = lax.ppermute(tile_index, "sub", swap)
    base, corr, x, xs, ss, tiles, index = call(
        prepare_kernel,
        [
            (half, f32), ((2, chunk, width), f32), (half, f32), ((2,) + half, bf16),
            ((2, width, rows), bf16), (tile_values.shape, bf16), (tile_index.shape, jnp.int32),
        ],
        "hhhhhhh",
        [
            pltpu.VMEM((1, rows), f32), pltpu.VMEM(half, f32), pltpu.VMEM((block, block), f32),
            pltpu.VMEM((width, rows), f32), pltpu.SemaphoreType.DMA((7,)),
        ],
    )(
        *(
            pltpu.with_memory_space_constraint(a, pltpu.HBM)
            for a in (
                start_block.T, onsite_energy.reshape(1, rows), previous_block.T, previous_coupling,
                stored_basis.transpose(0, 2, 1).reshape(width, rows), tile_values, tile_index,
            )
        )
    )
    pairs = [(step, step - 1) for step in range(bands - 1, 1, -2)] + [(1, 1)]
    sends = call(
        functools.partial(push_kernel, pairs, columns),
        [((block + chunk, rows), f32)]
        + [((2 * block, rows) if a != b else (4 * block, rows // 2), bf16) for a, b in pairs],
        "vvvvvv",
    )(index, other_index, xs, corr, tiles, other_tiles)
    received = []
    for send, pair in zip(sends[1:], pairs):
        moves = [(2 * r + c, 2 * (r ^ pair[c]) + c) for r in range(bands) for c in range(2)]
        received.append(lax.ppermute(send, ("rows", "sub"), moves))
    received = [y for x in received for y in (x, lax.ppermute(x, "sub", swap))]
    small = block // parts // 2
    y, mine = call(
        functools.partial(image_kernel, pairs, columns, parts),
        [(half, f32), ((block + small + chunk, rows), f32)],
        "v" * (8 + len(received)),
    )(index, other_index, base, xs, ss, tiles, other_tiles, sends[0], *received)
    distances = [2**k for k in range(columns.bit_length() - 1)]
    for distance in distances[:-1]:
        mine = mine + exchange(mine, "cols", distance)
    total, send = call(
        functools.partial(combine_kernel, block, small),
        [(mine.shape, f32), ((block + 2 * small + chunk, rows), bf16)],
        "vv",
    )(mine, exchange(mine, "cols", distances[-1]))
    steps = [*range(2, bands), 1]
    (mine,) = call(
        functools.partial(project_kernel, steps, block, small, total_rows),
        [((2 * block + 2 * small, rows), f32)],
        "v" * (1 + bands),
    )(total, ss, *(exchange(send, "rows", step) for step in steps))
    other = lax.ppermute(mine, "sub", swap)
    images, send, diagonal = call(
        functools.partial(gram_kernel, parts),
        [(half, f32), ((peers, block // 2, 2 * block), f32), ((block, block), f32)],
        "vvvv",
    )(mine, other, x, y)
    got = lax.all_to_all(send, ("rows", "cols"), 0, 0, tiled=True)
    following, coupling, diagonal = call(
        functools.partial(factor_kernel, total_rows),
        [(half, f32), ((block, block), f32), ((block, block), f32)],
        "vvv",
    )(got, images, diagonal)
    return following.T[None], diagonal[None], coupling[None]


def solution(mesh):
    return jax.shard_map(
        local,
        mesh=mesh,
        in_specs=(
            P(("groups", "rows", "cols", "sub"), None),
            P(("groups", "rows", "cols", "sub"), None, None),
            P(("groups", "rows", "cols")),
            P(("groups", "rows", "cols"), None),
            P(("groups", "rows", "cols"), None),
            P("groups", None),
            P("sub", ("groups", "rows", "cols"), None),
        ),
        out_specs=(
            P(None, ("groups", "rows", "cols"), None),
            P(None, "groups", None),
            P(None, "groups", None),
        ),
        check_vma=False,
    )
```

```python
import functools

import jax
import jax.numpy as jnp
from jax import lax
from jax.experimental import pallas as pl
from jax.experimental.pallas import tpu as pltpu
from jax.sharding import PartitionSpec as P

f32 = jnp.float32
bf16 = jnp.bfloat16
GROUP = 16
HIGHEST = lax.Precision.HIGHEST
GRANT = 16 * 1024 * 1024
NN = (((1,), (0,)), ((), ()))
NT = (((1,), (1,)), ((), ()))


def split(x):
    high = x.astype(bf16)
    return high, (x - high.astype(f32)).astype(bf16)


def dot_bf16(a, b, dims):
    return lax.dot_general(a, b, dims, preferred_element_type=f32)


def dot_split(a, b, dims):
    (ah, al), (bh, bl) = a, b
    return dot_bf16(ah, bh, dims) + dot_bf16(ah, bl, dims) + dot_bf16(al, bh, dims)


def dot_exact(a, b, dims):
    return lax.dot_general(a, b, dims, precision=HIGHEST, preferred_element_type=f32)


def fold(x, parts):
    rows = x.shape[0] // parts
    return jnp.concatenate([x[i * rows : (i + 1) * rows] for i in range(parts)], axis=1)


def unfold(x, parts):
    lanes = x.shape[1] // parts
    return jnp.concatenate([x[:, i * lanes : (i + 1) * lanes] for i in range(parts)], axis=0)


def call(kernel, outs, ins, scratch=(), work=40000000):
    spaces = {"v": pltpu.VMEM, "h": pltpu.HBM}
    return pl.pallas_call(
        kernel,
        out_shape=[jax.ShapeDtypeStruct(s, d) for s, d in outs],
        in_specs=[pl.BlockSpec(memory_space=spaces[c]) for c in ins],
        out_specs=[pl.BlockSpec(memory_space=pltpu.VMEM)] * len(outs),
        scratch_shapes=list(scratch),
        cost_estimate=pl.CostEstimate(flops=work, bytes_accessed=1000000, transcendentals=0),
        compiler_params=pltpu.CompilerParams(vmem_limit_bytes=GRANT),
    )


def prepare_kernel(
    x_hbm, e_hbm, p_hbm, c_hbm, s_hbm, t_hbm, i_hbm,
    base_ref, corr_ref, sx_ref, t_ref, i_ref,
    x_ref, e_ref, p_ref, c_ref, s_ref, sems,
):
    pairs = (
        (s_hbm, s_ref), (x_hbm, x_ref), (p_hbm, p_ref), (c_hbm, c_ref),
        (e_hbm, e_ref), (t_hbm, t_ref), (i_hbm, i_ref),
    )
    copies = [pltpu.make_async_copy(a, b, sems.at[k]) for k, (a, b) in enumerate(pairs)]
    for copy in copies:
        copy.start()
    for copy in copies[:5]:
        copy.wait()
    block = x_ref.shape[0]
    row = lax.broadcasted_iota(jnp.int32, (block, block), 0)
    column = lax.broadcasted_iota(jnp.int32, (block, block), 1)
    coupling = jnp.where(row <= column, c_ref[...], 0.0)
    x = x_ref[...]
    xs = split(x)
    ss = split(s_ref[...])
    for half in range(2):
        sx_ref[half] = jnp.concatenate([ss[half], xs[half]], axis=0)
    base_ref[...] = e_ref[...] * x - dot_split(split(coupling), split(p_ref[...]), NN)
    corr = dot_split(xs, ss, NT)
    chunk = corr_ref.shape[1]
    for band in range(corr_ref.shape[0]):
        corr_ref[band] = corr[band * chunk : (band + 1) * chunk]
    for copy in copies[5:]:
        copy.wait()


def tile_columns(index_refs, shape):
    found = []
    for ref in index_refs:
        index = ref[...]
        for k in range(ref.shape[0]):
            found.append(jnp.broadcast_to(index[k : k + 1, 1:2], shape))
    return found


def target_band(me, core, pair):
    return jnp.bitwise_xor(me, jnp.where(core == 0, pair[0], pair[1]))


def push_kernel(pairs, columns, i_ref, j_ref, sx_ref, corr_ref, t_ref, u_ref, *outs):
    width, rows = corr_ref.shape[2], sx_ref.shape[2]
    block = sx_ref.shape[1] - width
    x = sx_ref[0, width:]
    me, core = lax.axis_index("rows"), lax.axis_index("sub")
    targets = tile_columns((i_ref, j_ref), (block, rows))
    products = [dot_bf16(x, ref[k], NN) for ref in (t_ref, u_ref) for k in range(ref.shape[0])]

    def pushed(band):
        first = band * columns
        total = jnp.zeros((block, rows), f32)
        for target, product in zip(targets, products):
            inside = (target >= first) & (target < first + columns)
            total = total + jnp.where(inside, product, 0.0)
        return total

    parity = jnp.bitwise_and(me, 1)
    outs[0][...] = jnp.concatenate([pushed(me), corr_ref[parity]], axis=0)
    for ref, pair in zip(outs[1:], pairs):
        message = jnp.concatenate([x.astype(f32), pushed(target_band(me, core, pair))], axis=0)
        if pair[0] != pair[1]:
            ref[...] = message.astype(bf16)
        else:
            message = jnp.where(core == 0, message[:, : rows // 2], message[:, rows // 2 :])
            halves = [unfold(h.astype(f32), 2) for h in split(corr_ref[1 - parity])]
            ref[...] = jnp.concatenate([message, *halves], axis=0).astype(bf16)


def image_kernel(pairs, columns, i_ref, j_ref, base_ref, sx_ref, t_ref, u_ref, own_ref, *refs):
    received, send_ref = refs[:-1], refs[-1]
    block, rows = base_ref.shape
    me, core = lax.axis_index("rows"), lax.axis_index("sub")
    y = base_ref[...] + own_ref[0:block]
    corr = own_ref[block:]
    blocks = [(me, sx_ref[0, sx_ref.shape[1] - block :].astype(f32))]
    for k, pair in enumerate(pairs):
        mine, other = received[2 * k][...].astype(f32), received[2 * k + 1][...].astype(f32)
        if pair[0] != pair[1]:
            found = [(target_band(me, core, pair), mine), (target_band(me, core, pair[::-1]), other)]
        else:
            parts_of = mine[2 * block :]
            count = parts_of.shape[0] // 2
            corr = corr + fold(parts_of[:count] + parts_of[count:], 2)
            mine, other = mine[: 2 * block], other[: 2 * block]
            first, second = jnp.where(core == 0, mine, other), jnp.where(core == 0, other, mine)
            found = [(jnp.bitwise_xor(me, pair[0]), jnp.concatenate([first, second], axis=1))]
        for band, message in found:
            blocks.append((band, message[0:block]))
            y = y + message[block:]
    tiles = [ref[k] for ref in (t_ref, u_ref) for k in range(ref.shape[0])]
    for target, tile in zip(tile_columns((i_ref, j_ref), (block, rows)), tiles):
        source = jnp.zeros((block, rows), f32)
        for band, held in blocks:
            first = band * columns
            inside = (target >= first) & (target < first + columns)
            source = jnp.where(inside, held, source)
        y = y + dot_bf16(source.astype(bf16), tile, NT)
    send_ref[0:block, :] = y
    send_ref[block:, :] = corr


def pack(total, block, small):
    high, low = split(total[block : block + small])
    message = [total[0:block], high.astype(f32), low.astype(f32), total[block + small :]]
    return jnp.concatenate(message, axis=0).astype(bf16)


def inner_kernel(block, parts, mine_ref, other_ref, sx_ref, sy_ref, total_ref, *send_refs):
    width = sx_ref.shape[1] - block
    stored = diagonal = 0.0
    for y_ref, s_ref in ((mine_ref, sx_ref), (other_ref, sy_ref)):
        halves = split(y_ref[0:block])
        stored = stored + dot_split(halves, (s_ref[0, :width], s_ref[1, :width]), NT)
        diagonal = diagonal + dot_split(halves, (s_ref[0, width:], s_ref[1, width:]), NT)
    corr = mine_ref[block:] + other_ref[block:]
    total = jnp.concatenate([stored, fold(diagonal, parts), corr], axis=0)
    total_ref[...] = total
    for ref in send_refs:
        ref[...] = pack(total, block, block // parts)


def project_kernel(steps, block, parts, total_rows, total_ref, sx_ref, sy_ref, *refs):
    received, (out_ref, diagonal_ref) = refs[:-2], refs[-2:]
    me, core = lax.axis_index("rows"), lax.axis_index("sub")
    small = block // parts
    total = total_ref[...]
    stored, diagonal = total[0:block], total[block : block + small]
    same, other = total[block + small :], jnp.zeros((block // 2, total.shape[1]), f32)
    for step, ref in zip(steps, received):
        message = ref[...].astype(f32)
        stored = stored + message[0:block]
        diagonal = diagonal + message[block : block + small]
        diagonal = diagonal + message[block + small : block + 2 * small]
        part = message[block + 2 * small :]
        if step % 2:
            other = other + part
        else:
            same = same + part
    even = jnp.bitwise_and(me, 1) == 0
    corr = jnp.concatenate([jnp.where(even, same, other), jnp.where(even, other, same)], axis=0)
    scale = 1.0 / total_rows
    diagonal = unfold(diagonal * scale, parts)
    diagonal_ref[...] = diagonal
    projection = stored * scale - dot_split(split(diagonal), split(corr * scale), NN)
    weights = split(jnp.concatenate([projection, jnp.where(core == 0, diagonal, 0.0)], axis=1))
    for k, ref in enumerate((sx_ref, sy_ref)):
        out_ref[k * block : (k + 1) * block, :] = dot_split(weights, (ref[0], ref[1]), NN)


def gram_kernel(mine_ref, other_ref, y_ref, z_ref, images_ref, full_ref, half_ref):
    block = images_ref.shape[0]
    removed = mine_ref[...] + other_ref[...]
    images = y_ref[0:block] - removed[0:block]
    images_ref[...] = images
    gram = 0.0
    for x in (images, z_ref[0:block] - removed[block:]):
        halves = split(x)
        gram = gram + dot_split(halves, halves, NT)
    gram = fold(gram, 2)
    full_ref[...] = gram
    middle = half_ref.shape[0]
    half_ref[...] = jnp.where(lax.axis_index("sub") == 0, gram[:middle], gram[middle:])


def factor_kernel(pairs, total_rows, own_ref, images_ref, d_ref, *refs):
    received, (following_ref, coupling_ref, diagonal_ref) = refs[:-3], refs[-3:]
    block = images_ref.shape[0]
    lanes = 2 * block
    core = lax.axis_index("sub")
    gram = own_ref[...]
    for k, pair in enumerate(pairs):
        mine, other = received[2 * k][...], received[2 * k + 1][...]
        if pair[0] != pair[1]:
            gram = gram + (mine + other)
        else:
            first, second = jnp.where(core == 0, mine, other), jnp.where(core == 0, other, mine)
            gram = gram + jnp.concatenate([first, second], axis=0)
    gram = gram * (1.0 / total_rows)
    row = lax.broadcasted_iota(jnp.int32, (block, lanes), 0)
    column = lax.broadcasted_iota(jnp.int32, (block, lanes), 1)
    left = column < block
    m = jnp.concatenate([gram, pltpu.roll(gram, block, 1)], axis=0)
    m = jnp.where(left, m, jnp.where(column == row + block, 1.0, 0.0))
    finished = []
    for start in range(0, block, GROUP):
        spread = [
            jnp.broadcast_to(m[:, start + p : start + p + 1], m.shape) for p in range(GROUP)
        ]
        for p in range(GROUP):
            at = p % 8
            root = lax.rsqrt(spread[p][at : at + 1])
            lower = spread[p] * root
            done = m[at : at + 1] * root
            finished.append(done)
            for q in range(p + 1, GROUP):
                pivot = q - p + at
                spread[q] = spread[q] - lower * lower[pivot : pivot + 1]
            m = m - lower * done
            if at == 7:
                m = m[8:]
                spread = [column[8:] for column in spread]
    done = jnp.concatenate(finished, axis=0)
    coupling_ref[...] = jnp.where((row <= column) & left, done, 0.0)[:, 0:block]
    inverse = jnp.where((row + block >= column) & ~left, done, 0.0)
    images = images_ref[...]
    following_ref[...] = dot_exact(inverse, jnp.concatenate([images, images], axis=0), NN)
    diagonal_ref[...] = d_ref[...].T


def exchange(x, axis, distance):
    return lax.ppermute(x, axis, [(i, i ^ distance) for i in range(lax.axis_size(axis))])


def local(
    tile_index,
    tile_values,
    onsite_energy,
    start_block,
    previous_block,
    previous_coupling,
    stored_basis,
):
    rows, block = start_block.shape
    bands, columns = lax.axis_size("rows"), lax.axis_size("cols")
    cores = lax.axis_size("sub")
    stored = stored_basis.shape[0]
    width = stored * block
    total_rows = rows * bands * columns
    parts = width // block
    chunk = block // 2
    assert rows == tile_values.shape[1] and cores == 2 and width == rows
    assert bands > 1 and columns > 1 and bands & (bands - 1) == 0 and columns & (columns - 1) == 0
    half = (block, rows)
    swap = [(0, 1), (1, 0)]
    other_tiles = lax.ppermute(tile_values, "sub", swap)
    other_index = lax.ppermute(tile_index, "sub", swap)
    prepare = call(
        prepare_kernel,
        [
            (half, f32), ((2, chunk, width), f32), ((2, width + block, rows), bf16),
            (tile_values.shape, bf16), (tile_index.shape, jnp.int32),
        ],
        "hhhhhhh",
        [
            pltpu.VMEM(half, f32), pltpu.VMEM((1, rows), f32), pltpu.VMEM(half, f32),
            pltpu.VMEM((block, block), f32), pltpu.VMEM((width, rows), f32),
            pltpu.SemaphoreType.DMA((7,)),
        ],
    )
    sources = (
        start_block.T, onsite_energy.reshape(1, rows), previous_block.T, previous_coupling,
        stored_basis.transpose(0, 2, 1).reshape(width, rows), tile_values, tile_index,
    )
    base, corr, sx, tiles, index = prepare(
        *(pltpu.with_memory_space_constraint(a, pltpu.HBM) for a in sources)
    )
    pairs = [(step - 1, step) for step in range(bands - 1, 1, -2)] + [(1, 1)]

    def serve(sends):
        received = []
        for send, pair in zip(sends, pairs):
            moves = [(2 * r + c, 2 * (r ^ pair[c]) + c) for r in range(bands) for c in range(2)]
            received.append(lax.ppermute(send, ("rows", "sub"), moves))
        return [y for x in received for y in (x, lax.ppermute(x, "sub", swap))]

    sends = call(
        functools.partial(push_kernel, pairs, columns),
        [((block + chunk, rows), f32)]
        + [((2 * block, rows) if a != b else (4 * block, rows // 2), bf16) for a, b in pairs],
        "vvvvvv",
    )(index, other_index, sx, corr, tiles, other_tiles)
    sy = exchange(sx, "cols", 1)
    received = serve(sends[1:])
    (mine,) = call(
        functools.partial(image_kernel, pairs, columns),
        [((block + chunk, rows), f32)],
        "v" * (7 + len(received)),
    )(index, other_index, base, sx, tiles, other_tiles, sends[0], *received)
    other = exchange(mine, "cols", 1)
    distances = [2**k for k in range(1, columns.bit_length() - 1)]
    small = block // parts
    total, *send = call(
        functools.partial(inner_kernel, block, parts),
        [((block + small + chunk, rows), f32)]
        + [((block + 2 * small + chunk, rows), bf16)] * (not distances),
        "vvvv",
    )(mine, other, sx, sy)
    for distance in distances:
        total = total + exchange(total, "cols", distance)
    send = send[0] if send else pack(total, block, small)
    steps = [*range(2, bands), 1]
    removed, diagonal = call(
        functools.partial(project_kernel, steps, block, parts, total_rows),
        [((2 * block, rows), f32), ((block, block), f32)],
        "v" * (2 + bands),
    )(total, sx, sy, *(exchange(send, "rows", step) for step in steps))
    images, full, part = call(
        gram_kernel,
        [(half, f32), ((block // 2, 2 * block), f32), ((block // 4, 2 * block), f32)],
        "vvvv",
    )(removed, lax.ppermute(removed, "sub", swap), mine, other)
    for distance in distances:
        full = full + exchange(full, "cols", distance)
        middle = part.shape[0]
        part = jnp.where(lax.axis_index("sub") == 0, full[:middle], full[middle:])
    following, coupling, diagonal = call(
        functools.partial(factor_kernel, pairs, total_rows),
        [(half, f32), ((block, block), f32), ((block, block), f32)],
        "v" * (3 + 2 * len(pairs)),
    )(full, images, diagonal, *serve([full] * (len(pairs) - 1) + [part]))
    return following.T[None], diagonal[None], coupling[None]


def solution(mesh):
    return jax.shard_map(
        local,
        mesh=mesh,
        in_specs=(
            P(("groups", "rows", "cols", "sub"), None),
            P(("groups", "rows", "cols", "sub"), None, None),
            P(("groups", "rows", "cols")),
            P(("groups", "rows", "cols"), None),
            P(("groups", "rows", "cols"), None),
            P("groups", None),
            P("sub", ("groups", "rows", "cols"), None),
        ),
        out_specs=(
            P(None, ("groups", "rows", "cols"), None),
            P(None, "groups", None),
            P(None, "groups", None),
        ),
        check_vma=False,
    )
```

```python
import functools

import jax
import jax.numpy as jnp
from jax import lax
from jax.experimental import pallas as pl
from jax.experimental.pallas import tpu as pltpu
from jax.sharding import PartitionSpec as P

f32 = jnp.float32
bf16 = jnp.bfloat16
GROUP = 16
GRANT = 16 * 1024 * 1024
NN = (((1,), (0,)), ((), ()))
NT = (((1,), (1,)), ((), ()))


def split(x):
    high = x.astype(bf16)
    return high, (x - high.astype(f32)).astype(bf16)


def dot_bf16(a, b, dims):
    return lax.dot_general(a, b, dims, preferred_element_type=f32)


def dot_split(a, b, dims):
    (ah, al), (bh, bl) = a, b
    return dot_bf16(ah, bh, dims) + dot_bf16(ah, bl, dims) + dot_bf16(al, bh, dims)


def fold(x, parts):
    rows = x.shape[0] // parts
    return jnp.concatenate([x[i * rows : (i + 1) * rows] for i in range(parts)], axis=1)


def unfold(x, parts):
    lanes = x.shape[1] // parts
    return jnp.concatenate([x[:, i * lanes : (i + 1) * lanes] for i in range(parts)], axis=0)


def call(kernel, outs, ins, scratch=(), work=40000000):
    spaces = {"v": pltpu.VMEM, "h": pltpu.HBM}
    return pl.pallas_call(
        kernel,
        out_shape=[jax.ShapeDtypeStruct(s, d) for s, d in outs],
        in_specs=[pl.BlockSpec(memory_space=spaces[c]) for c in ins],
        out_specs=[pl.BlockSpec(memory_space=pltpu.VMEM)] * len(outs),
        scratch_shapes=list(scratch),
        cost_estimate=pl.CostEstimate(flops=work, bytes_accessed=1000000, transcendentals=0),
        compiler_params=pltpu.CompilerParams(vmem_limit_bytes=GRANT),
    )


def prepare_kernel(
    x_hbm, e_hbm, p_hbm, c_hbm, s_hbm, t_hbm, i_hbm,
    base_ref, corr_ref, sx_ref, t_ref, i_ref,
    x_ref, e_ref, p_ref, c_ref, s_ref, sems,
):
    pairs = (
        (s_hbm, s_ref), (x_hbm, x_ref), (p_hbm, p_ref), (c_hbm, c_ref),
        (e_hbm, e_ref), (t_hbm, t_ref), (i_hbm, i_ref),
    )
    copies = [pltpu.make_async_copy(a, b, sems.at[k]) for k, (a, b) in enumerate(pairs)]
    for copy in copies:
        copy.start()
    for copy in copies[:5]:
        copy.wait()
    block = x_ref.shape[0]
    row = lax.broadcasted_iota(jnp.int32, (block, block), 0)
    column = lax.broadcasted_iota(jnp.int32, (block, block), 1)
    coupling = jnp.where(row <= column, c_ref[...], 0.0)
    x = x_ref[...]
    xs = split(x)
    ss = split(s_ref[...])
    for half in range(2):
        sx_ref[half] = jnp.concatenate([ss[half], xs[half]], axis=0)
    base_ref[...] = e_ref[...] * x - dot_split(split(coupling), split(p_ref[...]), NN)
    corr = dot_split(xs, ss, NT)
    chunk = corr_ref.shape[1]
    for band in range(corr_ref.shape[0]):
        corr_ref[band] = corr[band * chunk : (band + 1) * chunk]
    for copy in copies[5:]:
        copy.wait()


def tile_columns(index_refs, shape):
    found = []
    for ref in index_refs:
        index = ref[...]
        for k in range(ref.shape[0]):
            found.append(jnp.broadcast_to(index[k : k + 1, 1:2], shape))
    return found


def target_band(me, core, pair):
    return jnp.bitwise_xor(me, jnp.where(core == 0, pair[0], pair[1]))


def push_kernel(pairs, columns, i_ref, j_ref, sx_ref, corr_ref, t_ref, u_ref, *outs):
    width, rows = corr_ref.shape[2], sx_ref.shape[2]
    block = sx_ref.shape[1] - width
    x = sx_ref[0, width:]
    me, core = lax.axis_index("rows"), lax.axis_index("sub")
    targets = tile_columns((i_ref, j_ref), (block, rows))
    products = [dot_bf16(x, ref[k], NN) for ref in (t_ref, u_ref) for k in range(ref.shape[0])]

    def pushed(band):
        first = band * columns
        total = jnp.zeros((block, rows), f32)
        for target, product in zip(targets, products):
            inside = (target >= first) & (target < first + columns)
            total = total + jnp.where(inside, product, 0.0)
        return total

    parity = jnp.bitwise_and(me, 1)
    outs[0][...] = jnp.concatenate([pushed(me), corr_ref[parity]], axis=0)
    for ref, pair in zip(outs[1:], pairs):
        message = jnp.concatenate([x.astype(f32), pushed(target_band(me, core, pair))], axis=0)
        if pair[0] != pair[1]:
            ref[...] = message.astype(bf16)
        else:
            message = jnp.where(core == 0, message[:, : rows // 2], message[:, rows // 2 :])
            halves = [unfold(h.astype(f32), 2) for h in split(corr_ref[1 - parity])]
            ref[...] = jnp.concatenate([message, *halves], axis=0).astype(bf16)


def image_kernel(pairs, columns, i_ref, j_ref, base_ref, sx_ref, t_ref, u_ref, own_ref, *refs):
    received, send_ref = refs[:-1], refs[-1]
    block, rows = base_ref.shape
    me, core = lax.axis_index("rows"), lax.axis_index("sub")
    y = base_ref[...] + own_ref[0:block]
    corr = own_ref[block:]
    blocks = [(me, sx_ref[0, sx_ref.shape[1] - block :].astype(f32))]
    for k, pair in enumerate(pairs):
        mine, other = received[2 * k][...].astype(f32), received[2 * k + 1][...].astype(f32)
        if pair[0] != pair[1]:
            found = [(target_band(me, core, pair), mine), (target_band(me, core, pair[::-1]), other)]
        else:
            parts_of = mine[2 * block :]
            count = parts_of.shape[0] // 2
            corr = corr + fold(parts_of[:count] + parts_of[count:], 2)
            mine, other = mine[: 2 * block], other[: 2 * block]
            first, second = jnp.where(core == 0, mine, other), jnp.where(core == 0, other, mine)
            found = [(jnp.bitwise_xor(me, pair[0]), jnp.concatenate([first, second], axis=1))]
        for band, message in found:
            blocks.append((band, message[0:block]))
            y = y + message[block:]
    tiles = [ref[k] for ref in (t_ref, u_ref) for k in range(ref.shape[0])]
    for target, tile in zip(tile_columns((i_ref, j_ref), (block, rows)), tiles):
        source = jnp.zeros((block, rows), f32)
        for band, held in blocks:
            first = band * columns
            inside = (target >= first) & (target < first + columns)
            source = jnp.where(inside, held, source)
        y = y + dot_bf16(source.astype(bf16), tile, NT)
    send_ref[0:block, :] = y
    send_ref[block:, :] = corr


def pack(total, block, small):
    high, low = split(total[block : block + small])
    message = [total[0:block], high.astype(f32), low.astype(f32), total[block + small :]]
    return jnp.concatenate(message, axis=0).astype(bf16)


def inner_kernel(block, parts, mine_ref, other_ref, sx_ref, sy_ref, total_ref, *send_refs):
    width = sx_ref.shape[1] - block
    stored = diagonal = 0.0
    for y_ref, s_ref in ((mine_ref, sx_ref), (other_ref, sy_ref)):
        halves = split(y_ref[0:block])
        stored = stored + dot_split(halves, (s_ref[0, :width], s_ref[1, :width]), NT)
        diagonal = diagonal + dot_split(halves, (s_ref[0, width:], s_ref[1, width:]), NT)
    corr = mine_ref[block:] + other_ref[block:]
    total = jnp.concatenate([stored, fold(diagonal, parts), corr], axis=0)
    total_ref[...] = total
    for ref in send_refs:
        ref[...] = pack(total, block, block // parts)


def project_kernel(steps, block, parts, total_rows, total_ref, sx_ref, sy_ref, *refs):
    received, (out_ref, diagonal_ref) = refs[:-2], refs[-2:]
    me, core = lax.axis_index("rows"), lax.axis_index("sub")
    small = block // parts
    total = total_ref[...]
    stored, diagonal = total[0:block], total[block : block + small]
    same, other = total[block + small :], jnp.zeros((block // 2, total.shape[1]), f32)
    for step, ref in zip(steps, received):
        message = ref[...].astype(f32)
        stored = stored + message[0:block]
        diagonal = diagonal + message[block : block + small]
        diagonal = diagonal + message[block + small : block + 2 * small]
        part = message[block + 2 * small :]
        if step % 2:
            other = other + part
        else:
            same = same + part
    even = jnp.bitwise_and(me, 1) == 0
    corr = jnp.concatenate([jnp.where(even, same, other), jnp.where(even, other, same)], axis=0)
    scale = 1.0 / total_rows
    diagonal = unfold(diagonal * scale, parts)
    diagonal_ref[...] = diagonal
    projection = stored * scale - dot_split(split(diagonal), split(corr * scale), NN)
    weights = split(jnp.concatenate([projection, jnp.where(core == 0, diagonal, 0.0)], axis=1))
    for k, ref in enumerate((sx_ref, sy_ref)):
        out_ref[k * block : (k + 1) * block, :] = dot_split(weights, (ref[0], ref[1]), NN)


def gram_kernel(mine_ref, other_ref, y_ref, z_ref, images_ref, full_ref, half_ref):
    block = images_ref.shape[0]
    removed = mine_ref[...] + other_ref[...]
    images = y_ref[0:block] - removed[0:block]
    images_ref[...] = images
    gram = 0.0
    for x in (images, z_ref[0:block] - removed[block:]):
        halves = split(x)
        gram = gram + dot_split(halves, halves, NT)
    gram = fold(gram, 2)
    full_ref[...] = gram
    middle = half_ref.shape[0]
    half_ref[...] = jnp.where(lax.axis_index("sub") == 0, gram[:middle], gram[middle:])


def factor_kernel(pairs, total_rows, own_ref, images_ref, d_ref, *refs):
    received, (following_ref, coupling_ref, diagonal_ref) = refs[:-3], refs[-3:]
    block = images_ref.shape[0]
    lanes = 2 * block
    core = lax.axis_index("sub")
    gram = own_ref[...]
    for k, pair in enumerate(pairs):
        mine, other = received[2 * k][...], received[2 * k + 1][...]
        if pair[0] != pair[1]:
            gram = gram + (mine + other)
        else:
            first, second = jnp.where(core == 0, mine, other), jnp.where(core == 0, other, mine)
            gram = gram + jnp.concatenate([first, second], axis=0)
    gram = gram * (1.0 / total_rows)
    row = lax.broadcasted_iota(jnp.int32, (block, lanes), 0)
    column = lax.broadcasted_iota(jnp.int32, (block, lanes), 1)
    left = column < block
    m = jnp.concatenate([gram, pltpu.roll(gram, block, 1)], axis=0)
    m = jnp.where(left, m, jnp.where(column == row + block, 1.0, 0.0))
    finished = []
    for start in range(0, block, GROUP):
        spread = [
            jnp.broadcast_to(m[:, start + p : start + p + 1], m.shape) for p in range(GROUP)
        ]
        for p in range(GROUP):
            at = p % 8
            root = lax.rsqrt(spread[p][at : at + 1])
            lower = spread[p] * root
            done = m[at : at + 1] * root
            finished.append(done)
            for q in range(p + 1, GROUP):
                pivot = q - p + at
                spread[q] = spread[q] - lower * lower[pivot : pivot + 1]
            m = m - lower * done
            if at == 7:
                m = m[8:]
                spread = [column[8:] for column in spread]
    done = jnp.concatenate(finished, axis=0)
    coupling_ref[...] = jnp.where((row <= column) & left, done, 0.0)[:, 0:block]
    inverse = jnp.where((row + block >= column) & ~left, done, 0.0)
    images = images_ref[...]
    images = jnp.concatenate([images, images], axis=0)
    following_ref[...] = dot_split(split(inverse), split(images), NN)
    diagonal_ref[...] = d_ref[...].T


def exchange(x, axis, distance):
    return lax.ppermute(x, axis, [(i, i ^ distance) for i in range(lax.axis_size(axis))])


def local(
    tile_index,
    tile_values,
    onsite_energy,
    start_block,
    previous_block,
    previous_coupling,
    stored_basis,
):
    rows, block = start_block.shape
    bands, columns = lax.axis_size("rows"), lax.axis_size("cols")
    cores = lax.axis_size("sub")
    stored = stored_basis.shape[0]
    width = stored * block
    total_rows = rows * bands * columns
    parts = width // block
    chunk = block // 2
    assert rows == tile_values.shape[1] and cores == 2 and width == rows
    assert bands > 1 and columns > 1 and bands & (bands - 1) == 0 and columns & (columns - 1) == 0
    half = (block, rows)
    swap = [(0, 1), (1, 0)]
    other_tiles = lax.ppermute(tile_values, "sub", swap)
    other_index = lax.ppermute(tile_index, "sub", swap)
    prepare = call(
        prepare_kernel,
        [
            (half, f32), ((2, chunk, width), f32), ((2, width + block, rows), bf16),
            (tile_values.shape, bf16), (tile_index.shape, jnp.int32),
        ],
        "hhhhhhh",
        [
            pltpu.VMEM(half, f32), pltpu.VMEM((1, rows), f32), pltpu.VMEM(half, f32),
            pltpu.VMEM((block, block), f32), pltpu.VMEM((width, rows), f32),
            pltpu.SemaphoreType.DMA((7,)),
        ],
    )
    sources = (
        start_block.T, onsite_energy.reshape(1, rows), previous_block.T, previous_coupling,
        stored_basis.transpose(0, 2, 1).reshape(width, rows), tile_values, tile_index,
    )
    base, corr, sx, tiles, index = prepare(
        *(pltpu.with_memory_space_constraint(a, pltpu.HBM) for a in sources)
    )
    pairs = [(step - 1, step) for step in range(bands - 1, 1, -2)] + [(1, 1)]

    def serve(sends):
        received = []
        for send, pair in zip(sends, pairs):
            moves = [(2 * r + c, 2 * (r ^ pair[c]) + c) for r in range(bands) for c in range(2)]
            received.append(lax.ppermute(send, ("rows", "sub"), moves))
        return [y for x in received for y in (x, lax.ppermute(x, "sub", swap))]

    sends = call(
        functools.partial(push_kernel, pairs, columns),
        [((block + chunk, rows), f32)]
        + [((2 * block, rows) if a != b else (4 * block, rows // 2), bf16) for a, b in pairs],
        "vvvvvv",
    )(index, other_index, sx, corr, tiles, other_tiles)
    sy = exchange(sx, "cols", 1)
    received = serve(sends[1:])
    (mine,) = call(
        functools.partial(image_kernel, pairs, columns),
        [((block + chunk, rows), f32)],
        "v" * (7 + len(received)),
    )(index, other_index, base, sx, tiles, other_tiles, sends[0], *received)
    other = exchange(mine, "cols", 1)
    distances = [2**k for k in range(1, columns.bit_length() - 1)]
    small = block // parts
    total, *send = call(
        functools.partial(inner_kernel, block, parts),
        [((block + small + chunk, rows), f32)]
        + [((block + 2 * small + chunk, rows), bf16)] * (not distances),
        "vvvv",
    )(mine, other, sx, sy)
    for distance in distances:
        total = total + exchange(total, "cols", distance)
    send = send[0] if send else pack(total, block, small)
    steps = [*range(2, bands), 1]
    removed, diagonal = call(
        functools.partial(project_kernel, steps, block, parts, total_rows),
        [((2 * block, rows), f32), ((block, block), f32)],
        "v" * (2 + bands),
    )(total, sx, sy, *(exchange(send, "rows", step) for step in steps))
    images, full, part = call(
        gram_kernel,
        [(half, f32), ((block // 2, 2 * block), f32), ((block // 4, 2 * block), f32)],
        "vvvv",
    )(removed, lax.ppermute(removed, "sub", swap), mine, other)
    for distance in distances:
        full = full + exchange(full, "cols", distance)
        middle = part.shape[0]
        part = jnp.where(lax.axis_index("sub") == 0, full[:middle], full[middle:])
    following, coupling, diagonal = call(
        functools.partial(factor_kernel, pairs, total_rows),
        [(half, f32), ((block, block), f32), ((block, block), f32)],
        "v" * (3 + 2 * len(pairs)),
    )(full, images, diagonal, *serve([full] * (len(pairs) - 1) + [part]))
    return following.T[None], diagonal[None], coupling[None]


def solution(mesh):
    return jax.shard_map(
        local,
        mesh=mesh,
        in_specs=(
            P(("groups", "rows", "cols", "sub"), None),
            P(("groups", "rows", "cols", "sub"), None, None),
            P(("groups", "rows", "cols")),
            P(("groups", "rows", "cols"), None),
            P(("groups", "rows", "cols"), None),
            P("groups", None),
            P("sub", ("groups", "rows", "cols"), None),
        ),
        out_specs=(
            P(None, ("groups", "rows", "cols"), None),
            P(None, "groups", None),
            P(None, "groups", None),
        ),
        check_vma=False,
    )
```

```python
import functools

import jax
import jax.numpy as jnp
from jax import lax
from jax.experimental import pallas as pl
from jax.experimental.pallas import tpu as pltpu
from jax.sharding import PartitionSpec as P

f32 = jnp.float32
bf16 = jnp.bfloat16
GROUP = 16
GRANT = 16 * 1024 * 1024
NN = (((1,), (0,)), ((), ()))
NT = (((1,), (1,)), ((), ()))


def split(x):
    high = x.astype(bf16)
    return high, (x - high.astype(f32)).astype(bf16)


def dot_bf16(a, b, dims):
    return lax.dot_general(a, b, dims, preferred_element_type=f32)


def dot_split(a, b, dims):
    (ah, al), (bh, bl) = a, b
    return dot_bf16(ah, bh, dims) + dot_bf16(ah, bl, dims) + dot_bf16(al, bh, dims)


def fold(x, parts):
    rows = x.shape[0] // parts
    return jnp.concatenate([x[i * rows : (i + 1) * rows] for i in range(parts)], axis=1)


def unfold(x, parts):
    lanes = x.shape[1] // parts
    return jnp.concatenate([x[:, i * lanes : (i + 1) * lanes] for i in range(parts)], axis=0)


def call(kernel, outs, ins, scratch=(), work=40000000):
    spaces = {"v": pltpu.VMEM, "h": pltpu.HBM}
    return pl.pallas_call(
        kernel,
        out_shape=[jax.ShapeDtypeStruct(s, d) for s, d in outs],
        in_specs=[pl.BlockSpec(memory_space=spaces[c]) for c in ins],
        out_specs=[pl.BlockSpec(memory_space=pltpu.VMEM)] * len(outs),
        scratch_shapes=list(scratch),
        cost_estimate=pl.CostEstimate(flops=work, bytes_accessed=1000000, transcendentals=0),
        compiler_params=pltpu.CompilerParams(vmem_limit_bytes=GRANT),
    )


def prepare_kernel(
    x_hbm, e_hbm, p_hbm, c_hbm, s_hbm, t_hbm, i_hbm,
    base_ref, corr_ref, high_ref, low_ref, t_ref, i_ref,
    x_ref, e_ref, p_ref, c_ref, s_ref, sems,
):
    pairs = (
        (s_hbm, s_ref), (x_hbm, x_ref), (p_hbm, p_ref), (c_hbm, c_ref),
        (e_hbm, e_ref), (t_hbm, t_ref), (i_hbm, i_ref),
    )
    copies = [pltpu.make_async_copy(a, b, sems.at[k]) for k, (a, b) in enumerate(pairs)]
    for copy in copies:
        copy.start()
    for copy in copies[:5]:
        copy.wait()
    block = x_ref.shape[0]
    row = lax.broadcasted_iota(jnp.int32, (block, block), 0)
    column = lax.broadcasted_iota(jnp.int32, (block, block), 1)
    coupling = jnp.where(row <= column, c_ref[...], 0.0)
    x = x_ref[...]
    xs = split(x)
    ss = split(s_ref[...])
    for k, ref in enumerate((high_ref, low_ref)):
        ref[...] = jnp.concatenate([ss[k], xs[k]], axis=0)
    base_ref[...] = e_ref[...] * x - dot_split(split(coupling), split(p_ref[...]), NN)
    corr = dot_split(xs, ss, NT)
    chunk = corr_ref.shape[1]
    for band in range(corr_ref.shape[0]):
        corr_ref[band] = corr[band * chunk : (band + 1) * chunk]
    for copy in copies[5:]:
        copy.wait()


def tile_columns(index_refs, shape):
    found = []
    for ref in index_refs:
        index = ref[...]
        for k in range(ref.shape[0]):
            found.append(jnp.broadcast_to(index[k : k + 1, 1:2], shape))
    return found


def target_band(me, core, pair):
    return jnp.bitwise_xor(me, jnp.where(core == 0, pair[0], pair[1]))


def push_kernel(pairs, columns, i_ref, j_ref, high_ref, corr_ref, t_ref, u_ref, *outs):
    width, rows = corr_ref.shape[2], high_ref.shape[1]
    block = high_ref.shape[0] - width
    x = high_ref[width:]
    me, core = lax.axis_index("rows"), lax.axis_index("sub")
    targets = tile_columns((i_ref, j_ref), (block, rows))
    products = [dot_bf16(x, ref[k], NN) for ref in (t_ref, u_ref) for k in range(ref.shape[0])]

    def pushed(band):
        first = band * columns
        total = jnp.zeros((block, rows), f32)
        for target, product in zip(targets, products):
            inside = (target >= first) & (target < first + columns)
            total = total + jnp.where(inside, product, 0.0)
        return total

    parity = jnp.bitwise_and(me, 1)
    outs[0][...] = jnp.concatenate([pushed(me), corr_ref[parity]], axis=0)
    for ref, pair in zip(outs[1:], pairs):
        message = jnp.concatenate([x.astype(f32), pushed(target_band(me, core, pair))], axis=0)
        if pair[0] != pair[1]:
            ref[...] = message.astype(bf16)
        else:
            message = jnp.where(core == 0, message[:, : rows // 2], message[:, rows // 2 :])
            halves = [unfold(h.astype(f32), 2) for h in split(corr_ref[1 - parity])]
            ref[...] = jnp.concatenate([message, *halves], axis=0).astype(bf16)


def image_kernel(pairs, columns, parts, i_ref, j_ref, base_ref, high_ref, low_ref, t_ref, u_ref, own_ref, *refs):
    received, (y_ref, send_ref, late_ref) = refs[:-3], refs[-3:]
    block, rows = base_ref.shape
    width = high_ref.shape[0] - block
    me, core = lax.axis_index("rows"), lax.axis_index("sub")
    y = base_ref[...] + own_ref[0:block]
    corr = own_ref[block:]
    blocks = [(me, high_ref[width:].astype(f32))]
    for k, pair in enumerate(pairs):
        mine, other = received[2 * k][...].astype(f32), received[2 * k + 1][...].astype(f32)
        if pair[0] != pair[1]:
            found = [(target_band(me, core, pair), mine), (target_band(me, core, pair[::-1]), other)]
        else:
            parts_of = mine[2 * block :]
            count = parts_of.shape[0] // 2
            corr = corr + fold(parts_of[:count] + parts_of[count:], 2)
            mine, other = mine[: 2 * block], other[: 2 * block]
            first, second = jnp.where(core == 0, mine, other), jnp.where(core == 0, other, mine)
            found = [(jnp.bitwise_xor(me, pair[0]), jnp.concatenate([first, second], axis=1))]
        for band, message in found:
            blocks.append((band, message[0:block]))
            y = y + message[block:]
    tiles = [ref[k] for ref in (t_ref, u_ref) for k in range(ref.shape[0])]
    for target, tile in zip(tile_columns((i_ref, j_ref), (block, rows)), tiles):
        source = jnp.zeros((block, rows), f32)
        for band, held in blocks:
            first = band * columns
            inside = (target >= first) & (target < first + columns)
            source = jnp.where(inside, held, source)
        y = y + dot_bf16(source.astype(bf16), tile, NT)
    y_ref[...] = y
    halves = split(y)
    stored = dot_split(halves, (high_ref[:width], low_ref[:width]), NT)
    diagonal = dot_split(halves, (high_ref[width:], low_ref[width:]), NT)
    send_ref[...] = jnp.concatenate([stored, fold(diagonal, parts), corr], axis=0)
    late_ref[...] = jnp.concatenate([low_ref[...], *halves], axis=0)


def pack(total, block, small):
    high, low = split(total[block : block + small])
    message = [total[0:block], high.astype(f32), low.astype(f32), total[block + small :]]
    return jnp.concatenate(message, axis=0).astype(bf16)


def combine_kernel(block, small, mine_ref, other_ref, total_ref, *send_refs):
    total = mine_ref[...] + other_ref[...]
    total_ref[...] = total
    for ref in send_refs:
        ref[...] = pack(total, block, small)


def project_kernel(steps, block, parts, total_rows, total_ref, high_ref, low_ref, near_ref, late_ref, *refs):
    received, (out_ref, diagonal_ref) = refs[:-2], refs[-2:]
    me, core = lax.axis_index("rows"), lax.axis_index("sub")
    small = block // parts
    total = total_ref[...]
    stored, diagonal = total[0:block], total[block : block + small]
    same, other = total[block + small :], jnp.zeros((block // 2, total.shape[1]), f32)
    for step, ref in zip(steps, received):
        message = ref[...].astype(f32)
        stored = stored + message[0:block]
        diagonal = diagonal + message[block : block + small]
        diagonal = diagonal + message[block + small : block + 2 * small]
        part = message[block + 2 * small :]
        if step % 2:
            other = other + part
        else:
            same = same + part
    even = jnp.bitwise_and(me, 1) == 0
    corr = jnp.concatenate([jnp.where(even, same, other), jnp.where(even, other, same)], axis=0)
    scale = 1.0 / total_rows
    diagonal = unfold(diagonal * scale, parts)
    diagonal_ref[...] = diagonal
    projection = stored * scale - dot_split(split(diagonal), split(corr * scale), NN)
    weights = split(jnp.concatenate([projection, jnp.where(core == 0, diagonal, 0.0)], axis=1))
    out_ref[0:block, :] = dot_split(weights, (high_ref[...], low_ref[...]), NN)
    out_ref[block:, :] = dot_split(weights, (near_ref[...], late_ref[: low_ref.shape[0]]), NN)


def gram_kernel(mine_ref, other_ref, y_ref, late_ref, images_ref, full_ref, half_ref):
    block = images_ref.shape[0]
    removed = mine_ref[...] + other_ref[...]
    images = y_ref[...] - removed[0:block]
    images_ref[...] = images
    halves = late_ref[late_ref.shape[0] - 2 * block :].astype(f32)
    gram = 0.0
    for x in (images, halves[0:block] + halves[block:] - removed[block:]):
        halves = split(x)
        gram = gram + dot_split(halves, halves, NT)
    gram = fold(gram, 2)
    full_ref[...] = gram
    middle = half_ref.shape[0]
    half_ref[...] = jnp.where(lax.axis_index("sub") == 0, gram[:middle], gram[middle:])


def factor_kernel(pairs, total_rows, own_ref, images_ref, d_ref, *refs):
    received, (following_ref, coupling_ref, diagonal_ref) = refs[:-3], refs[-3:]
    block = images_ref.shape[0]
    lanes = 2 * block
    core = lax.axis_index("sub")
    gram = own_ref[...]
    for k, pair in enumerate(pairs):
        mine, other = received[2 * k][...], received[2 * k + 1][...]
        if pair[0] != pair[1]:
            gram = gram + (mine + other)
        else:
            first, second = jnp.where(core == 0, mine, other), jnp.where(core == 0, other, mine)
            gram = gram + jnp.concatenate([first, second], axis=0)
    gram = gram * (1.0 / total_rows)
    row = lax.broadcasted_iota(jnp.int32, (block, lanes), 0)
    column = lax.broadcasted_iota(jnp.int32, (block, lanes), 1)
    left = column < block
    m = jnp.concatenate([gram, pltpu.roll(gram, block, 1)], axis=0)
    m = jnp.where(left, m, jnp.where(column == row + block, 1.0, 0.0))
    finished = []
    for start in range(0, block, GROUP):
        spread = [
            jnp.broadcast_to(m[:, start + p : start + p + 1], m.shape) for p in range(GROUP)
        ]
        for p in range(GROUP):
            at = p % 8
            root = lax.rsqrt(spread[p][at : at + 1])
            lower = spread[p] * root
            done = m[at : at + 1] * root
            finished.append(done)
            for q in range(p + 1, GROUP):
                pivot = q - p + at
                spread[q] = spread[q] - lower * lower[pivot : pivot + 1]
            m = m - lower * done
            if at == 7:
                m = m[8:]
                spread = [column[8:] for column in spread]
    done = jnp.concatenate(finished, axis=0)
    coupling_ref[...] = jnp.where((row <= column) & left, done, 0.0)[:, 0:block]
    inverse = jnp.where((row + block >= column) & ~left, done, 0.0)
    images = images_ref[...]
    images = jnp.concatenate([images, images], axis=0)
    following_ref[...] = dot_split(split(inverse), split(images), NN)
    diagonal_ref[...] = d_ref[...].T


def exchange(x, axis, distance):
    return lax.ppermute(x, axis, [(i, i ^ distance) for i in range(lax.axis_size(axis))])


def local(
    tile_index,
    tile_values,
    onsite_energy,
    start_block,
    previous_block,
    previous_coupling,
    stored_basis,
):
    rows, block = start_block.shape
    bands, columns = lax.axis_size("rows"), lax.axis_size("cols")
    cores = lax.axis_size("sub")
    stored = stored_basis.shape[0]
    width = stored * block
    total_rows = rows * bands * columns
    parts = width // block
    chunk = block // 2
    assert rows == tile_values.shape[1] and cores == 2 and width == rows
    assert bands > 1 and columns > 1 and bands & (bands - 1) == 0 and columns & (columns - 1) == 0
    half = (block, rows)
    swap = [(0, 1), (1, 0)]
    other_tiles = lax.ppermute(tile_values, "sub", swap)
    other_index = lax.ppermute(tile_index, "sub", swap)
    prepare = call(
        prepare_kernel,
        [
            (half, f32), ((2, chunk, width), f32), *[((width + block, rows), bf16)] * 2,
            (tile_values.shape, bf16), (tile_index.shape, jnp.int32),
        ],
        "hhhhhhh",
        [
            pltpu.VMEM(half, f32), pltpu.VMEM((1, rows), f32), pltpu.VMEM(half, f32),
            pltpu.VMEM((block, block), f32), pltpu.VMEM((width, rows), f32),
            pltpu.SemaphoreType.DMA((7,)),
        ],
    )
    sources = (
        start_block.T, onsite_energy.reshape(1, rows), previous_block.T, previous_coupling,
        stored_basis.transpose(0, 2, 1).reshape(width, rows), tile_values, tile_index,
    )
    base, corr, high, low, tiles, index = prepare(
        *(pltpu.with_memory_space_constraint(a, pltpu.HBM) for a in sources)
    )
    pairs = [(step - 1, step) for step in range(bands - 1, 1, -2)] + [(1, 1)]

    def serve(sends):
        received = []
        for send, pair in zip(sends, pairs):
            moves = [(2 * r + c, 2 * (r ^ pair[c]) + c) for r in range(bands) for c in range(2)]
            received.append(lax.ppermute(send, ("rows", "sub"), moves))
        return [y for x in received for y in (x, lax.ppermute(x, "sub", swap))]

    sends = call(
        functools.partial(push_kernel, pairs, columns),
        [((block + chunk, rows), f32)]
        + [((2 * block, rows) if a != b else (4 * block, rows // 2), bf16) for a, b in pairs],
        "vvvvvv",
    )(index, other_index, high, corr, tiles, other_tiles)
    near = exchange(high, "cols", 1)
    received = serve(sends[1:])
    small = block // parts
    y, mine, late = call(
        functools.partial(image_kernel, pairs, columns, parts),
        [(half, f32), ((block + small + chunk, rows), f32), ((width + 3 * block, rows), bf16)],
        "v" * (8 + len(received)),
    )(index, other_index, base, high, low, tiles, other_tiles, sends[0], *received)
    other = exchange(mine, "cols", 1)
    late = exchange(late, "cols", 1)
    distances = [2**k for k in range(1, columns.bit_length() - 1)]
    total, *send = call(
        functools.partial(combine_kernel, block, small),
        [((block + small + chunk, rows), f32)]
        + [((block + 2 * small + chunk, rows), bf16)] * (not distances),
        "vv",
    )(mine, other)
    for distance in distances:
        total = total + exchange(total, "cols", distance)
    send = send[0] if send else pack(total, block, small)
    steps = [*range(2, bands), 1]
    removed, diagonal = call(
        functools.partial(project_kernel, steps, block, parts, total_rows),
        [((2 * block, rows), f32), ((block, block), f32)],
        "v" * (4 + bands),
    )(total, high, low, near, late, *(exchange(send, "rows", step) for step in steps))
    images, full, part = call(
        gram_kernel,
        [(half, f32), ((block // 2, 2 * block), f32), ((block // 4, 2 * block), f32)],
        "vvvv",
    )(removed, lax.ppermute(removed, "sub", swap), y, late)
    for distance in distances:
        full = full + exchange(full, "cols", distance)
        middle = part.shape[0]
        part = jnp.where(lax.axis_index("sub") == 0, full[:middle], full[middle:])
    following, coupling, diagonal = call(
        functools.partial(factor_kernel, pairs, total_rows),
        [(half, f32), ((block, block), f32), ((block, block), f32)],
        "v" * (3 + 2 * len(pairs)),
    )(full, images, diagonal, *serve([full] * (len(pairs) - 1) + [part]))
    return following.T[None], diagonal[None], coupling[None]


def solution(mesh):
    return jax.shard_map(
        local,
        mesh=mesh,
        in_specs=(
            P(("groups", "rows", "cols", "sub"), None),
            P(("groups", "rows", "cols", "sub"), None, None),
            P(("groups", "rows", "cols")),
            P(("groups", "rows", "cols"), None),
            P(("groups", "rows", "cols"), None),
            P("groups", None),
            P("sub", ("groups", "rows", "cols"), None),
        ),
        out_specs=(
            P(None, ("groups", "rows", "cols"), None),
            P(None, "groups", None),
            P(None, "groups", None),
        ),
        check_vma=False,
    )
```

```python
import functools

import jax
import jax.numpy as jnp
from jax import lax
from jax.experimental import pallas as pl
from jax.experimental.pallas import tpu as pltpu
from jax.sharding import PartitionSpec as P

f32 = jnp.float32
bf16 = jnp.bfloat16
GROUP = 16
GRANT = 16 * 1024 * 1024
NN = (((1,), (0,)), ((), ()))
NT = (((1,), (1,)), ((), ()))


def split(x):
    high = x.astype(bf16)
    return high, (x - high.astype(f32)).astype(bf16)


def dot_bf16(a, b, dims):
    return lax.dot_general(a, b, dims, preferred_element_type=f32)


def dot_split(a, b, dims):
    (ah, al), (bh, bl) = a, b
    return dot_bf16(ah, bh, dims) + dot_bf16(ah, bl, dims) + dot_bf16(al, bh, dims)


def fold(x, parts):
    rows = x.shape[0] // parts
    return jnp.concatenate([x[i * rows : (i + 1) * rows] for i in range(parts)], axis=1)


def unfold(x, parts):
    lanes = x.shape[1] // parts
    return jnp.concatenate([x[:, i * lanes : (i + 1) * lanes] for i in range(parts)], axis=0)


def call(kernel, outs, ins, scratch=(), work=40000000):
    spaces = {"v": pltpu.VMEM, "h": pltpu.HBM}
    return pl.pallas_call(
        kernel,
        out_shape=[jax.ShapeDtypeStruct(s, d) for s, d in outs],
        in_specs=[pl.BlockSpec(memory_space=spaces[c]) for c in ins],
        out_specs=[pl.BlockSpec(memory_space=pltpu.VMEM)] * len(outs),
        scratch_shapes=list(scratch),
        cost_estimate=pl.CostEstimate(flops=work, bytes_accessed=1000000, transcendentals=0),
        compiler_params=pltpu.CompilerParams(vmem_limit_bytes=GRANT),
    )


def prepare_kernel(
    x_hbm, e_hbm, p_hbm, c_hbm, s_hbm, t_hbm, i_hbm,
    base_ref, corr_ref, high_ref, low_ref, t_ref, i_ref,
    x_ref, e_ref, p_ref, c_ref, s_ref, sems,
):
    pairs = (
        (s_hbm, s_ref), (x_hbm, x_ref), (p_hbm, p_ref), (c_hbm, c_ref),
        (e_hbm, e_ref), (t_hbm, t_ref), (i_hbm, i_ref),
    )
    copies = [pltpu.make_async_copy(a, b, sems.at[k]) for k, (a, b) in enumerate(pairs)]
    for copy in copies:
        copy.start()
    for copy in copies[:5]:
        copy.wait()
    block = x_ref.shape[0]
    row = lax.broadcasted_iota(jnp.int32, (block, block), 0)
    column = lax.broadcasted_iota(jnp.int32, (block, block), 1)
    coupling = jnp.where(row <= column, c_ref[...], 0.0)
    x = x_ref[...]
    xs = split(x)
    ss = split(s_ref[...])
    for k, ref in enumerate((high_ref, low_ref)):
        ref[...] = jnp.concatenate([ss[k], xs[k]], axis=0)
    base_ref[...] = e_ref[...] * x - dot_split(split(coupling), split(p_ref[...]), NN)
    corr = dot_split(xs, ss, NT)
    chunk = corr_ref.shape[1]
    for band in range(corr_ref.shape[0]):
        corr_ref[band] = corr[band * chunk : (band + 1) * chunk]
    for copy in copies[5:]:
        copy.wait()


def tile_columns(index_refs, shape):
    found = []
    for ref in index_refs:
        index = ref[...]
        for k in range(ref.shape[0]):
            found.append(jnp.broadcast_to(index[k : k + 1, 1:2], shape))
    return found


def target_band(me, core, pair):
    return jnp.bitwise_xor(me, jnp.where(core == 0, pair[0], pair[1]))


def push_kernel(pairs, columns, i_ref, j_ref, high_ref, corr_ref, t_ref, u_ref, *outs):
    width, rows = corr_ref.shape[2], high_ref.shape[1]
    block = high_ref.shape[0] - width
    x = high_ref[width:]
    me, core = lax.axis_index("rows"), lax.axis_index("sub")
    targets = tile_columns((i_ref, j_ref), (block, rows))
    products = [dot_bf16(x, ref[k], NN) for ref in (t_ref, u_ref) for k in range(ref.shape[0])]

    def pushed(band):
        first = band * columns
        total = jnp.zeros((block, rows), f32)
        for target, product in zip(targets, products):
            inside = (target >= first) & (target < first + columns)
            total = total + jnp.where(inside, product, 0.0)
        return total

    parity = jnp.bitwise_and(me, 1)
    outs[0][...] = jnp.concatenate([pushed(me), corr_ref[parity]], axis=0)
    for ref, pair in zip(outs[1:], pairs):
        message = jnp.concatenate([x.astype(f32), pushed(target_band(me, core, pair))], axis=0)
        if pair[0] != pair[1]:
            ref[...] = message.astype(bf16)
        else:
            message = jnp.where(core == 0, message[:, : rows // 2], message[:, rows // 2 :])
            halves = [unfold(h.astype(f32), 2) for h in split(corr_ref[1 - parity])]
            ref[...] = jnp.concatenate([message, *halves], axis=0).astype(bf16)


def image_kernel(pairs, columns, parts, i_ref, j_ref, base_ref, high_ref, low_ref, t_ref, u_ref, own_ref, *refs):
    received, (y_ref, send_ref, late_ref) = refs[:-3], refs[-3:]
    block, rows = base_ref.shape
    width = high_ref.shape[0] - block
    me, core = lax.axis_index("rows"), lax.axis_index("sub")
    y = base_ref[...] + own_ref[0:block]
    corr = own_ref[block:]
    blocks = [(me, high_ref[width:].astype(f32))]
    for k, pair in enumerate(pairs):
        mine, other = received[2 * k][...].astype(f32), received[2 * k + 1][...].astype(f32)
        if pair[0] != pair[1]:
            found = [(target_band(me, core, pair), mine), (target_band(me, core, pair[::-1]), other)]
        else:
            parts_of = mine[2 * block :]
            count = parts_of.shape[0] // 2
            corr = corr + fold(parts_of[:count] + parts_of[count:], 2)
            mine, other = mine[: 2 * block], other[: 2 * block]
            first, second = jnp.where(core == 0, mine, other), jnp.where(core == 0, other, mine)
            found = [(jnp.bitwise_xor(me, pair[0]), jnp.concatenate([first, second], axis=1))]
        for band, message in found:
            blocks.append((band, message[0:block]))
            y = y + message[block:]
    tiles = [ref[k] for ref in (t_ref, u_ref) for k in range(ref.shape[0])]
    for target, tile in zip(tile_columns((i_ref, j_ref), (block, rows)), tiles):
        source = jnp.zeros((block, rows), f32)
        for band, held in blocks:
            first = band * columns
            inside = (target >= first) & (target < first + columns)
            source = jnp.where(inside, held, source)
        y = y + dot_bf16(source.astype(bf16), tile, NT)
    y_ref[...] = y
    halves = split(y)
    stored = dot_split(halves, (high_ref[:width], low_ref[:width]), NT)
    diagonal = dot_split(halves, (high_ref[width:], low_ref[width:]), NT)
    send_ref[...] = jnp.concatenate([stored, fold(diagonal, parts), corr], axis=0)
    late_ref[...] = jnp.concatenate([low_ref[...], *halves], axis=0)


def pack(total, block, small):
    high, low = split(total[block : block + small])
    message = [total[0:block], high.astype(f32), low.astype(f32), total[block + small :]]
    return jnp.concatenate(message, axis=0).astype(bf16)


def combine_kernel(block, small, mine_ref, other_ref, total_ref, *send_refs):
    total = mine_ref[...] + other_ref[...]
    total_ref[...] = total
    for ref in send_refs:
        ref[...] = pack(total, block, small)


def project_kernel(steps, block, parts, total_rows, total_ref, high_ref, low_ref, near_ref, late_ref, *refs):
    received, (out_ref, diagonal_ref) = refs[:-2], refs[-2:]
    me, core = lax.axis_index("rows"), lax.axis_index("sub")
    small = block // parts
    total = total_ref[...]
    stored, diagonal = total[0:block], total[block : block + small]
    same, other = total[block + small :], jnp.zeros((block // 2, total.shape[1]), f32)
    for step, ref in zip(steps, received):
        message = ref[...].astype(f32)
        stored = stored + message[0:block]
        diagonal = diagonal + message[block : block + small]
        diagonal = diagonal + message[block + small : block + 2 * small]
        part = message[block + 2 * small :]
        if step % 2:
            other = other + part
        else:
            same = same + part
    even = jnp.bitwise_and(me, 1) == 0
    corr = jnp.concatenate([jnp.where(even, same, other), jnp.where(even, other, same)], axis=0)
    scale = 1.0 / total_rows
    diagonal = unfold(diagonal * scale, parts)
    diagonal_ref[...] = diagonal
    projection = stored * scale - dot_split(split(diagonal), split(corr * scale), NN)
    weights = split(jnp.concatenate([projection, jnp.where(core == 0, diagonal, 0.0)], axis=1))
    out_ref[0:block, :] = dot_split(weights, (high_ref[...], low_ref[...]), NN)
    out_ref[block:, :] = dot_split(weights, (near_ref[...], late_ref[: low_ref.shape[0]]), NN)


def gram_kernel(mine_ref, other_ref, y_ref, late_ref, images_ref, full_ref, half_ref):
    block = images_ref.shape[0]
    removed = mine_ref[...] + other_ref[...]
    images = y_ref[...] - removed[0:block]
    images_ref[...] = images
    halves = late_ref[late_ref.shape[0] - 2 * block :].astype(f32)
    gram = 0.0
    for x in (images, halves[0:block] + halves[block:] - removed[block:]):
        halves = split(x)
        gram = gram + dot_split(halves, halves, NT)
    gram = fold(gram, 2)
    full_ref[...] = gram
    middle = half_ref.shape[0]
    half_ref[...] = jnp.where(lax.axis_index("sub") == 0, gram[:middle], gram[middle:])


def factor_kernel(pairs, total_rows, own_ref, images_ref, d_ref, *refs):
    received, (following_ref, coupling_ref, diagonal_ref) = refs[:-3], refs[-3:]
    block = images_ref.shape[0]
    lanes = 2 * block
    core = lax.axis_index("sub")
    gram = own_ref[...]
    for k, pair in enumerate(pairs):
        mine, other = received[2 * k][...], received[2 * k + 1][...]
        if pair[0] != pair[1]:
            gram = gram + (mine + other)
        else:
            first, second = jnp.where(core == 0, mine, other), jnp.where(core == 0, other, mine)
            gram = gram + jnp.concatenate([first, second], axis=0)
    gram = gram * (1.0 / total_rows)
    row = lax.broadcasted_iota(jnp.int32, (block, lanes), 0)
    column = lax.broadcasted_iota(jnp.int32, (block, lanes), 1)
    left = column < block
    m = jnp.concatenate([gram, pltpu.roll(gram, block, 1)], axis=0)
    m = jnp.where(left, m, jnp.where(column == row + block, 1.0, 0.0))
    finished = []
    for start in range(0, block, GROUP):
        spread = [
            jnp.broadcast_to(m[:, start + p : start + p + 1], m.shape) for p in range(GROUP)
        ]
        for p in range(GROUP):
            at = p % 8
            root = lax.rsqrt(spread[p][at : at + 1])
            lower = spread[p] * root
            done = m[at : at + 1] * root
            finished.append(done)
            for q in range(p + 1, GROUP):
                pivot = q - p + at
                spread[q] = spread[q] - lower * lower[pivot : pivot + 1]
            m = m - lower * done
            if at == 7:
                m = m[8:]
                spread = [column[8:] for column in spread]
    done = jnp.concatenate(finished, axis=0)
    coupling_ref[...] = jnp.where((row <= column) & left, done, 0.0)[:, 0:block]
    inverse = jnp.where((row + block >= column) & ~left, done, 0.0)
    images = images_ref[...]
    images = jnp.concatenate([images, images], axis=0)
    following_ref[...] = dot_split(split(inverse), split(images), NN)
    diagonal_ref[...] = d_ref[...].T


def exchange(x, axis, distance):
    return lax.ppermute(x, axis, [(i, i ^ distance) for i in range(lax.axis_size(axis))])


def local(
    tile_index,
    tile_values,
    onsite_energy,
    start_block,
    previous_block,
    previous_coupling,
    stored_basis,
):
    rows, block = start_block.shape
    bands, columns = lax.axis_size("rows"), lax.axis_size("cols")
    cores = lax.axis_size("sub")
    stored = stored_basis.shape[0]
    width = stored * block
    total_rows = rows * bands * columns
    parts = width // block
    chunk = block // 2
    assert rows == tile_values.shape[1] and cores == 2 and width == rows
    assert bands > 1 and columns > 1 and bands & (bands - 1) == 0 and columns & (columns - 1) == 0
    half = (block, rows)
    swap = [(0, 1), (1, 0)]
    other_tiles = lax.ppermute(tile_values, "sub", swap)
    other_index = lax.ppermute(tile_index, "sub", swap)
    prepare = call(
        prepare_kernel,
        [
            (half, f32), ((2, chunk, width), f32), *[((width + block, rows), bf16)] * 2,
            (tile_values.shape, bf16), (tile_index.shape, jnp.int32),
        ],
        "hhhhhhh",
        [
            pltpu.VMEM(half, f32), pltpu.VMEM((1, rows), f32), pltpu.VMEM(half, f32),
            pltpu.VMEM((block, block), f32), pltpu.VMEM((width, rows), f32),
            pltpu.SemaphoreType.DMA((7,)),
        ],
    )
    sources = (
        start_block.T, onsite_energy.reshape(1, rows), previous_block.T, previous_coupling,
        stored_basis.transpose(0, 2, 1).reshape(width, rows), tile_values, tile_index,
    )
    base, corr, high, low, tiles, index = prepare(
        *(pltpu.with_memory_space_constraint(a, pltpu.HBM) for a in sources)
    )
    pairs = [(step - 1, step) for step in range(bands - 1, 1, -2)] + [(1, 1)]

    def serve(sends):
        received = []
        for send, pair in zip(sends, pairs):
            moves = [(2 * r + c, 2 * (r ^ pair[c]) + c) for r in range(bands) for c in range(2)]
            received.append(lax.ppermute(send, ("rows", "sub"), moves))
        swapped = []
        for x, pair in zip(received, pairs):
            swapped += [x, lax.ppermute(x, "sub", swap)]
        return swapped

    sends = call(
        functools.partial(push_kernel, pairs, columns),
        [((block + chunk, rows), f32)]
        + [((2 * block, rows) if a != b else (4 * block, rows // 2), bf16) for a, b in pairs],
        "vvvvvv",
    )(index, other_index, high, corr, tiles, other_tiles)
    near = exchange(high, "cols", 1)
    received = serve(sends[1:])
    small = block // parts
    y, mine, late = call(
        functools.partial(image_kernel, pairs, columns, parts),
        [(half, f32), ((block + small + chunk, rows), f32), ((width + 3 * block, rows), bf16)],
        "v" * (8 + len(received)),
    )(index, other_index, base, high, low, tiles, other_tiles, sends[0], *received)
    other = exchange(mine, "cols", 1)
    late = exchange(late, "cols", 1)
    distances = [2**k for k in range(1, columns.bit_length() - 1)]
    total, *send = call(
        functools.partial(combine_kernel, block, small),
        [((block + small + chunk, rows), f32)]
        + [((block + 2 * small + chunk, rows), bf16)] * (not distances),
        "vv",
    )(mine, other)
    for distance in distances:
        total = total + exchange(total, "cols", distance)
    send = send[0] if send else pack(total, block, small)
    steps = [*range(2, bands), 1]
    removed, diagonal = call(
        functools.partial(project_kernel, steps, block, parts, total_rows),
        [((2 * block, rows), f32), ((block, block), f32)],
        "v" * (4 + bands),
    )(total, high, low, near, late, *(exchange(send, "rows", step) for step in steps))
    images, full, part = call(
        gram_kernel,
        [(half, f32), ((block // 2, 2 * block), f32), ((block // 4, 2 * block), f32)],
        "vvvv",
    )(removed, lax.ppermute(removed, "sub", swap), y, late)
    for distance in distances:
        full = full + exchange(full, "cols", distance)
        middle = part.shape[0]
        part = jnp.where(lax.axis_index("sub") == 0, full[:middle], full[middle:])
    following, coupling, diagonal = call(
        functools.partial(factor_kernel, pairs, total_rows),
        [(half, f32), ((block, block), f32), ((block, block), f32)],
        "v" * (3 + 2 * len(pairs)),
    )(full, images, diagonal, *serve([full] * (len(pairs) - 1) + [part]))
    return following.T[None], diagonal[None], coupling[None]


def solution(mesh):
    return jax.shard_map(
        local,
        mesh=mesh,
        in_specs=(
            P(("groups", "rows", "cols", "sub"), None),
            P(("groups", "rows", "cols", "sub"), None, None),
            P(("groups", "rows", "cols")),
            P(("groups", "rows", "cols"), None),
            P(("groups", "rows", "cols"), None),
            P("groups", None),
            P("sub", ("groups", "rows", "cols"), None),
        ),
        out_specs=(
            P(None, ("groups", "rows", "cols"), None),
            P(None, "groups", None),
            P(None, "groups", None),
        ),
        check_vma=False,
    )
```

```python
import functools

import jax
import jax.numpy as jnp
from jax import lax
from jax.experimental import pallas as pl
from jax.experimental.pallas import tpu as pltpu
from jax.sharding import PartitionSpec as P

f32 = jnp.float32
bf16 = jnp.bfloat16
GROUP = 16
GRANT = 16 * 1024 * 1024
NN = (((1,), (0,)), ((), ()))
NT = (((1,), (1,)), ((), ()))


def split(x):
    high = x.astype(bf16)
    return high, (x - high.astype(f32)).astype(bf16)


def dot_bf16(a, b, dims):
    return lax.dot_general(a, b, dims, preferred_element_type=f32)


def dot_split(a, b, dims):
    (ah, al), (bh, bl) = a, b
    return dot_bf16(ah, bh, dims) + dot_bf16(ah, bl, dims) + dot_bf16(al, bh, dims)


def fold(x, parts):
    rows = x.shape[0] // parts
    return jnp.concatenate([x[i * rows : (i + 1) * rows] for i in range(parts)], axis=1)


def unfold(x, parts):
    lanes = x.shape[1] // parts
    return jnp.concatenate([x[:, i * lanes : (i + 1) * lanes] for i in range(parts)], axis=0)


def call(kernel, outs, ins, scratch=(), work=40000000):
    spaces = {"v": pltpu.VMEM, "h": pltpu.HBM}
    return pl.pallas_call(
        kernel,
        out_shape=[jax.ShapeDtypeStruct(s, d) for s, d in outs],
        in_specs=[pl.BlockSpec(memory_space=spaces[c]) for c in ins],
        out_specs=[pl.BlockSpec(memory_space=pltpu.VMEM)] * len(outs),
        scratch_shapes=list(scratch),
        cost_estimate=pl.CostEstimate(flops=work, bytes_accessed=1000000, transcendentals=0),
        compiler_params=pltpu.CompilerParams(vmem_limit_bytes=GRANT),
    )


def prepare_kernel(
    x_hbm, e_hbm, p_hbm, c_hbm, s_hbm, t_hbm, i_hbm,
    base_ref, corr_ref, high_ref, low_ref, t_ref, i_ref,
    x_ref, e_ref, p_ref, c_ref, s_ref, sems,
):
    pairs = (
        (s_hbm, s_ref), (x_hbm, x_ref), (p_hbm, p_ref), (c_hbm, c_ref),
        (e_hbm, e_ref), (t_hbm, t_ref), (i_hbm, i_ref),
    )
    copies = [pltpu.make_async_copy(a, b, sems.at[k]) for k, (a, b) in enumerate(pairs)]
    for copy in copies:
        copy.start()
    for copy in copies[:5]:
        copy.wait()
    block = x_ref.shape[0]
    row = lax.broadcasted_iota(jnp.int32, (block, block), 0)
    column = lax.broadcasted_iota(jnp.int32, (block, block), 1)
    coupling = jnp.where(row <= column, c_ref[...], 0.0)
    x = x_ref[...]
    xs = split(x)
    ss = split(s_ref[...])
    for k, ref in enumerate((high_ref, low_ref)):
        ref[...] = jnp.concatenate([ss[k], xs[k]], axis=0)
    base_ref[...] = e_ref[...] * x - dot_split(split(coupling), split(p_ref[...]), NN)
    corr = dot_split(xs, ss, NT)
    chunk = corr_ref.shape[1]
    for band in range(corr_ref.shape[0]):
        corr_ref[band] = corr[band * chunk : (band + 1) * chunk]
    for copy in copies[5:]:
        copy.wait()


def tile_columns(index_refs, shape):
    found = []
    for ref in index_refs:
        index = ref[...]
        for k in range(ref.shape[0]):
            found.append(jnp.broadcast_to(index[k : k + 1, 1:2], shape))
    return found


def target_band(me, core, pair):
    return jnp.bitwise_xor(me, jnp.where(core == 0, pair[0], pair[1]))


def push_kernel(pairs, columns, i_ref, j_ref, high_ref, corr_ref, t_ref, u_ref, *outs):
    width, rows = corr_ref.shape[2], high_ref.shape[1]
    block = high_ref.shape[0] - width
    x = high_ref[width:]
    me, core = lax.axis_index("rows"), lax.axis_index("sub")
    targets = tile_columns((i_ref, j_ref), (block, rows))
    products = [dot_bf16(x, ref[k], NN) for ref in (t_ref, u_ref) for k in range(ref.shape[0])]

    def pushed(band):
        first = band * columns
        total = jnp.zeros((block, rows), f32)
        for target, product in zip(targets, products):
            inside = (target >= first) & (target < first + columns)
            total = total + jnp.where(inside, product, 0.0)
        return total

    parity = jnp.bitwise_and(me, 1)
    outs[0][...] = jnp.concatenate([pushed(me), corr_ref[parity]], axis=0)
    for ref, pair in zip(outs[1:], pairs):
        message = jnp.concatenate([x.astype(f32), pushed(target_band(me, core, pair))], axis=0)
        if pair[0] != pair[1]:
            ref[...] = message.astype(bf16)
        else:
            message = jnp.where(core == 0, message[:, : rows // 2], message[:, rows // 2 :])
            halves = [unfold(h.astype(f32), 2) for h in split(corr_ref[1 - parity])]
            ref[...] = jnp.concatenate([message, *halves], axis=0).astype(bf16)


def image_kernel(pairs, columns, parts, i_ref, j_ref, base_ref, high_ref, low_ref, t_ref, u_ref, own_ref, *refs):
    received, (y_ref, send_ref) = refs[:-2], refs[-2:]
    block, rows = base_ref.shape
    width = high_ref.shape[0] - block
    me, core = lax.axis_index("rows"), lax.axis_index("sub")
    y = base_ref[...] + own_ref[0:block]
    corr = own_ref[block:]
    blocks = [(me, high_ref[width:].astype(f32))]
    for k, pair in enumerate(pairs):
        mine, other = received[2 * k][...].astype(f32), received[2 * k + 1][...].astype(f32)
        if pair[0] != pair[1]:
            found = [(target_band(me, core, pair), mine), (target_band(me, core, pair[::-1]), other)]
        else:
            parts_of = mine[2 * block :]
            count = parts_of.shape[0] // 2
            corr = corr + fold(parts_of[:count] + parts_of[count:], 2)
            mine, other = mine[: 2 * block], other[: 2 * block]
            first, second = jnp.where(core == 0, mine, other), jnp.where(core == 0, other, mine)
            found = [(jnp.bitwise_xor(me, pair[0]), jnp.concatenate([first, second], axis=1))]
        for band, message in found:
            blocks.append((band, message[0:block]))
            y = y + message[block:]
    tiles = [ref[k] for ref in (t_ref, u_ref) for k in range(ref.shape[0])]
    for target, tile in zip(tile_columns((i_ref, j_ref), (block, rows)), tiles):
        source = jnp.zeros((block, rows), f32)
        for band, held in blocks:
            first = band * columns
            inside = (target >= first) & (target < first + columns)
            source = jnp.where(inside, held, source)
        y = y + dot_bf16(source.astype(bf16), tile, NT)
    y_ref[...] = y
    halves = split(y)
    stored = dot_split(halves, (high_ref[:width], low_ref[:width]), NT)
    diagonal = dot_split(halves, (high_ref[width:], low_ref[width:]), NT)
    send_ref[...] = jnp.concatenate([stored, fold(diagonal, parts), corr], axis=0)


def pack(total, block, small):
    high, low = split(total[block : block + small])
    message = [total[0:block], high.astype(f32), low.astype(f32), total[block + small :]]
    return jnp.concatenate(message, axis=0).astype(bf16)


def combine_kernel(block, small, mine_ref, other_ref, total_ref, *send_refs):
    total = mine_ref[...] + other_ref[...]
    total_ref[...] = total
    for ref in send_refs:
        ref[...] = pack(total, block, small)


def project_kernel(steps, block, parts, total_rows, total_ref, high_ref, low_ref, near_ref, *refs):
    received, (out_ref, diagonal_ref) = refs[:-2], refs[-2:]
    me, core = lax.axis_index("rows"), lax.axis_index("sub")
    small = block // parts
    total = total_ref[...]
    stored, diagonal = total[0:block], total[block : block + small]
    same, other = total[block + small :], jnp.zeros((block // 2, total.shape[1]), f32)
    for step, ref in zip(steps, received):
        message = ref[...].astype(f32)
        stored = stored + message[0:block]
        diagonal = diagonal + message[block : block + small]
        diagonal = diagonal + message[block + small : block + 2 * small]
        part = message[block + 2 * small :]
        if step % 2:
            other = other + part
        else:
            same = same + part
    even = jnp.bitwise_and(me, 1) == 0
    corr = jnp.concatenate([jnp.where(even, same, other), jnp.where(even, other, same)], axis=0)
    scale = 1.0 / total_rows
    diagonal = unfold(diagonal * scale, parts)
    diagonal_ref[...] = diagonal
    projection = stored * scale - dot_split(split(diagonal), split(corr * scale), NN)
    weights = split(jnp.concatenate([projection, jnp.where(core == 0, diagonal, 0.0)], axis=1))
    for k, ref in enumerate((high_ref, near_ref)):
        rounded = dot_bf16(weights[0], ref[...], NN) + dot_bf16(weights[1], ref[...], NN)
        out_ref[k * block : (k + 1) * block, :] = rounded
    out_ref[2 * block :, :] = dot_bf16(weights[0], low_ref[...], NN)


def gram_kernel(mine_ref, other_ref, y_ref, z_ref, images_ref, full_ref, half_ref):
    block = images_ref.shape[0]
    removed = mine_ref[...] + other_ref[...]
    images = y_ref[...] - removed[0:block]
    images_ref[...] = images - removed[2 * block :]
    gram = 0.0
    for x in (images, z_ref[...] - removed[block : 2 * block]):
        halves = split(x)
        gram = gram + dot_split(halves, halves, NT)
    gram = fold(gram, 2)
    full_ref[...] = gram
    middle = half_ref.shape[0]
    half_ref[...] = jnp.where(lax.axis_index("sub") == 0, gram[:middle], gram[middle:])


def factor_kernel(pairs, total_rows, own_ref, images_ref, d_ref, *refs):
    received, (following_ref, coupling_ref, diagonal_ref) = refs[:-3], refs[-3:]
    block = images_ref.shape[0]
    lanes = 2 * block
    core = lax.axis_index("sub")
    gram = own_ref[...]
    for k, pair in enumerate(pairs):
        mine, other = received[2 * k][...], received[2 * k + 1][...]
        if pair[0] != pair[1]:
            gram = gram + (mine + other)
        else:
            first, second = jnp.where(core == 0, mine, other), jnp.where(core == 0, other, mine)
            gram = gram + jnp.concatenate([first, second], axis=0)
    gram = gram * (1.0 / total_rows)
    row = lax.broadcasted_iota(jnp.int32, (block, lanes), 0)
    column = lax.broadcasted_iota(jnp.int32, (block, lanes), 1)
    left = column < block
    m = jnp.concatenate([gram, pltpu.roll(gram, block, 1)], axis=0)
    m = jnp.where(left, m, jnp.where(column == row + block, 1.0, 0.0))
    finished = []
    for start in range(0, block, GROUP):
        spread = [
            jnp.broadcast_to(m[:, start + p : start + p + 1], m.shape) for p in range(GROUP)
        ]
        for p in range(GROUP):
            at = p % 8
            root = lax.rsqrt(spread[p][at : at + 1])
            lower = spread[p] * root
            done = m[at : at + 1] * root
            finished.append(done)
            for q in range(p + 1, GROUP):
                pivot = q - p + at
                spread[q] = spread[q] - lower * lower[pivot : pivot + 1]
            m = m - lower * done
            if at == 7:
                m = m[8:]
                spread = [column[8:] for column in spread]
    done = jnp.concatenate(finished, axis=0)
    coupling_ref[...] = jnp.where((row <= column) & left, done, 0.0)[:, 0:block]
    inverse = jnp.where((row + block >= column) & ~left, done, 0.0)
    images = images_ref[...]
    images = jnp.concatenate([images, images], axis=0)
    following_ref[...] = dot_split(split(inverse), split(images), NN)
    diagonal_ref[...] = d_ref[...].T


def exchange(x, axis, distance):
    return lax.ppermute(x, axis, [(i, i ^ distance) for i in range(lax.axis_size(axis))])


def local(
    tile_index,
    tile_values,
    onsite_energy,
    start_block,
    previous_block,
    previous_coupling,
    stored_basis,
):
    rows, block = start_block.shape
    bands, columns = lax.axis_size("rows"), lax.axis_size("cols")
    cores = lax.axis_size("sub")
    stored = stored_basis.shape[0]
    width = stored * block
    total_rows = rows * bands * columns
    parts = width // block
    chunk = block // 2
    assert rows == tile_values.shape[1] and cores == 2 and width == rows
    assert bands > 1 and columns > 1 and bands & (bands - 1) == 0 and columns & (columns - 1) == 0
    half = (block, rows)
    swap = [(0, 1), (1, 0)]
    other_tiles = lax.ppermute(tile_values, "sub", swap)
    other_index = lax.ppermute(tile_index, "sub", swap)
    prepare = call(
        prepare_kernel,
        [
            (half, f32), ((2, chunk, width), f32), *[((width + block, rows), bf16)] * 2,
            (tile_values.shape, bf16), (tile_index.shape, jnp.int32),
        ],
        "hhhhhhh",
        [
            pltpu.VMEM(half, f32), pltpu.VMEM((1, rows), f32), pltpu.VMEM(half, f32),
            pltpu.VMEM((block, block), f32), pltpu.VMEM((width, rows), f32),
            pltpu.SemaphoreType.DMA((7,)),
        ],
    )
    sources = (
        start_block.T, onsite_energy.reshape(1, rows), previous_block.T, previous_coupling,
        stored_basis.transpose(0, 2, 1).reshape(width, rows), tile_values, tile_index,
    )
    base, corr, high, low, tiles, index = prepare(
        *(pltpu.with_memory_space_constraint(a, pltpu.HBM) for a in sources)
    )
    pairs = [(step - 1, step) for step in range(bands - 1, 1, -2)] + [(1, 1)]

    def serve(sends):
        received = []
        for send, pair in zip(sends, pairs):
            moves = [(2 * r + c, 2 * (r ^ pair[c]) + c) for r in range(bands) for c in range(2)]
            received.append(lax.ppermute(send, ("rows", "sub"), moves))
        swapped = []
        for x, pair in zip(received, pairs):
            swapped += [x, lax.ppermute(x, "sub", swap)]
        return swapped

    sends = call(
        functools.partial(push_kernel, pairs, columns),
        [((block + chunk, rows), f32)]
        + [((2 * block, rows) if a != b else (4 * block, rows // 2), bf16) for a, b in pairs],
        "vvvvvv",
    )(index, other_index, high, corr, tiles, other_tiles)
    near = exchange(high, "cols", 1)
    received = serve(sends[1:])
    small = block // parts
    y, mine = call(
        functools.partial(image_kernel, pairs, columns, parts),
        [(half, f32), ((block + small + chunk, rows), f32)],
        "v" * (8 + len(received)),
    )(index, other_index, base, high, low, tiles, other_tiles, sends[0], *received)
    other = exchange(mine, "cols", 1)
    late = exchange(y, "cols", 1)
    distances = [2**k for k in range(1, columns.bit_length() - 1)]
    total, *send = call(
        functools.partial(combine_kernel, block, small),
        [((block + small + chunk, rows), f32)]
        + [((block + 2 * small + chunk, rows), bf16)] * (not distances),
        "vv",
    )(mine, other)
    for distance in distances:
        total = total + exchange(total, "cols", distance)
    send = send[0] if send else pack(total, block, small)
    steps = [*range(2, bands), 1]
    received = []
    for step in steps:
        received.append(exchange(send, "rows", step))
    project = call(
        functools.partial(project_kernel, steps, block, parts, total_rows),
        [((3 * block, rows), f32), ((block, block), f32)],
        "v" * (3 + bands),
    )
    removed, diagonal = project(total, high, low, near, *received)
    images, full, part = call(
        gram_kernel,
        [(half, f32), ((block // 2, 2 * block), f32), ((block // 4, 2 * block), f32)],
        "vvvv",
    )(removed, lax.ppermute(removed, "sub", swap), y, late)
    for distance in distances:
        full = full + exchange(full, "cols", distance)
        middle = part.shape[0]
        part = jnp.where(lax.axis_index("sub") == 0, full[:middle], full[middle:])
    following, coupling, diagonal = call(
        functools.partial(factor_kernel, pairs, total_rows),
        [(half, f32), ((block, block), f32), ((block, block), f32)],
        "v" * (3 + 2 * len(pairs)),
    )(full, images, diagonal, *serve([full] * (len(pairs) - 1) + [part]))
    return following.T[None], diagonal[None], coupling[None]


def solution(mesh):
    return jax.shard_map(
        local,
        mesh=mesh,
        in_specs=(
            P(("groups", "rows", "cols", "sub"), None),
            P(("groups", "rows", "cols", "sub"), None, None),
            P(("groups", "rows", "cols")),
            P(("groups", "rows", "cols"), None),
            P(("groups", "rows", "cols"), None),
            P("groups", None),
            P("sub", ("groups", "rows", "cols"), None),
        ),
        out_specs=(
            P(None, ("groups", "rows", "cols"), None),
            P(None, "groups", None),
            P(None, "groups", None),
        ),
        check_vma=False,
    )
```

```python
import functools

import jax
import jax.numpy as jnp
from jax import lax
from jax.experimental import pallas as pl
from jax.experimental.pallas import tpu as pltpu
from jax.sharding import PartitionSpec as P

f32 = jnp.float32
bf16 = jnp.bfloat16
GROUPS = (16,)
GRANT = 16 * 1024 * 1024
NN = (((1,), (0,)), ((), ()))
NT = (((1,), (1,)), ((), ()))


def split(x):
    high = x.astype(bf16)
    return high, (x - high.astype(f32)).astype(bf16)


def dot_bf16(a, b, dims):
    return lax.dot_general(a, b, dims, preferred_element_type=f32)


def dot_split(a, b, dims):
    (ah, al), (bh, bl) = a, b
    return dot_bf16(ah, bh, dims) + dot_bf16(ah, bl, dims) + dot_bf16(al, bh, dims)


def fold(x, parts):
    rows = x.shape[0] // parts
    return jnp.concatenate([x[i * rows : (i + 1) * rows] for i in range(parts)], axis=1)


def unfold(x, parts):
    lanes = x.shape[1] // parts
    return jnp.concatenate([x[:, i * lanes : (i + 1) * lanes] for i in range(parts)], axis=0)


def call(kernel, outs, ins, scratch=(), work=40000000):
    spaces = {"v": pltpu.VMEM, "h": pltpu.HBM}
    return pl.pallas_call(
        kernel,
        out_shape=[jax.ShapeDtypeStruct(s, d) for s, d in outs],
        in_specs=[pl.BlockSpec(memory_space=spaces[c]) for c in ins],
        out_specs=[pl.BlockSpec(memory_space=pltpu.VMEM)] * len(outs),
        scratch_shapes=list(scratch),
        cost_estimate=pl.CostEstimate(flops=work, bytes_accessed=1000000, transcendentals=0),
        compiler_params=pltpu.CompilerParams(vmem_limit_bytes=GRANT),
    )


def prepare_kernel(
    x_hbm, e_hbm, p_hbm, c_hbm, s_hbm, t_hbm, i_hbm,
    base_ref, corr_ref, high_ref, low_ref, t_ref, i_ref,
    x_ref, e_ref, p_ref, c_ref, s_ref, sems,
):
    pairs = (
        (s_hbm, s_ref), (x_hbm, x_ref), (p_hbm, p_ref), (c_hbm, c_ref),
        (e_hbm, e_ref), (t_hbm, t_ref), (i_hbm, i_ref),
    )
    copies = [pltpu.make_async_copy(a, b, sems.at[k]) for k, (a, b) in enumerate(pairs)]
    for copy in copies:
        copy.start()
    for copy in copies[:5]:
        copy.wait()
    block = x_ref.shape[0]
    row = lax.broadcasted_iota(jnp.int32, (block, block), 0)
    column = lax.broadcasted_iota(jnp.int32, (block, block), 1)
    coupling = jnp.where(row <= column, c_ref[...], 0.0)
    x = x_ref[...]
    xs = split(x)
    ss = split(s_ref[...])
    for k, ref in enumerate((high_ref, low_ref)):
        ref[...] = jnp.concatenate([ss[k], xs[k]], axis=0)
    base_ref[...] = e_ref[...] * x - dot_split(split(coupling), split(p_ref[...]), NN)
    corr = dot_split(xs, ss, NT)
    chunk = corr_ref.shape[1]
    for band in range(corr_ref.shape[0]):
        corr_ref[band] = corr[band * chunk : (band + 1) * chunk]
    for copy in copies[5:]:
        copy.wait()


def tile_columns(index_refs, shape):
    found = []
    for ref in index_refs:
        index = ref[...]
        for k in range(ref.shape[0]):
            found.append(jnp.broadcast_to(index[k : k + 1, 1:2], shape))
    return found


def target_band(me, core, pair):
    return jnp.bitwise_xor(me, jnp.where(core == 0, pair[0], pair[1]))


def push_kernel(pairs, columns, i_ref, j_ref, high_ref, corr_ref, t_ref, u_ref, *outs):
    width, rows = corr_ref.shape[2], high_ref.shape[1]
    block = high_ref.shape[0] - width
    x = high_ref[width:]
    me, core = lax.axis_index("rows"), lax.axis_index("sub")
    targets = tile_columns((i_ref, j_ref), (block, rows))
    products = [dot_bf16(x, ref[k], NN) for ref in (t_ref, u_ref) for k in range(ref.shape[0])]

    def pushed(band):
        first = band * columns
        total = jnp.zeros((block, rows), f32)
        for target, product in zip(targets, products):
            inside = (target >= first) & (target < first + columns)
            total = total + jnp.where(inside, product, 0.0)
        return total

    parity = jnp.bitwise_and(me, 1)
    outs[0][...] = jnp.concatenate([pushed(me), corr_ref[parity]], axis=0)
    for ref, pair in zip(outs[1:], pairs):
        message = jnp.concatenate([x.astype(f32), pushed(target_band(me, core, pair))], axis=0)
        if pair[0] != pair[1]:
            ref[...] = message.astype(bf16)
        else:
            message = jnp.where(core == 0, message[:, : rows // 2], message[:, rows // 2 :])
            halves = [unfold(h.astype(f32), 2) for h in split(corr_ref[1 - parity])]
            ref[...] = jnp.concatenate([message, *halves], axis=0).astype(bf16)


def image_kernel(pairs, columns, parts, i_ref, j_ref, base_ref, high_ref, low_ref, t_ref, u_ref, own_ref, *refs):
    received, (y_ref, send_ref) = refs[:-2], refs[-2:]
    block, rows = base_ref.shape
    width = high_ref.shape[0] - block
    me, core = lax.axis_index("rows"), lax.axis_index("sub")
    y = base_ref[...] + own_ref[0:block]
    corr = own_ref[block:]
    blocks = [(me, high_ref[width:].astype(f32))]
    for k, pair in enumerate(pairs):
        mine, other = received[2 * k][...].astype(f32), received[2 * k + 1][...].astype(f32)
        if pair[0] != pair[1]:
            found = [(target_band(me, core, pair), mine), (target_band(me, core, pair[::-1]), other)]
        else:
            parts_of = mine[2 * block :]
            count = parts_of.shape[0] // 2
            corr = corr + fold(parts_of[:count] + parts_of[count:], 2)
            mine, other = mine[: 2 * block], other[: 2 * block]
            first, second = jnp.where(core == 0, mine, other), jnp.where(core == 0, other, mine)
            found = [(jnp.bitwise_xor(me, pair[0]), jnp.concatenate([first, second], axis=1))]
        for band, message in found:
            blocks.append((band, message[0:block]))
            y = y + message[block:]
    tiles = [ref[k] for ref in (t_ref, u_ref) for k in range(ref.shape[0])]
    for target, tile in zip(tile_columns((i_ref, j_ref), (block, rows)), tiles):
        source = jnp.zeros((block, rows), f32)
        for band, held in blocks:
            first = band * columns
            inside = (target >= first) & (target < first + columns)
            source = jnp.where(inside, held, source)
        source = source.astype(bf16)
        halves = [dot_bf16(source, tile[k * rows // 2 : (k + 1) * rows // 2], NT) for k in range(2)]
        y = y + jnp.concatenate(halves, axis=1)
    y_ref[...] = y
    halves = split(y)
    stored = dot_split(halves, (high_ref[:width], low_ref[:width]), NT)
    diagonal = dot_split(halves, (high_ref[width:], low_ref[width:]), NT)
    send_ref[...] = jnp.concatenate([stored, fold(diagonal, parts), corr], axis=0)


def pack(total, block, small):
    high, low = split(total[block : block + small])
    message = [total[0:block], high.astype(f32), low.astype(f32), total[block + small :]]
    return jnp.concatenate(message, axis=0).astype(bf16)


def combine_kernel(block, small, mine_ref, other_ref, total_ref, *send_refs):
    total = mine_ref[...] + other_ref[...]
    total_ref[...] = total
    for ref in send_refs:
        ref[...] = pack(total, block, small)


def project_kernel(steps, block, parts, total_rows, total_ref, high_ref, low_ref, near_ref, *refs):
    received, (out_ref, diagonal_ref) = refs[:-2], refs[-2:]
    me, core = lax.axis_index("rows"), lax.axis_index("sub")
    small = block // parts
    total = total_ref[...]
    stored, diagonal = total[0:block], total[block : block + small]
    same, other = total[block + small :], jnp.zeros((block // 2, total.shape[1]), f32)
    for step, ref in zip(steps, received):
        message = ref[...].astype(f32)
        stored = stored + message[0:block]
        diagonal = diagonal + message[block : block + small]
        diagonal = diagonal + message[block + small : block + 2 * small]
        part = message[block + 2 * small :]
        if step % 2:
            other = other + part
        else:
            same = same + part
    even = jnp.bitwise_and(me, 1) == 0
    corr = jnp.concatenate([jnp.where(even, same, other), jnp.where(even, other, same)], axis=0)
    scale = 1.0 / total_rows
    diagonal = unfold(diagonal * scale, parts)
    diagonal_ref[...] = diagonal
    projection = stored * scale - dot_split(split(diagonal), split(corr * scale), NN)
    weights = split(jnp.concatenate([projection, jnp.where(core == 0, diagonal, 0.0)], axis=1))
    for k, ref in enumerate((high_ref, near_ref)):
        rounded = dot_bf16(weights[0], ref[...], NN) + dot_bf16(weights[1], ref[...], NN)
        out_ref[k * block : (k + 1) * block, :] = rounded
    out_ref[2 * block :, :] = dot_bf16(weights[0], low_ref[...], NN)


def gram_kernel(mine_ref, other_ref, y_ref, z_ref, images_ref, full_ref, half_ref):
    block = images_ref.shape[0]
    removed = mine_ref[...] + other_ref[...]
    images = y_ref[...] - removed[0:block]
    images_ref[...] = images - removed[2 * block :]
    gram = 0.0
    for x in (images, z_ref[...] - removed[block : 2 * block]):
        halves = split(x)
        gram = gram + dot_split(halves, halves, NT)
    gram = fold(gram, 2)
    full_ref[...] = gram
    middle = half_ref.shape[0]
    half_ref[...] = jnp.where(lax.axis_index("sub") == 0, gram[:middle], gram[middle:])


def factor_kernel(pairs, total_rows, own_ref, images_ref, d_ref, *refs):
    received, (following_ref, coupling_ref, diagonal_ref) = refs[:-3], refs[-3:]
    block = images_ref.shape[0]
    lanes = 2 * block
    core = lax.axis_index("sub")
    gram = own_ref[...]
    for k, pair in enumerate(pairs):
        mine, other = received[2 * k][...], received[2 * k + 1][...]
        if pair[0] != pair[1]:
            gram = gram + (mine + other)
        else:
            first, second = jnp.where(core == 0, mine, other), jnp.where(core == 0, other, mine)
            gram = gram + jnp.concatenate([first, second], axis=0)
    gram = gram * (1.0 / total_rows)
    row = lax.broadcasted_iota(jnp.int32, (block, lanes), 0)
    column = lax.broadcasted_iota(jnp.int32, (block, lanes), 1)
    left = column < block
    m = jnp.concatenate([gram, pltpu.roll(gram, block, 1)], axis=0)
    m = jnp.where(left, m, jnp.where(column == row + block, 1.0, 0.0))
    finished = []
    while len(finished) < block:
        start = len(finished)
        group = min(GROUPS[start * len(GROUPS) // block], block - start)
        spread = [
            jnp.broadcast_to(m[:, start + p : start + p + 1], m.shape) for p in range(group)
        ]
        for p in range(group):
            at = p % 8
            pivot = spread[p][at : at + 1]
            lower = spread[p] * (1.0 / pivot)
            done = m[at : at + 1]
            finished.append(done * lax.rsqrt(pivot))
            for q in range(p + 1, group):
                other = q - p + at
                spread[q] = spread[q] - lower * spread[p][other : other + 1]
            m = m - lower * done
            if at == 7:
                m = m[8:]
                spread = [column[8:] for column in spread]
    done = jnp.concatenate(finished, axis=0)
    coupling_ref[...] = jnp.where((row <= column) & left, done, 0.0)[:, 0:block]
    inverse = jnp.where((row + block >= column) & ~left, done, 0.0)
    images = images_ref[...]
    images = jnp.concatenate([images, images], axis=0)
    following_ref[...] = dot_split(split(inverse), split(images), NN)
    diagonal_ref[...] = d_ref[...].T


def exchange(x, axis, distance):
    return lax.ppermute(x, axis, [(i, i ^ distance) for i in range(lax.axis_size(axis))])


def local(
    tile_index,
    tile_values,
    onsite_energy,
    start_block,
    previous_block,
    previous_coupling,
    stored_basis,
):
    rows, block = start_block.shape
    bands, columns = lax.axis_size("rows"), lax.axis_size("cols")
    cores = lax.axis_size("sub")
    stored = stored_basis.shape[0]
    width = stored * block
    total_rows = rows * bands * columns
    parts = width // block
    chunk = block // 2
    assert rows == tile_values.shape[1] and cores == 2 and width == rows
    assert bands > 1 and columns > 1 and bands & (bands - 1) == 0 and columns & (columns - 1) == 0
    half = (block, rows)
    swap = [(0, 1), (1, 0)]
    other_tiles = lax.ppermute(tile_values, "sub", swap)
    other_index = lax.ppermute(tile_index, "sub", swap)
    prepare = call(
        prepare_kernel,
        [
            (half, f32), ((2, chunk, width), f32), *[((width + block, rows), bf16)] * 2,
            (tile_values.shape, bf16), (tile_index.shape, jnp.int32),
        ],
        "hhhhhhh",
        [
            pltpu.VMEM(half, f32), pltpu.VMEM((1, rows), f32), pltpu.VMEM(half, f32),
            pltpu.VMEM((block, block), f32), pltpu.VMEM((width, rows), f32),
            pltpu.SemaphoreType.DMA((7,)),
        ],
    )
    sources = (
        start_block.T, onsite_energy.reshape(1, rows), previous_block.T, previous_coupling,
        stored_basis.transpose(0, 2, 1).reshape(width, rows), tile_values, tile_index,
    )
    base, corr, high, low, tiles, index = prepare(
        *(pltpu.with_memory_space_constraint(a, pltpu.HBM) for a in sources)
    )
    pairs = [(step - 1, step) for step in range(bands - 1, 1, -2)] + [(1, 1)]

    def serve(sends):
        received = []
        for send, pair in zip(sends, pairs):
            moves = [(2 * r + c, 2 * (r ^ pair[c]) + c) for r in range(bands) for c in range(2)]
            received.append(lax.ppermute(send, ("rows", "sub"), moves))
        swapped = []
        for x, pair in zip(received, pairs):
            swapped += [x, lax.ppermute(x, "sub", swap)]
        return swapped

    sends = call(
        functools.partial(push_kernel, pairs, columns),
        [((block + chunk, rows), f32)]
        + [((2 * block, rows) if a != b else (4 * block, rows // 2), bf16) for a, b in pairs],
        "vvvvvv",
    )(index, other_index, high, corr, tiles, other_tiles)
    near = exchange(high, "cols", 1)
    received = serve(sends[1:])
    small = block // parts
    y, mine = call(
        functools.partial(image_kernel, pairs, columns, parts),
        [(half, f32), ((block + small + chunk, rows), f32)],
        "v" * (8 + len(received)),
    )(index, other_index, base, high, low, tiles, other_tiles, sends[0], *received)
    other = exchange(mine, "cols", 1)
    late = exchange(y, "cols", 1)
    distances = [2**k for k in range(1, columns.bit_length() - 1)]
    total, *send = call(
        functools.partial(combine_kernel, block, small),
        [((block + small + chunk, rows), f32)]
        + [((block + 2 * small + chunk, rows), bf16)] * (not distances),
        "vv",
    )(mine, other)
    for distance in distances:
        total = total + exchange(total, "cols", distance)
    send = send[0] if send else pack(total, block, small)
    steps = [*range(2, bands), 1]
    received = []
    for step in steps:
        received.append(exchange(send, "rows", step))
    project = call(
        functools.partial(project_kernel, steps, block, parts, total_rows),
        [((3 * block, rows), f32), ((block, block), f32)],
        "v" * (3 + bands),
    )
    removed, diagonal = project(total, high, low, near, *received)
    images, full, part = call(
        gram_kernel,
        [(half, f32), ((block // 2, 2 * block), f32), ((block // 4, 2 * block), f32)],
        "vvvv",
    )(removed, lax.ppermute(removed, "sub", swap), y, late)
    for distance in distances:
        full = full + exchange(full, "cols", distance)
        middle = part.shape[0]
        part = jnp.where(lax.axis_index("sub") == 0, full[:middle], full[middle:])
    following, coupling, diagonal = call(
        functools.partial(factor_kernel, pairs, total_rows),
        [(half, f32), ((block, block), f32), ((block, block), f32)],
        "v" * (3 + 2 * len(pairs)),
    )(full, images, diagonal, *serve([full] * (len(pairs) - 1) + [part]))
    return following.T[None], diagonal[None], coupling[None]


def solution(mesh):
    return jax.shard_map(
        local,
        mesh=mesh,
        in_specs=(
            P(("groups", "rows", "cols", "sub"), None),
            P(("groups", "rows", "cols", "sub"), None, None),
            P(("groups", "rows", "cols")),
            P(("groups", "rows", "cols"), None),
            P(("groups", "rows", "cols"), None),
            P("groups", None),
            P("sub", ("groups", "rows", "cols"), None),
        ),
        out_specs=(
            P(None, ("groups", "rows", "cols"), None),
            P(None, "groups", None),
            P(None, "groups", None),
        ),
        check_vma=False,
    )
```

```python
import functools

import jax
import jax.numpy as jnp
from jax import lax
from jax.experimental import pallas as pl
from jax.experimental.pallas import tpu as pltpu
from jax.sharding import PartitionSpec as P

f32 = jnp.float32
bf16 = jnp.bfloat16
GROUP = 16
GRANT = 16 * 1024 * 1024
NN = (((1,), (0,)), ((), ()))
NT = (((1,), (1,)), ((), ()))


def split(x):
    high = x.astype(bf16)
    return high, (x - high.astype(f32)).astype(bf16)


def dot_bf16(a, b, dims):
    return lax.dot_general(a, b, dims, preferred_element_type=f32)


def dot_split(a, b, dims):
    (ah, al), (bh, bl) = a, b
    return dot_bf16(ah, bh, dims) + dot_bf16(ah, bl, dims) + dot_bf16(al, bh, dims)


def dot_stacked(a, b, dims):
    (ah, al), (bh, bl) = a, b
    rows = ah.shape[0]
    both = dot_bf16(jnp.concatenate([ah, al], axis=0), bh, dims)
    return both[:rows] + both[rows:] + dot_bf16(ah, bl, dims)


def fold(x, parts):
    rows = x.shape[0] // parts
    return jnp.concatenate([x[i * rows : (i + 1) * rows] for i in range(parts)], axis=1)


def unfold(x, parts):
    lanes = x.shape[1] // parts
    return jnp.concatenate([x[:, i * lanes : (i + 1) * lanes] for i in range(parts)], axis=0)


def call(kernel, outs, ins, scratch=(), work=40000000):
    spaces = {"v": pltpu.VMEM, "h": pltpu.HBM}
    return pl.pallas_call(
        kernel,
        out_shape=[jax.ShapeDtypeStruct(s, d) for s, d in outs],
        in_specs=[pl.BlockSpec(memory_space=spaces[c]) for c in ins],
        out_specs=[pl.BlockSpec(memory_space=pltpu.VMEM)] * len(outs),
        scratch_shapes=list(scratch),
        cost_estimate=pl.CostEstimate(flops=work, bytes_accessed=1000000, transcendentals=0),
        compiler_params=pltpu.CompilerParams(vmem_limit_bytes=GRANT),
    )


def prepare_kernel(
    x_hbm, e_hbm, p_hbm, c_hbm, s_hbm, t_hbm, i_hbm,
    base_ref, corr_ref, high_ref, low_ref, t_ref, i_ref,
    x_ref, e_ref, p_ref, c_ref, s_ref, sems,
):
    pairs = (
        (s_hbm, s_ref), (x_hbm, x_ref), (p_hbm, p_ref), (c_hbm, c_ref),
        (e_hbm, e_ref), (t_hbm, t_ref), (i_hbm, i_ref),
    )
    copies = [pltpu.make_async_copy(a, b, sems.at[k]) for k, (a, b) in enumerate(pairs)]
    for copy in copies:
        copy.start()
    for copy in copies[:5]:
        copy.wait()
    block = x_ref.shape[0]
    row = lax.broadcasted_iota(jnp.int32, (block, block), 0)
    column = lax.broadcasted_iota(jnp.int32, (block, block), 1)
    coupling = jnp.where(row <= column, c_ref[...], 0.0)
    x = x_ref[...]
    xs = split(x)
    ss = split(s_ref[...])
    for k, ref in enumerate((high_ref, low_ref)):
        ref[...] = jnp.concatenate([ss[k], xs[k]], axis=0)
    base_ref[...] = e_ref[...] * x - dot_stacked(split(coupling), split(p_ref[...]), NN)
    corr = dot_stacked(xs, ss, NT)
    chunk = corr_ref.shape[1]
    for band in range(corr_ref.shape[0]):
        corr_ref[band] = corr[band * chunk : (band + 1) * chunk]
    for copy in copies[5:]:
        copy.wait()


def tile_columns(index_refs, shape):
    found = []
    for ref in index_refs:
        index = ref[...]
        for k in range(ref.shape[0]):
            found.append(jnp.broadcast_to(index[k : k + 1, 1:2], shape))
    return found


def target_band(me, core, pair):
    return jnp.bitwise_xor(me, jnp.where(core == 0, pair[0], pair[1]))


def push_kernel(pairs, columns, i_ref, j_ref, high_ref, corr_ref, t_ref, u_ref, *outs):
    width, rows = corr_ref.shape[2], high_ref.shape[1]
    block = high_ref.shape[0] - width
    x = high_ref[width:]
    me, core = lax.axis_index("rows"), lax.axis_index("sub")
    targets = tile_columns((i_ref, j_ref), (block, rows))
    products = [dot_bf16(x, ref[k], NN) for ref in (t_ref, u_ref) for k in range(ref.shape[0])]

    def pushed(band):
        first = band * columns
        total = jnp.zeros((block, rows), f32)
        for target, product in zip(targets, products):
            inside = (target >= first) & (target < first + columns)
            total = total + jnp.where(inside, product, 0.0)
        return total

    parity = jnp.bitwise_and(me, 1)
    outs[0][...] = jnp.concatenate([pushed(me), corr_ref[parity]], axis=0)
    for ref, pair in zip(outs[1:], pairs):
        message = jnp.concatenate([x.astype(f32), pushed(target_band(me, core, pair))], axis=0)
        if pair[0] != pair[1]:
            ref[...] = message.astype(bf16)
        else:
            message = jnp.where(core == 0, message[:, : rows // 2], message[:, rows // 2 :])
            halves = [unfold(h.astype(f32), 2) for h in split(corr_ref[1 - parity])]
            ref[...] = jnp.concatenate([message, *halves], axis=0).astype(bf16)


def image_kernel(pairs, columns, parts, i_ref, j_ref, base_ref, high_ref, low_ref, t_ref, u_ref, own_ref, *refs):
    received, (y_ref, send_ref) = refs[:-2], refs[-2:]
    block, rows = base_ref.shape
    width = high_ref.shape[0] - block
    me, core = lax.axis_index("rows"), lax.axis_index("sub")
    y = base_ref[...] + own_ref[0:block]
    corr = own_ref[block:]
    blocks = [(me, high_ref[width:].astype(f32))]
    for k, pair in enumerate(pairs):
        mine, other = received[2 * k][...].astype(f32), received[2 * k + 1][...].astype(f32)
        if pair[0] != pair[1]:
            found = [(target_band(me, core, pair), mine), (target_band(me, core, pair[::-1]), other)]
        else:
            parts_of = mine[2 * block :]
            count = parts_of.shape[0] // 2
            corr = corr + fold(parts_of[:count] + parts_of[count:], 2)
            mine, other = mine[: 2 * block], other[: 2 * block]
            first, second = jnp.where(core == 0, mine, other), jnp.where(core == 0, other, mine)
            found = [(jnp.bitwise_xor(me, pair[0]), jnp.concatenate([first, second], axis=1))]
        for band, message in found:
            blocks.append((band, message[0:block]))
            y = y + message[block:]
    tiles = [ref[k] for ref in (t_ref, u_ref) for k in range(ref.shape[0])]
    for target, tile in zip(tile_columns((i_ref, j_ref), (block, rows)), tiles):
        source = jnp.zeros((block, rows), f32)
        for band, held in blocks:
            first = band * columns
            inside = (target >= first) & (target < first + columns)
            source = jnp.where(inside, held, source)
        source = source.astype(bf16)
        halves = [dot_bf16(source, tile[k * rows // 2 : (k + 1) * rows // 2], NT) for k in range(2)]
        y = y + jnp.concatenate(halves, axis=1)
    y_ref[...] = y
    halves = split(y)
    diagonal = fold(dot_split(halves, (high_ref[width:], low_ref[width:]), NT), parts)
    stored = dot_split(halves, (high_ref[:width], low_ref[:width]), NT)
    send_ref[...] = jnp.concatenate([stored, diagonal, corr], axis=0)


def pack(total, block, small):
    high, low = split(total[block : block + small])
    message = [total[0:block], high.astype(f32), low.astype(f32), total[block + small :]]
    return jnp.concatenate(message, axis=0).astype(bf16)


def combine_kernel(block, small, mine_ref, other_ref, total_ref, *send_refs):
    total = mine_ref[...] + other_ref[...]
    total_ref[...] = total
    for ref in send_refs:
        ref[...] = pack(total, block, small)


def project_kernel(steps, block, parts, total_rows, total_ref, high_ref, low_ref, near_ref, *refs):
    received, (out_ref, diagonal_ref) = refs[:-2], refs[-2:]
    me, core = lax.axis_index("rows"), lax.axis_index("sub")
    small = block // parts
    total = total_ref[...]
    stored, diagonal = total[0:block], total[block : block + small]
    same, other = total[block + small :], jnp.zeros((block // 2, total.shape[1]), f32)
    for step, ref in zip(steps, received):
        message = ref[...].astype(f32)
        stored = stored + message[0:block]
        diagonal = diagonal + message[block : block + small]
        diagonal = diagonal + message[block + small : block + 2 * small]
        part = message[block + 2 * small :]
        if step % 2:
            other = other + part
        else:
            same = same + part
    even = jnp.bitwise_and(me, 1) == 0
    corr = jnp.concatenate([jnp.where(even, same, other), jnp.where(even, other, same)], axis=0)
    scale = 1.0 / total_rows
    diagonal = diagonal * scale
    lane = lax.broadcasted_iota(jnp.int32, diagonal.shape, 1)
    inside = [(lane >= k * block) & (lane < (k + 1) * block) for k in range(parts)]
    spread = jnp.concatenate([jnp.where(k, diagonal, 0.0) for k in inside], axis=0)
    many = [jnp.concatenate([h] * parts, axis=0) for h in split(corr * scale)]
    projection = stored * scale - dot_split(split(spread), many, NN)
    diagonal = unfold(diagonal, parts)
    diagonal_ref[...] = diagonal
    weights = split(jnp.concatenate([projection, jnp.where(core == 0, diagonal, 0.0)], axis=1))
    for k, ref in enumerate((high_ref, near_ref)):
        rounded = dot_bf16(weights[0], ref[...], NN) + dot_bf16(weights[1], ref[...], NN)
        out_ref[k * block : (k + 1) * block, :] = rounded
    out_ref[2 * block :, :] = dot_bf16(weights[0], low_ref[...], NN)


def gram_kernel(mine_ref, other_ref, y_ref, z_ref, images_ref, full_ref, half_ref):
    block = images_ref.shape[0]
    removed = mine_ref[...] + other_ref[...]
    images = y_ref[...] - removed[0:block]
    images_ref[...] = images - removed[2 * block :]
    gram = 0.0
    for x in (images, z_ref[...] - removed[block : 2 * block]):
        halves = split(x)
        twice = [jnp.concatenate([h, h], axis=0) for h in halves]
        gram = gram + dot_stacked(halves, twice, NT)
    left = lax.broadcasted_iota(jnp.int32, full_ref.shape, 1) < block
    gram = jnp.where(left, gram[: block // 2], gram[block // 2 :])
    full_ref[...] = gram
    middle = half_ref.shape[0]
    half_ref[...] = jnp.where(lax.axis_index("sub") == 0, gram[:middle], gram[middle:])


def factor_kernel(pairs, total_rows, own_ref, images_ref, d_ref, *refs):
    received, (following_ref, coupling_ref, diagonal_ref) = refs[:-3], refs[-3:]
    block = images_ref.shape[0]
    lanes = 2 * block
    core = lax.axis_index("sub")
    gram = own_ref[...]
    for k, pair in enumerate(pairs):
        mine, other = received[2 * k][...], received[2 * k + 1][...]
        if pair[0] != pair[1]:
            gram = gram + (mine + other)
        else:
            first, second = jnp.where(core == 0, mine, other), jnp.where(core == 0, other, mine)
            gram = gram + jnp.concatenate([first, second], axis=0)
    gram = gram * (1.0 / total_rows)
    row = lax.broadcasted_iota(jnp.int32, (block, lanes), 0)
    column = lax.broadcasted_iota(jnp.int32, (block, lanes), 1)
    left = column < block
    m = jnp.concatenate([gram, pltpu.roll(gram, block, 1)], axis=0)
    m = jnp.where(left, m, jnp.where(column == row + block, 1.0, 0.0))
    finished = []
    for start in range(0, block, GROUP):
        spread = [
            jnp.broadcast_to(m[:, start + p : start + p + 1], m.shape) for p in range(GROUP)
        ]
        for p in range(GROUP):
            at = p % 8
            root = lax.rsqrt(spread[p][at : at + 1])
            lower = spread[p] * root
            done = m[at : at + 1] * root
            finished.append(done)
            for q in range(p + 1, GROUP):
                pivot = q - p + at
                spread[q] = spread[q] - lower * lower[pivot : pivot + 1]
            m = m - lower * done
            if at == 7:
                m = m[8:]
                spread = [column[8:] for column in spread]
    done = jnp.concatenate(finished, axis=0)
    coupling_ref[...] = jnp.where((row <= column) & left, done, 0.0)[:, 0:block]
    inverse = jnp.where((row + block >= column) & ~left, done, 0.0)
    images = images_ref[...]
    images = jnp.concatenate([images, images], axis=0)
    following_ref[...] = dot_split(split(inverse), split(images), NN)
    diagonal_ref[...] = d_ref[...].T


def exchange(x, axis, distance):
    return lax.ppermute(x, axis, [(i, i ^ distance) for i in range(lax.axis_size(axis))])


def local(
    tile_index,
    tile_values,
    onsite_energy,
    start_block,
    previous_block,
    previous_coupling,
    stored_basis,
):
    rows, block = start_block.shape
    bands, columns = lax.axis_size("rows"), lax.axis_size("cols")
    cores = lax.axis_size("sub")
    stored = stored_basis.shape[0]
    width = stored * block
    total_rows = rows * bands * columns
    parts = width // block
    chunk = block // 2
    assert rows == tile_values.shape[1] and cores == 2 and width == rows
    assert bands > 1 and columns > 1 and bands & (bands - 1) == 0 and columns & (columns - 1) == 0
    half = (block, rows)
    swap = [(0, 1), (1, 0)]
    other_tiles = lax.ppermute(tile_values, "sub", swap)
    other_index = lax.ppermute(tile_index, "sub", swap)
    prepare = call(
        prepare_kernel,
        [
            (half, f32), ((2, chunk, width), f32), *[((width + block, rows), bf16)] * 2,
            (tile_values.shape, bf16), (tile_index.shape, jnp.int32),
        ],
        "hhhhhhh",
        [
            pltpu.VMEM(half, f32), pltpu.VMEM((1, rows), f32), pltpu.VMEM(half, f32),
            pltpu.VMEM((block, block), f32), pltpu.VMEM((width, rows), f32),
            pltpu.SemaphoreType.DMA((7,)),
        ],
    )
    sources = (
        start_block.T, onsite_energy.reshape(1, rows), previous_block.T, previous_coupling,
        stored_basis.transpose(0, 2, 1).reshape(width, rows), tile_values, tile_index,
    )
    base, corr, high, low, tiles, index = prepare(
        *(pltpu.with_memory_space_constraint(a, pltpu.HBM) for a in sources)
    )
    pairs = [(step - 1, step) for step in range(bands - 1, 1, -2)] + [(1, 1)]

    def serve(sends):
        received = []
        for send, pair in zip(sends, pairs):
            moves = [(2 * r + c, 2 * (r ^ pair[c]) + c) for r in range(bands) for c in range(2)]
            received.append(lax.ppermute(send, ("rows", "sub"), moves))
        swapped = []
        for x, pair in zip(received, pairs):
            swapped += [x, lax.ppermute(x, "sub", swap)]
        return swapped

    sends = call(
        functools.partial(push_kernel, pairs, columns),
        [((block + chunk, rows), f32)]
        + [((2 * block, rows) if a != b else (4 * block, rows // 2), bf16) for a, b in pairs],
        "vvvvvv",
    )(index, other_index, high, corr, tiles, other_tiles)
    near = exchange(high, "cols", 1)
    received = serve(sends[1:])
    small = block // parts
    y, mine = call(
        functools.partial(image_kernel, pairs, columns, parts),
        [(half, f32), ((block + small + chunk, rows), f32)],
        "v" * (8 + len(received)),
    )(index, other_index, base, high, low, tiles, other_tiles, sends[0], *received)
    other = exchange(mine, "cols", 1)
    late = exchange(y, "cols", 1)
    distances = [2**k for k in range(1, columns.bit_length() - 1)]
    total, *send = call(
        functools.partial(combine_kernel, block, small),
        [((block + small + chunk, rows), f32)]
        + [((block + 2 * small + chunk, rows), bf16)] * (not distances),
        "vv",
    )(mine, other)
    for distance in distances:
        total = total + exchange(total, "cols", distance)
    send = send[0] if send else pack(total, block, small)
    steps = [*range(2, bands), 1]
    received = []
    for step in steps:
        received.append(exchange(send, "rows", step))
    project = call(
        functools.partial(project_kernel, steps, block, parts, total_rows),
        [((3 * block, rows), f32), ((block, block), f32)],
        "v" * (3 + bands),
    )
    removed, diagonal = project(total, high, low, near, *received)
    images, full, part = call(
        gram_kernel,
        [(half, f32), ((block // 2, 2 * block), f32), ((block // 4, 2 * block), f32)],
        "vvvv",
    )(removed, lax.ppermute(removed, "sub", swap), y, late)
    for distance in distances:
        full = full + exchange(full, "cols", distance)
        middle = part.shape[0]
        part = jnp.where(lax.axis_index("sub") == 0, full[:middle], full[middle:])
    following, coupling, diagonal = call(
        functools.partial(factor_kernel, pairs, total_rows),
        [(half, f32), ((block, block), f32), ((block, block), f32)],
        "v" * (3 + 2 * len(pairs)),
    )(full, images, diagonal, *serve([full] * (len(pairs) - 1) + [part]))
    return following.T[None], diagonal[None], coupling[None]


def solution(mesh):
    return jax.shard_map(
        local,
        mesh=mesh,
        in_specs=(
            P(("groups", "rows", "cols", "sub"), None),
            P(("groups", "rows", "cols", "sub"), None, None),
            P(("groups", "rows", "cols")),
            P(("groups", "rows", "cols"), None),
            P(("groups", "rows", "cols"), None),
            P("groups", None),
            P("sub", ("groups", "rows", "cols"), None),
        ),
        out_specs=(
            P(None, ("groups", "rows", "cols"), None),
            P(None, "groups", None),
            P(None, "groups", None),
        ),
        check_vma=False,
    )
```

```python
import functools

import jax
import jax.numpy as jnp
from jax import lax
from jax.experimental import pallas as pl
from jax.experimental.pallas import tpu as pltpu
from jax.sharding import PartitionSpec as P

f32 = jnp.float32
bf16 = jnp.bfloat16
GROUP = 16
GRANT = 16 * 1024 * 1024
NN = (((1,), (0,)), ((), ()))
NT = (((1,), (1,)), ((), ()))


def split(x):
    high = x.astype(bf16)
    return high, (x - high.astype(f32)).astype(bf16)


def dot_bf16(a, b, dims):
    return lax.dot_general(a, b, dims, preferred_element_type=f32)


def dot_split(a, b, dims):
    (ah, al), (bh, bl) = a, b
    return dot_bf16(ah, bh, dims) + dot_bf16(ah, bl, dims) + dot_bf16(al, bh, dims)


def dot_stacked(a, b, dims):
    (ah, al), (bh, bl) = a, b
    rows = ah.shape[0]
    both = dot_bf16(jnp.concatenate([ah, al], axis=0), bh, dims)
    return both[:rows] + both[rows:] + dot_bf16(ah, bl, dims)


def fold(x, parts):
    rows = x.shape[0] // parts
    return jnp.concatenate([x[i * rows : (i + 1) * rows] for i in range(parts)], axis=1)


def unfold(x, parts):
    lanes = x.shape[1] // parts
    return jnp.concatenate([x[:, i * lanes : (i + 1) * lanes] for i in range(parts)], axis=0)


def call(kernel, outs, ins, scratch=(), work=40000000):
    spaces = {"v": pltpu.VMEM, "h": pltpu.HBM}
    return pl.pallas_call(
        kernel,
        out_shape=[jax.ShapeDtypeStruct(s, d) for s, d in outs],
        in_specs=[pl.BlockSpec(memory_space=spaces[c]) for c in ins],
        out_specs=[pl.BlockSpec(memory_space=pltpu.VMEM)] * len(outs),
        scratch_shapes=list(scratch),
        cost_estimate=pl.CostEstimate(flops=work, bytes_accessed=1000000, transcendentals=0),
        compiler_params=pltpu.CompilerParams(vmem_limit_bytes=GRANT),
    )


def prepare_kernel(
    x_hbm, e_hbm, p_hbm, c_hbm, s_hbm, t_hbm, i_hbm,
    base_ref, corr_ref, high_ref, low_ref, t_ref, i_ref,
    x_ref, e_ref, p_ref, c_ref, s_ref, sems,
):
    pairs = (
        (s_hbm, s_ref), (x_hbm, x_ref), (p_hbm, p_ref), (c_hbm, c_ref),
        (e_hbm, e_ref), (t_hbm, t_ref), (i_hbm, i_ref),
    )
    copies = [pltpu.make_async_copy(a, b, sems.at[k]) for k, (a, b) in enumerate(pairs)]
    for copy in copies:
        copy.start()
    for copy in copies[:5]:
        copy.wait()
    block = x_ref.shape[0]
    row = lax.broadcasted_iota(jnp.int32, (block, block), 0)
    column = lax.broadcasted_iota(jnp.int32, (block, block), 1)
    coupling = jnp.where(row <= column, c_ref[...], 0.0)
    x = x_ref[...]
    xs = split(x)
    ss = split(s_ref[...])
    for k, ref in enumerate((high_ref, low_ref)):
        ref[...] = jnp.concatenate([ss[k], xs[k]], axis=0)
    base_ref[...] = e_ref[...] * x - dot_stacked(split(coupling), split(p_ref[...]), NN)
    corr = dot_stacked(xs, ss, NT)
    chunk = corr_ref.shape[1]
    for band in range(corr_ref.shape[0]):
        corr_ref[band] = corr[band * chunk : (band + 1) * chunk]
    for copy in copies[5:]:
        copy.wait()


def tile_columns(index_refs, shape):
    found = []
    for ref in index_refs:
        index = ref[...]
        for k in range(ref.shape[0]):
            found.append(jnp.broadcast_to(index[k : k + 1, 1:2], shape))
    return found


def target_band(me, core, pair):
    return jnp.bitwise_xor(me, jnp.where(core == 0, pair[0], pair[1]))


def push_kernel(pairs, columns, i_ref, j_ref, high_ref, corr_ref, t_ref, u_ref, *outs):
    width, rows = corr_ref.shape[2], high_ref.shape[1]
    block = high_ref.shape[0] - width
    x = high_ref[width:]
    me, core = lax.axis_index("rows"), lax.axis_index("sub")
    targets = tile_columns((i_ref, j_ref), (block, rows))
    products = [dot_bf16(x, ref[k], NN) for ref in (t_ref, u_ref) for k in range(ref.shape[0])]

    def pushed(band):
        first = band * columns
        total = jnp.zeros((block, rows), f32)
        for target, product in zip(targets, products):
            inside = (target >= first) & (target < first + columns)
            total = total + jnp.where(inside, product, 0.0)
        return total

    parity = jnp.bitwise_and(me, 1)
    outs[0][...] = jnp.concatenate([pushed(me), corr_ref[parity]], axis=0)
    for ref, pair in zip(outs[1:], pairs):
        products_of = split(pushed(target_band(me, core, pair)))
        message = jnp.concatenate([h.astype(f32) for h in (x, *products_of)], axis=0)
        if pair[0] != pair[1]:
            ref[...] = message.astype(bf16)
        else:
            message = jnp.where(core == 0, message[:, : rows // 2], message[:, rows // 2 :])
            halves = [unfold(h.astype(f32), 2) for h in split(corr_ref[1 - parity])]
            ref[...] = jnp.concatenate([message, *halves], axis=0).astype(bf16)


def image_kernel(pairs, columns, parts, i_ref, j_ref, base_ref, high_ref, low_ref, t_ref, u_ref, own_ref, *refs):
    received, (y_ref, send_ref) = refs[:-2], refs[-2:]
    block, rows = base_ref.shape
    width = high_ref.shape[0] - block
    me, core = lax.axis_index("rows"), lax.axis_index("sub")
    y = base_ref[...] + own_ref[0:block]
    corr = own_ref[block:]
    blocks = [(me, high_ref[width:].astype(f32))]
    for k, pair in enumerate(pairs):
        mine, other = received[2 * k][...].astype(f32), received[2 * k + 1][...].astype(f32)
        if pair[0] != pair[1]:
            found = [(target_band(me, core, pair), mine), (target_band(me, core, pair[::-1]), other)]
        else:
            parts_of = mine[3 * block :]
            count = parts_of.shape[0] // 2
            corr = corr + fold(parts_of[:count] + parts_of[count:], 2)
            mine, other = mine[: 3 * block], other[: 3 * block]
            first, second = jnp.where(core == 0, mine, other), jnp.where(core == 0, other, mine)
            found = [(jnp.bitwise_xor(me, pair[0]), jnp.concatenate([first, second], axis=1))]
        for band, message in found:
            blocks.append((band, message[0:block]))
            y = y + (message[block : 2 * block] + message[2 * block :])
    tiles = [ref[k] for ref in (t_ref, u_ref) for k in range(ref.shape[0])]
    for target, tile in zip(tile_columns((i_ref, j_ref), (block, rows)), tiles):
        source = jnp.zeros((block, rows), f32)
        for band, held in blocks:
            first = band * columns
            inside = (target >= first) & (target < first + columns)
            source = jnp.where(inside, held, source)
        source = source.astype(bf16)
        halves = [dot_bf16(source, tile[k * rows // 2 : (k + 1) * rows // 2], NT) for k in range(2)]
        y = y + jnp.concatenate(halves, axis=1)
    y_ref[...] = y
    halves = split(y)
    diagonal = fold(dot_split(halves, (high_ref[width:], low_ref[width:]), NT), parts)
    stored = dot_split(halves, (high_ref[:width], low_ref[:width]), NT)
    send_ref[...] = jnp.concatenate([stored, diagonal, corr], axis=0)


def pack(total):
    return jnp.concatenate([h.astype(f32) for h in split(total)], axis=0).astype(bf16)


def combine_kernel(mine_ref, other_ref, total_ref, *send_refs):
    total = mine_ref[...] + other_ref[...]
    total_ref[...] = total
    for ref in send_refs:
        ref[...] = pack(total)


def project_kernel(steps, block, parts, total_rows, total_ref, high_ref, low_ref, near_ref, *refs):
    received, (out_ref, diagonal_ref) = refs[:-2], refs[-2:]
    me, core = lax.axis_index("rows"), lax.axis_index("sub")
    small = block // parts
    total = total_ref[...]
    stored, diagonal = total[0:block], total[block : block + small]
    same, other = total[block + small :], jnp.zeros((block // 2, total.shape[1]), f32)
    for step, ref in zip(steps, received):
        message = ref[...].astype(f32)
        message = message[: total.shape[0]] + message[total.shape[0] :]
        stored = stored + message[0:block]
        diagonal = diagonal + message[block : block + small]
        part = message[block + small :]
        if step % 2:
            other = other + part
        else:
            same = same + part
    even = jnp.bitwise_and(me, 1) == 0
    corr = jnp.concatenate([jnp.where(even, same, other), jnp.where(even, other, same)], axis=0)
    scale = 1.0 / total_rows
    diagonal = diagonal * scale
    lane = lax.broadcasted_iota(jnp.int32, diagonal.shape, 1)
    inside = [(lane >= k * block) & (lane < (k + 1) * block) for k in range(parts)]
    spread = jnp.concatenate([jnp.where(k, diagonal, 0.0) for k in inside], axis=0)
    many = [jnp.concatenate([h] * parts, axis=0) for h in split(corr * scale)]
    projection = stored * scale - dot_split(split(spread), many, NN)
    diagonal = unfold(diagonal, parts)
    diagonal_ref[...] = diagonal
    weights = split(jnp.concatenate([projection, jnp.where(core == 0, diagonal, 0.0)], axis=1))
    for k, ref in enumerate((high_ref, near_ref)):
        rounded = dot_bf16(weights[0], ref[...], NN) + dot_bf16(weights[1], ref[...], NN)
        out_ref[k * block : (k + 1) * block, :] = rounded
    out_ref[2 * block :, :] = dot_bf16(weights[0], low_ref[...], NN)


def gram_kernel(mine_ref, other_ref, y_ref, z_ref, images_ref, full_ref, half_ref):
    block = images_ref.shape[0]
    removed = mine_ref[...] + other_ref[...]
    images = y_ref[...] - removed[0:block]
    images_ref[...] = images - removed[2 * block :]
    gram = 0.0
    for x in (images, z_ref[...] - removed[block : 2 * block]):
        halves = split(x)
        twice = [jnp.concatenate([h, h], axis=0) for h in halves]
        gram = gram + dot_stacked(halves, twice, NT)
    left = lax.broadcasted_iota(jnp.int32, full_ref.shape, 1) < block
    gram = jnp.where(left, gram[: block // 2], gram[block // 2 :])
    full_ref[...] = gram
    middle = half_ref.shape[0]
    half_ref[...] = jnp.where(lax.axis_index("sub") == 0, gram[:middle], gram[middle:])


def factor_kernel(pairs, total_rows, own_ref, images_ref, d_ref, *refs):
    received, (following_ref, coupling_ref, diagonal_ref) = refs[:-3], refs[-3:]
    block = images_ref.shape[0]
    lanes = 2 * block
    core = lax.axis_index("sub")
    gram = own_ref[...]
    for k, pair in enumerate(pairs):
        mine, other = received[2 * k][...], received[2 * k + 1][...]
        if pair[0] != pair[1]:
            gram = gram + (mine + other)
        else:
            first, second = jnp.where(core == 0, mine, other), jnp.where(core == 0, other, mine)
            gram = gram + jnp.concatenate([first, second], axis=0)
    gram = gram * (1.0 / total_rows)
    row = lax.broadcasted_iota(jnp.int32, (block, lanes), 0)
    column = lax.broadcasted_iota(jnp.int32, (block, lanes), 1)
    left = column < block
    m = jnp.concatenate([gram, pltpu.roll(gram, block, 1)], axis=0)
    m = jnp.where(left, m, jnp.where(column == row + block, 1.0, 0.0))
    finished = []
    for start in range(0, block, GROUP):
        spread = [
            jnp.broadcast_to(m[:, start + p : start + p + 1], m.shape) for p in range(GROUP)
        ]
        for p in range(GROUP):
            at = p % 8
            root = lax.rsqrt(spread[p][at : at + 1])
            lower = spread[p] * root
            done = m[at : at + 1] * root
            finished.append(done)
            for q in range(p + 1, GROUP):
                pivot = q - p + at
                spread[q] = spread[q] - lower * lower[pivot : pivot + 1]
            m = m - lower * done
            if at == 7:
                m = m[8:]
                spread = [column[8:] for column in spread]
    done = jnp.concatenate(finished, axis=0)
    coupling_ref[...] = jnp.where((row <= column) & left, done, 0.0)[:, 0:block]
    inverse = jnp.where((row + block >= column) & ~left, done, 0.0)
    images = images_ref[...]
    images = jnp.concatenate([images, images], axis=0)
    following_ref[...] = dot_split(split(inverse), split(images), NN)
    diagonal_ref[...] = d_ref[...].T


def exchange(x, axis, distance):
    return lax.ppermute(x, axis, [(i, i ^ distance) for i in range(lax.axis_size(axis))])


def local(
    tile_index,
    tile_values,
    onsite_energy,
    start_block,
    previous_block,
    previous_coupling,
    stored_basis,
):
    rows, block = start_block.shape
    bands, columns = lax.axis_size("rows"), lax.axis_size("cols")
    cores = lax.axis_size("sub")
    stored = stored_basis.shape[0]
    width = stored * block
    total_rows = rows * bands * columns
    parts = width // block
    chunk = block // 2
    assert rows == tile_values.shape[1] and cores == 2 and width == rows
    assert bands > 1 and columns > 1 and bands & (bands - 1) == 0 and columns & (columns - 1) == 0
    half = (block, rows)
    swap = [(0, 1), (1, 0)]
    other_tiles = lax.ppermute(tile_values, "sub", swap)
    other_index = lax.ppermute(tile_index, "sub", swap)
    prepare = call(
        prepare_kernel,
        [
            (half, f32), ((2, chunk, width), f32), *[((width + block, rows), bf16)] * 2,
            (tile_values.shape, bf16), (tile_index.shape, jnp.int32),
        ],
        "hhhhhhh",
        [
            pltpu.VMEM(half, f32), pltpu.VMEM((1, rows), f32), pltpu.VMEM(half, f32),
            pltpu.VMEM((block, block), f32), pltpu.VMEM((width, rows), f32),
            pltpu.SemaphoreType.DMA((7,)),
        ],
    )
    sources = (
        start_block.T, onsite_energy.reshape(1, rows), previous_block.T, previous_coupling,
        stored_basis.transpose(0, 2, 1).reshape(width, rows), tile_values, tile_index,
    )
    base, corr, high, low, tiles, index = prepare(
        *(pltpu.with_memory_space_constraint(a, pltpu.HBM) for a in sources)
    )
    pairs = [(step - 1, step) for step in range(bands - 1, 1, -2)] + [(1, 1)]

    def serve(sends):
        received = []
        for send, pair in zip(sends, pairs):
            moves = [(2 * r + c, 2 * (r ^ pair[c]) + c) for r in range(bands) for c in range(2)]
            received.append(lax.ppermute(send, ("rows", "sub"), moves))
        swapped = []
        for x, pair in zip(received, pairs):
            swapped += [x, lax.ppermute(x, "sub", swap)]
        return swapped

    sends = call(
        functools.partial(push_kernel, pairs, columns),
        [((block + chunk, rows), f32)]
        + [((3 * block, rows) if a != b else (5 * block, rows // 2), bf16) for a, b in pairs],
        "vvvvvv",
    )(index, other_index, high, corr, tiles, other_tiles)
    near = exchange(high, "cols", 1)
    received = serve(sends[1:])
    small = block // parts
    y, mine = call(
        functools.partial(image_kernel, pairs, columns, parts),
        [(half, f32), ((block + small + chunk, rows), f32)],
        "v" * (8 + len(received)),
    )(index, other_index, base, high, low, tiles, other_tiles, sends[0], *received)
    other = exchange(mine, "cols", 1)
    late = exchange(y, "cols", 1)
    distances = [2**k for k in range(1, columns.bit_length() - 1)]
    total, *send = call(
        combine_kernel,
        [((block + small + chunk, rows), f32)]
        + [((2 * (block + small + chunk), rows), bf16)] * (not distances),
        "vv",
    )(mine, other)
    for distance in distances:
        total = total + exchange(total, "cols", distance)
    send = send[0] if send else pack(total)
    steps = [*range(2, bands), 1]
    received = []
    for step in steps:
        received.append(exchange(send, "rows", step))
    project = call(
        functools.partial(project_kernel, steps, block, parts, total_rows),
        [((3 * block, rows), f32), ((block, block), f32)],
        "v" * (3 + bands),
    )
    removed, diagonal = project(total, high, low, near, *received)
    images, full, part = call(
        gram_kernel,
        [(half, f32), ((block // 2, 2 * block), f32), ((block // 4, 2 * block), f32)],
        "vvvv",
    )(removed, lax.ppermute(removed, "sub", swap), y, late)
    for distance in distances:
        full = full + exchange(full, "cols", distance)
        middle = part.shape[0]
        part = jnp.where(lax.axis_index("sub") == 0, full[:middle], full[middle:])
    following, coupling, diagonal = call(
        functools.partial(factor_kernel, pairs, total_rows),
        [(half, f32), ((block, block), f32), ((block, block), f32)],
        "v" * (3 + 2 * len(pairs)),
    )(full, images, diagonal, *serve([full] * (len(pairs) - 1) + [part]))
    return following.T[None], diagonal[None], coupling[None]


def solution(mesh):
    return jax.shard_map(
        local,
        mesh=mesh,
        in_specs=(
            P(("groups", "rows", "cols", "sub"), None),
            P(("groups", "rows", "cols", "sub"), None, None),
            P(("groups", "rows", "cols")),
            P(("groups", "rows", "cols"), None),
            P(("groups", "rows", "cols"), None),
            P("groups", None),
            P("sub", ("groups", "rows", "cols"), None),
        ),
        out_specs=(
            P(None, ("groups", "rows", "cols"), None),
            P(None, "groups", None),
            P(None, "groups", None),
        ),
        check_vma=False,
    )
```

```python
import functools

import jax
import jax.numpy as jnp
from jax import lax
from jax.experimental import pallas as pl
from jax.experimental.pallas import tpu as pltpu
from jax.sharding import PartitionSpec as P

f32 = jnp.float32
bf16 = jnp.bfloat16
GROUP = 16
GRANT = 16 * 1024 * 1024
NN = (((1,), (0,)), ((), ()))
NT = (((1,), (1,)), ((), ()))


def split(x):
    high = x.astype(bf16)
    return high, (x - high.astype(f32)).astype(bf16)


def dot_bf16(a, b, dims):
    return lax.dot_general(a, b, dims, preferred_element_type=f32)


def dot_split(a, b, dims):
    (ah, al), (bh, bl) = a, b
    return dot_bf16(ah, bh, dims) + dot_bf16(ah, bl, dims) + dot_bf16(al, bh, dims)


def dot_stacked(a, b, dims):
    (ah, al), (bh, bl) = a, b
    rows = ah.shape[0]
    both = dot_bf16(jnp.concatenate([ah, al], axis=0), bh, dims)
    return both[:rows] + both[rows:] + dot_bf16(ah, bl, dims)


def fold(x, parts):
    rows = x.shape[0] // parts
    return jnp.concatenate([x[i * rows : (i + 1) * rows] for i in range(parts)], axis=1)


def unfold(x, parts):
    lanes = x.shape[1] // parts
    return jnp.concatenate([x[:, i * lanes : (i + 1) * lanes] for i in range(parts)], axis=0)


def call(kernel, outs, ins, scratch=(), work=40000000):
    spaces = {"v": pltpu.VMEM, "h": pltpu.HBM}
    return pl.pallas_call(
        kernel,
        out_shape=[jax.ShapeDtypeStruct(s, d) for s, d in outs],
        in_specs=[pl.BlockSpec(memory_space=spaces[c]) for c in ins],
        out_specs=[pl.BlockSpec(memory_space=pltpu.VMEM)] * len(outs),
        scratch_shapes=list(scratch),
        cost_estimate=pl.CostEstimate(flops=work, bytes_accessed=1000000, transcendentals=0),
        compiler_params=pltpu.CompilerParams(vmem_limit_bytes=GRANT),
    )


def prepare_kernel(
    x_hbm, e_hbm, p_hbm, c_hbm, s_hbm, t_hbm, i_hbm,
    base_ref, high_ref, low_ref, t_ref, i_ref,
    x_ref, e_ref, p_ref, c_ref, s_ref, sems,
):
    pairs = (
        (s_hbm, s_ref), (x_hbm, x_ref), (p_hbm, p_ref), (c_hbm, c_ref),
        (e_hbm, e_ref), (t_hbm, t_ref), (i_hbm, i_ref),
    )
    copies = [pltpu.make_async_copy(a, b, sems.at[k]) for k, (a, b) in enumerate(pairs)]
    for copy in copies:
        copy.start()
    for copy in copies[:5]:
        copy.wait()
    block = x_ref.shape[0]
    row = lax.broadcasted_iota(jnp.int32, (block, block), 0)
    column = lax.broadcasted_iota(jnp.int32, (block, block), 1)
    coupling = jnp.where(row <= column, c_ref[...], 0.0)
    x = x_ref[...]
    xs = split(x)
    ss = split(s_ref[...])
    base_ref[...] = e_ref[...] * x - dot_stacked(split(coupling), split(p_ref[...]), NN)
    corr = split(dot_stacked(xs, ss, NT))
    high_ref[...] = jnp.concatenate([ss[0], xs[0], *corr], axis=0)
    low_ref[...] = jnp.concatenate([ss[1], xs[1]], axis=0)
    for copy in copies[5:]:
        copy.wait()


def tile_columns(index_refs, shape):
    found = []
    for ref in index_refs:
        index = ref[...]
        for k in range(ref.shape[0]):
            found.append(jnp.broadcast_to(index[k : k + 1, 1:2], shape))
    return found


def target_band(me, core, pair):
    return jnp.bitwise_xor(me, jnp.where(core == 0, pair[0], pair[1]))


def push_kernel(pairs, columns, i_ref, j_ref, high_ref, t_ref, u_ref, *outs):
    block, rows = outs[0].shape
    width = high_ref.shape[0] - 3 * block
    x = high_ref[width : width + block]
    me, core = lax.axis_index("rows"), lax.axis_index("sub")
    targets = tile_columns((i_ref, j_ref), (block, rows))
    products = [dot_bf16(x, ref[k], NN) for ref in (t_ref, u_ref) for k in range(ref.shape[0])]

    def pushed(band):
        first = band * columns
        total = jnp.zeros((block, rows), f32)
        for target, product in zip(targets, products):
            inside = (target >= first) & (target < first + columns)
            total = total + jnp.where(inside, product, 0.0)
        return total

    outs[0][...] = pushed(me)
    for ref, pair in zip(outs[1:], pairs):
        message = jnp.concatenate([x.astype(f32), pushed(target_band(me, core, pair))], axis=0)
        if pair[0] == pair[1]:
            message = jnp.where(core == 0, message[:, : rows // 2], message[:, rows // 2 :])
        ref[...] = message.astype(bf16)


def image_kernel(pairs, columns, parts, i_ref, j_ref, base_ref, high_ref, low_ref, near_ref, t_ref, u_ref, own_ref, *refs):
    received, (y_ref, send_ref, corr_ref, part_ref) = refs[:-4], refs[-4:]
    block, rows = base_ref.shape
    width = low_ref.shape[0] - block
    me, core = lax.axis_index("rows"), lax.axis_index("sub")
    y = base_ref[...] + own_ref[...]
    halves = [r[k : k + block].astype(f32) for r in (high_ref, near_ref) for k in (width + block, width + 2 * block)]
    corr = (halves[0] + halves[1]) + (halves[2] + halves[3])
    corr_ref[...] = corr
    part_ref[...] = corr.astype(bf16)
    blocks = [(me, high_ref[width : width + block].astype(f32))]
    for k, pair in enumerate(pairs):
        mine, other = received[2 * k][...].astype(f32), received[2 * k + 1][...].astype(f32)
        if pair[0] != pair[1]:
            found = [(target_band(me, core, pair), mine), (target_band(me, core, pair[::-1]), other)]
        else:
            first, second = jnp.where(core == 0, mine, other), jnp.where(core == 0, other, mine)
            found = [(jnp.bitwise_xor(me, pair[0]), jnp.concatenate([first, second], axis=1))]
        for band, message in found:
            blocks.append((band, message[0:block]))
            y = y + message[block:]
    tiles = [ref[k] for ref in (t_ref, u_ref) for k in range(ref.shape[0])]
    for target, tile in zip(tile_columns((i_ref, j_ref), (block, rows)), tiles):
        source = jnp.zeros((block, rows), f32)
        for band, held in blocks:
            first = band * columns
            inside = (target >= first) & (target < first + columns)
            source = jnp.where(inside, held, source)
        source = source.astype(bf16)
        halves = [dot_bf16(source, tile[k * rows // 2 : (k + 1) * rows // 2], NT) for k in range(2)]
        y = y + jnp.concatenate(halves, axis=1)
    y_ref[...] = y
    halves = split(y)
    diagonal = fold(dot_split(halves, (high_ref[width : width + block], low_ref[width:]), NT), parts)
    stored = dot_split(halves, (high_ref[:width], low_ref[:width]), NT)
    send_ref[...] = jnp.concatenate([stored, diagonal], axis=0)


def pack(total, block):
    high, low = split(total[block:])
    message = [total[0:block], high.astype(f32), low.astype(f32)]
    return jnp.concatenate(message, axis=0).astype(bf16)


def combine_kernel(block, mine_ref, other_ref, total_ref, *send_refs):
    total = mine_ref[...] + other_ref[...]
    total_ref[...] = total
    for ref in send_refs:
        ref[...] = pack(total, block)


def project_kernel(block, parts, total_rows, total_ref, corr_ref, high_ref, low_ref, near_ref, *refs):
    received, (out_ref, diagonal_ref) = refs[:-2], refs[-2:]
    core = lax.axis_index("sub")
    count = len(received) // 2
    small = block // parts
    corr = corr_ref[...]
    for ref in received[count:]:
        corr = corr + ref[...].astype(f32)
    total = total_ref[...]
    stored, diagonal = total[0:block], total[block:]
    for ref in received[:count]:
        message = ref[...].astype(f32)
        stored = stored + message[0:block]
        diagonal = diagonal + (message[block : block + small] + message[block + small :])
    scale = 1.0 / total_rows
    diagonal = diagonal * scale
    lane = lax.broadcasted_iota(jnp.int32, diagonal.shape, 1)
    inside = [(lane >= k * block) & (lane < (k + 1) * block) for k in range(parts)]
    spread = jnp.concatenate([jnp.where(k, diagonal, 0.0) for k in inside], axis=0)
    many = [jnp.concatenate([h] * parts, axis=0) for h in split(corr * scale)]
    projection = stored * scale - dot_split(split(spread), many, NN)
    diagonal = unfold(diagonal, parts)
    diagonal_ref[...] = diagonal
    weights = split(jnp.concatenate([projection, jnp.where(core == 0, diagonal, 0.0)], axis=1))
    for k, ref in enumerate((high_ref, near_ref)):
        stacked = ref[: low_ref.shape[0]]
        rounded = dot_bf16(weights[0], stacked, NN) + dot_bf16(weights[1], stacked, NN)
        out_ref[k * block : (k + 1) * block, :] = rounded
    out_ref[2 * block :, :] = dot_bf16(weights[0], low_ref[...], NN)


def gram_kernel(mine_ref, other_ref, y_ref, z_ref, images_ref, full_ref, half_ref):
    block = images_ref.shape[0]
    removed = mine_ref[...] + other_ref[...]
    images = y_ref[...] - removed[0:block]
    images_ref[...] = images - removed[2 * block :]
    gram = 0.0
    for x in (images, z_ref[...] - removed[block : 2 * block]):
        halves = split(x)
        twice = [jnp.concatenate([h, h], axis=0) for h in halves]
        gram = gram + dot_stacked(halves, twice, NT)
    left = lax.broadcasted_iota(jnp.int32, full_ref.shape, 1) < block
    gram = jnp.where(left, gram[: block // 2], gram[block // 2 :])
    full_ref[...] = gram
    middle = half_ref.shape[0]
    half_ref[...] = jnp.where(lax.axis_index("sub") == 0, gram[:middle], gram[middle:])


def factor_kernel(pairs, total_rows, own_ref, images_ref, d_ref, *refs):
    received, (following_ref, coupling_ref, diagonal_ref) = refs[:-3], refs[-3:]
    block = images_ref.shape[0]
    lanes = 2 * block
    core = lax.axis_index("sub")
    gram = own_ref[...]
    for k, pair in enumerate(pairs):
        mine, other = received[2 * k][...], received[2 * k + 1][...]
        if pair[0] != pair[1]:
            gram = gram + (mine + other)
        else:
            first, second = jnp.where(core == 0, mine, other), jnp.where(core == 0, other, mine)
            gram = gram + jnp.concatenate([first, second], axis=0)
    gram = gram * (1.0 / total_rows)
    row = lax.broadcasted_iota(jnp.int32, (block, lanes), 0)
    column = lax.broadcasted_iota(jnp.int32, (block, lanes), 1)
    left = column < block
    m = jnp.concatenate([gram, pltpu.roll(gram, block, 1)], axis=0)
    m = jnp.where(left, m, jnp.where(column == row + block, 1.0, 0.0))
    finished = []
    for start in range(0, block, GROUP):
        spread = [
            jnp.broadcast_to(m[:, start + p : start + p + 1], m.shape) for p in range(GROUP)
        ]
        for p in range(GROUP):
            at = p % 8
            root = lax.rsqrt(spread[p][at : at + 1])
            lower = spread[p] * root
            done = m[at : at + 1] * root
            finished.append(done)
            for q in range(p + 1, GROUP):
                pivot = q - p + at
                spread[q] = spread[q] - lower * lower[pivot : pivot + 1]
            m = m - lower * done
            if at == 7:
                m = m[8:]
                spread = [column[8:] for column in spread]
    done = jnp.concatenate(finished, axis=0)
    coupling_ref[...] = jnp.where((row <= column) & left, done, 0.0)[:, 0:block]
    inverse = jnp.where((row + block >= column) & ~left, done, 0.0)
    images = images_ref[...]
    images = jnp.concatenate([images, images], axis=0)
    following_ref[...] = dot_split(split(inverse), split(images), NN)
    diagonal_ref[...] = d_ref[...].T


def exchange(x, axis, distance):
    return lax.ppermute(x, axis, [(i, i ^ distance) for i in range(lax.axis_size(axis))])


def local(
    tile_index,
    tile_values,
    onsite_energy,
    start_block,
    previous_block,
    previous_coupling,
    stored_basis,
):
    rows, block = start_block.shape
    bands, columns = lax.axis_size("rows"), lax.axis_size("cols")
    cores = lax.axis_size("sub")
    stored = stored_basis.shape[0]
    width = stored * block
    total_rows = rows * bands * columns
    parts = width // block
    assert rows == tile_values.shape[1] and cores == 2 and width == rows
    assert bands > 1 and columns > 1 and bands & (bands - 1) == 0 and columns & (columns - 1) == 0
    half = (block, rows)
    swap = [(0, 1), (1, 0)]
    other_tiles = lax.ppermute(tile_values, "sub", swap)
    other_index = lax.ppermute(tile_index, "sub", swap)
    prepare = call(
        prepare_kernel,
        [
            (half, f32), ((width + 3 * block, rows), bf16), ((width + block, rows), bf16),
            (tile_values.shape, bf16), (tile_index.shape, jnp.int32),
        ],
        "hhhhhhh",
        [
            pltpu.VMEM(half, f32), pltpu.VMEM((1, rows), f32), pltpu.VMEM(half, f32),
            pltpu.VMEM((block, block), f32), pltpu.VMEM((width, rows), f32),
            pltpu.SemaphoreType.DMA((7,)),
        ],
    )
    sources = (
        start_block.T, onsite_energy.reshape(1, rows), previous_block.T, previous_coupling,
        stored_basis.transpose(0, 2, 1).reshape(width, rows), tile_values, tile_index,
    )
    base, high, low, tiles, index = prepare(
        *(pltpu.with_memory_space_constraint(a, pltpu.HBM) for a in sources)
    )
    pairs = [(step - 1, step) for step in range(bands - 1, 1, -2)] + [(1, 1)]

    def serve(sends):
        received = []
        for send, pair in zip(sends, pairs):
            moves = [(2 * r + c, 2 * (r ^ pair[c]) + c) for r in range(bands) for c in range(2)]
            received.append(lax.ppermute(send, ("rows", "sub"), moves))
        swapped = []
        for x, pair in zip(received, pairs):
            swapped += [x, lax.ppermute(x, "sub", swap)]
        return swapped

    sends = call(
        functools.partial(push_kernel, pairs, columns),
        [(half, f32)] + [((2 * block, rows if a != b else rows // 2), bf16) for a, b in pairs],
        "vvvvv",
    )(index, other_index, high, tiles, other_tiles)
    near = exchange(high, "cols", 1)
    received = serve(sends[1:])
    small = block // parts
    y, mine, corr, part = call(
        functools.partial(image_kernel, pairs, columns, parts),
        [(half, f32), ((block + small, rows), f32), (half, f32), (half, bf16)],
        "v" * (9 + len(received)),
    )(index, other_index, base, high, low, near, tiles, other_tiles, sends[0], *received)
    other = exchange(mine, "cols", 1)
    late = exchange(y, "cols", 1)
    distances = [2**k for k in range(1, columns.bit_length() - 1)]
    total, *send = call(
        functools.partial(combine_kernel, block),
        [((block + small, rows), f32)]
        + [((block + 2 * small, rows), bf16)] * (not distances),
        "vv",
    )(mine, other)
    for distance in distances:
        total = total + exchange(total, "cols", distance)
        corr = corr + exchange(corr, "cols", distance)
        part = corr.astype(bf16)
    send = send[0] if send else pack(total, block)
    steps = [*range(2, bands), 1]
    received = []
    for message in (send, part):
        for step in steps:
            received.append(exchange(message, "rows", step))
    project = call(
        functools.partial(project_kernel, block, parts, total_rows),
        [((3 * block, rows), f32), ((block, block), f32)],
        "v" * (5 + len(received)),
    )
    removed, diagonal = project(total, corr, high, low, near, *received)
    images, full, part = call(
        gram_kernel,
        [(half, f32), ((block // 2, 2 * block), f32), ((block // 4, 2 * block), f32)],
        "vvvv",
    )(removed, lax.ppermute(removed, "sub", swap), y, late)
    for distance in distances:
        full = full + exchange(full, "cols", distance)
        middle = part.shape[0]
        part = jnp.where(lax.axis_index("sub") == 0, full[:middle], full[middle:])
    following, coupling, diagonal = call(
        functools.partial(factor_kernel, pairs, total_rows),
        [(half, f32), ((block, block), f32), ((block, block), f32)],
        "v" * (3 + 2 * len(pairs)),
    )(full, images, diagonal, *serve([full] * (len(pairs) - 1) + [part]))
    return following.T[None], diagonal[None], coupling[None]


def solution(mesh):
    return jax.shard_map(
        local,
        mesh=mesh,
        in_specs=(
            P(("groups", "rows", "cols", "sub"), None),
            P(("groups", "rows", "cols", "sub"), None, None),
            P(("groups", "rows", "cols")),
            P(("groups", "rows", "cols"), None),
            P(("groups", "rows", "cols"), None),
            P("groups", None),
            P("sub", ("groups", "rows", "cols"), None),
        ),
        out_specs=(
            P(None, ("groups", "rows", "cols"), None),
            P(None, "groups", None),
            P(None, "groups", None),
        ),
        check_vma=False,
    )
```

```python
import functools

import jax
import jax.numpy as jnp
from jax import lax
from jax.experimental import pallas as pl
from jax.experimental.pallas import tpu as pltpu
from jax.sharding import PartitionSpec as P

f32 = jnp.float32
bf16 = jnp.bfloat16
GROUP = 16
GRANT = 16 * 1024 * 1024
NN = (((1,), (0,)), ((), ()))
NT = (((1,), (1,)), ((), ()))


def split(x):
    high = x.astype(bf16)
    return high, (x - high.astype(f32)).astype(bf16)


def dot_bf16(a, b, dims):
    return lax.dot_general(a, b, dims, preferred_element_type=f32)


def dot_split(a, b, dims):
    (ah, al), (bh, bl) = a, b
    return dot_bf16(ah, bh, dims) + dot_bf16(ah, bl, dims) + dot_bf16(al, bh, dims)


def dot_stacked(a, b, dims):
    (ah, al), (bh, bl) = a, b
    rows = ah.shape[0]
    both = dot_bf16(jnp.concatenate([ah, al], axis=0), bh, dims)
    return both[:rows] + both[rows:] + dot_bf16(ah, bl, dims)


def fold(x, parts):
    rows = x.shape[0] // parts
    return jnp.concatenate([x[i * rows : (i + 1) * rows] for i in range(parts)], axis=1)


def unfold(x, parts):
    lanes = x.shape[1] // parts
    return jnp.concatenate([x[:, i * lanes : (i + 1) * lanes] for i in range(parts)], axis=0)


def call(kernel, outs, ins, scratch=(), work=40000000):
    spaces = {"v": pltpu.VMEM, "h": pltpu.HBM}
    return pl.pallas_call(
        kernel,
        out_shape=[jax.ShapeDtypeStruct(s, d) for s, d in outs],
        in_specs=[pl.BlockSpec(memory_space=spaces[c]) for c in ins],
        out_specs=[pl.BlockSpec(memory_space=pltpu.VMEM)] * len(outs),
        scratch_shapes=list(scratch),
        cost_estimate=pl.CostEstimate(flops=work, bytes_accessed=1000000, transcendentals=0),
        compiler_params=pltpu.CompilerParams(vmem_limit_bytes=GRANT),
    )


def prepare_kernel(
    x_hbm, e_hbm, p_hbm, c_hbm, s_hbm, t_hbm, i_hbm,
    base_ref, high_ref, low_ref, t_ref, i_ref,
    x_ref, e_ref, p_ref, c_ref, s_ref, sems,
):
    pairs = (
        (s_hbm, s_ref), (x_hbm, x_ref), (p_hbm, p_ref), (c_hbm, c_ref),
        (e_hbm, e_ref), (t_hbm, t_ref), (i_hbm, i_ref),
    )
    copies = [pltpu.make_async_copy(a, b, sems.at[k]) for k, (a, b) in enumerate(pairs)]
    for copy in copies:
        copy.start()
    for copy in copies[:5]:
        copy.wait()
    block = x_ref.shape[0]
    row = lax.broadcasted_iota(jnp.int32, (block, block), 0)
    column = lax.broadcasted_iota(jnp.int32, (block, block), 1)
    coupling = jnp.where(row <= column, c_ref[...], 0.0)
    x = x_ref[...]
    xs = split(x)
    ss = split(s_ref[...])
    base_ref[...] = e_ref[...] * x - dot_stacked(split(coupling), split(p_ref[...]), NN)
    corr = split(dot_stacked(xs, ss, NT))
    high_ref[...] = jnp.concatenate([ss[0], xs[0], *corr], axis=0)
    low_ref[...] = jnp.concatenate([ss[1], xs[1]], axis=0)
    for copy in copies[5:]:
        copy.wait()


def tile_columns(index_refs, shape):
    found = []
    for ref in index_refs:
        index = ref[...]
        for k in range(ref.shape[0]):
            found.append(jnp.broadcast_to(index[k : k + 1, 1:2], shape))
    return found


def target_band(me, core, pair):
    return jnp.bitwise_xor(me, jnp.where(core == 0, pair[0], pair[1]))


def push_kernel(pairs, columns, i_ref, j_ref, high_ref, t_ref, u_ref, *outs):
    block, rows = outs[0].shape
    width = high_ref.shape[0] - 3 * block
    x = high_ref[width : width + block]
    me, core = lax.axis_index("rows"), lax.axis_index("sub")
    targets = tile_columns((i_ref, j_ref), (block, rows))
    products = [dot_bf16(x, ref[k], NN) for ref in (t_ref, u_ref) for k in range(ref.shape[0])]

    def pushed(band):
        first = band * columns
        total = jnp.zeros((block, rows), f32)
        for target, product in zip(targets, products):
            inside = (target >= first) & (target < first + columns)
            total = total + jnp.where(inside, product, 0.0)
        return total

    outs[0][...] = pushed(me)
    for ref, pair in zip(outs[1:], pairs):
        message = jnp.concatenate([x.astype(f32), pushed(target_band(me, core, pair))], axis=0)
        if pair[0] == pair[1]:
            message = jnp.where(core == 0, message[:, : rows // 2], message[:, rows // 2 :])
        ref[...] = message.astype(bf16)


def image_kernel(pairs, columns, parts, i_ref, j_ref, base_ref, high_ref, low_ref, t_ref, u_ref, own_ref, *refs):
    received, (y_ref, send_ref) = refs[:-2], refs[-2:]
    block, rows = base_ref.shape
    width = low_ref.shape[0] - block
    me, core = lax.axis_index("rows"), lax.axis_index("sub")
    y = base_ref[...] + own_ref[...]
    blocks = [(me, high_ref[width : width + block].astype(f32))]
    for k, pair in enumerate(pairs):
        mine, other = received[2 * k][...].astype(f32), received[2 * k + 1][...].astype(f32)
        if pair[0] != pair[1]:
            found = [(target_band(me, core, pair), mine), (target_band(me, core, pair[::-1]), other)]
        else:
            first, second = jnp.where(core == 0, mine, other), jnp.where(core == 0, other, mine)
            found = [(jnp.bitwise_xor(me, pair[0]), jnp.concatenate([first, second], axis=1))]
        for band, message in found:
            blocks.append((band, message[0:block]))
            y = y + message[block:]
    tiles = [ref[k] for ref in (t_ref, u_ref) for k in range(ref.shape[0])]
    for target, tile in zip(tile_columns((i_ref, j_ref), (block, rows)), tiles):
        source = jnp.zeros((block, rows), f32)
        for band, held in blocks:
            first = band * columns
            inside = (target >= first) & (target < first + columns)
            source = jnp.where(inside, held, source)
        source = source.astype(bf16)
        halves = [dot_bf16(source, tile[k * rows // 2 : (k + 1) * rows // 2], NT) for k in range(2)]
        y = y + jnp.concatenate(halves, axis=1)
    y_ref[...] = y
    halves = split(y)
    diagonal = fold(dot_split(halves, (high_ref[width : width + block], low_ref[width:]), NT), parts)
    stored = dot_split(halves, (high_ref[:width], low_ref[:width]), NT)
    send_ref[...] = jnp.concatenate([stored, diagonal], axis=0)


def stored_kernel(high_ref, near_ref, corr_ref, part_ref):
    block = corr_ref.shape[0]
    start = high_ref.shape[0] - 2 * block
    corr = 0.0
    for ref in (high_ref, near_ref):
        halves = ref[start:].astype(f32)
        corr = corr + (halves[:block] + halves[block:])
    corr_ref[...] = corr
    part_ref[...] = corr.astype(bf16)


def pack(total, block):
    high, low = split(total[block:])
    message = [total[0:block], high.astype(f32), low.astype(f32)]
    return jnp.concatenate(message, axis=0).astype(bf16)


def combine_kernel(block, mine_ref, other_ref, total_ref, *send_refs):
    total = mine_ref[...] + other_ref[...]
    total_ref[...] = total
    for ref in send_refs:
        ref[...] = pack(total, block)


def project_kernel(block, parts, total_rows, total_ref, corr_ref, high_ref, low_ref, near_ref, *refs):
    received, (out_ref, diagonal_ref) = refs[:-2], refs[-2:]
    core = lax.axis_index("sub")
    count = len(received) // 2
    small = block // parts
    corr = corr_ref[...]
    for ref in received[count:]:
        corr = corr + ref[...].astype(f32)
    total = total_ref[...]
    stored, diagonal = total[0:block], total[block:]
    for ref in received[:count]:
        message = ref[...].astype(f32)
        stored = stored + message[0:block]
        diagonal = diagonal + (message[block : block + small] + message[block + small :])
    scale = 1.0 / total_rows
    diagonal = diagonal * scale
    lane = lax.broadcasted_iota(jnp.int32, diagonal.shape, 1)
    inside = [(lane >= k * block) & (lane < (k + 1) * block) for k in range(parts)]
    spread = jnp.concatenate([jnp.where(k, diagonal, 0.0) for k in inside], axis=0)
    many = [jnp.concatenate([h] * parts, axis=0) for h in split(corr * scale)]
    projection = stored * scale - dot_split(split(spread), many, NN)
    diagonal = unfold(diagonal, parts)
    diagonal_ref[...] = diagonal
    weights = split(jnp.concatenate([projection, jnp.where(core == 0, diagonal, 0.0)], axis=1))
    for k, ref in enumerate((high_ref, near_ref)):
        stacked = ref[: low_ref.shape[0]]
        rounded = dot_bf16(weights[0], stacked, NN) + dot_bf16(weights[1], stacked, NN)
        out_ref[k * block : (k + 1) * block, :] = rounded
    out_ref[2 * block :, :] = dot_bf16(weights[0], low_ref[...], NN)


def gram_kernel(mine_ref, other_ref, y_ref, z_ref, images_ref, full_ref, half_ref):
    block = images_ref.shape[0]
    removed = mine_ref[...] + other_ref[...]
    images = y_ref[...] - removed[0:block]
    images_ref[...] = images - removed[2 * block :]
    gram = 0.0
    for x in (images, z_ref[...] - removed[block : 2 * block]):
        halves = split(x)
        twice = [jnp.concatenate([h, h], axis=0) for h in halves]
        gram = gram + dot_stacked(halves, twice, NT)
    left = lax.broadcasted_iota(jnp.int32, full_ref.shape, 1) < block
    gram = jnp.where(left, gram[: block // 2], gram[block // 2 :])
    full_ref[...] = gram
    middle = half_ref.shape[0]
    half_ref[...] = jnp.where(lax.axis_index("sub") == 0, gram[:middle], gram[middle:])


def factor_kernel(pairs, total_rows, own_ref, images_ref, d_ref, *refs):
    received, (following_ref, coupling_ref, diagonal_ref) = refs[:-3], refs[-3:]
    block = images_ref.shape[0]
    lanes = 2 * block
    core = lax.axis_index("sub")
    gram = own_ref[...]
    for k, pair in enumerate(pairs):
        mine, other = received[2 * k][...], received[2 * k + 1][...]
        if pair[0] != pair[1]:
            gram = gram + (mine + other)
        else:
            first, second = jnp.where(core == 0, mine, other), jnp.where(core == 0, other, mine)
            gram = gram + jnp.concatenate([first, second], axis=0)
    gram = gram * (1.0 / total_rows)
    row = lax.broadcasted_iota(jnp.int32, (block, lanes), 0)
    column = lax.broadcasted_iota(jnp.int32, (block, lanes), 1)
    left = column < block
    m = jnp.concatenate([gram, pltpu.roll(gram, block, 1)], axis=0)
    m = jnp.where(left, m, jnp.where(column == row + block, 1.0, 0.0))
    finished = []
    for start in range(0, block, GROUP):
        spread = [
            jnp.broadcast_to(m[:, start + p : start + p + 1], m.shape) for p in range(GROUP)
        ]
        for p in range(GROUP):
            at = p % 8
            root = lax.rsqrt(spread[p][at : at + 1])
            lower = spread[p] * root
            done = m[at : at + 1] * root
            finished.append(done)
            for q in range(p + 1, GROUP):
                pivot = q - p + at
                spread[q] = spread[q] - lower * lower[pivot : pivot + 1]
            m = m - lower * done
            if at == 7:
                m = m[8:]
                spread = [column[8:] for column in spread]
    done = jnp.concatenate(finished, axis=0)
    coupling_ref[...] = jnp.where((row <= column) & left, done, 0.0)[:, 0:block]
    inverse = jnp.where((row + block >= column) & ~left, done, 0.0)
    images = images_ref[...]
    images = jnp.concatenate([images, images], axis=0)
    following_ref[...] = dot_split(split(inverse), split(images), NN)
    diagonal_ref[...] = d_ref[...].T


def exchange(x, axis, distance):
    return lax.ppermute(x, axis, [(i, i ^ distance) for i in range(lax.axis_size(axis))])


def local(
    tile_index,
    tile_values,
    onsite_energy,
    start_block,
    previous_block,
    previous_coupling,
    stored_basis,
):
    rows, block = start_block.shape
    bands, columns = lax.axis_size("rows"), lax.axis_size("cols")
    cores = lax.axis_size("sub")
    stored = stored_basis.shape[0]
    width = stored * block
    total_rows = rows * bands * columns
    parts = width // block
    assert rows == tile_values.shape[1] and cores == 2 and width == rows
    assert bands > 1 and columns > 1 and bands & (bands - 1) == 0 and columns & (columns - 1) == 0
    half = (block, rows)
    swap = [(0, 1), (1, 0)]
    other_tiles = lax.ppermute(tile_values, "sub", swap)
    other_index = lax.ppermute(tile_index, "sub", swap)
    prepare = call(
        prepare_kernel,
        [
            (half, f32), ((width + 3 * block, rows), bf16), ((width + block, rows), bf16),
            (tile_values.shape, bf16), (tile_index.shape, jnp.int32),
        ],
        "hhhhhhh",
        [
            pltpu.VMEM(half, f32), pltpu.VMEM((1, rows), f32), pltpu.VMEM(half, f32),
            pltpu.VMEM((block, block), f32), pltpu.VMEM((width, rows), f32),
            pltpu.SemaphoreType.DMA((7,)),
        ],
    )
    sources = (
        start_block.T, onsite_energy.reshape(1, rows), previous_block.T, previous_coupling,
        stored_basis.transpose(0, 2, 1).reshape(width, rows), tile_values, tile_index,
    )
    base, high, low, tiles, index = prepare(
        *(pltpu.with_memory_space_constraint(a, pltpu.HBM) for a in sources)
    )
    pairs = [(step - 1, step) for step in range(bands - 1, 1, -2)] + [(1, 1)]

    def serve(sends):
        received = []
        for send, pair in zip(sends, pairs):
            moves = [(2 * r + c, 2 * (r ^ pair[c]) + c) for r in range(bands) for c in range(2)]
            received.append(lax.ppermute(send, ("rows", "sub"), moves))
        swapped = []
        for x, pair in zip(received, pairs):
            swapped += [x, lax.ppermute(x, "sub", swap)]
        return swapped

    sends = call(
        functools.partial(push_kernel, pairs, columns),
        [(half, f32)] + [((2 * block, rows if a != b else rows // 2), bf16) for a, b in pairs],
        "vvvvv",
    )(index, other_index, high, tiles, other_tiles)
    near = exchange(high, "cols", 1)
    received = serve(sends[1:])
    small = block // parts
    y, mine = call(
        functools.partial(image_kernel, pairs, columns, parts),
        [(half, f32), ((block + small, rows), f32)],
        "v" * (8 + len(received)),
    )(index, other_index, base, high, low, tiles, other_tiles, sends[0], *received)
    sum_stored = call(stored_kernel, [(half, f32), (half, bf16)], "vv")
    corr, part = sum_stored(high, near)
    other = exchange(mine, "cols", 1)
    late = exchange(y, "cols", 1)
    distances = [2**k for k in range(1, columns.bit_length() - 1)]
    total, *send = call(
        functools.partial(combine_kernel, block),
        [((block + small, rows), f32)]
        + [((block + 2 * small, rows), bf16)] * (not distances),
        "vv",
    )(mine, other)
    for distance in distances:
        total = total + exchange(total, "cols", distance)
        corr = corr + exchange(corr, "cols", distance)
        part = corr.astype(bf16)
    send = send[0] if send else pack(total, block)
    steps = [*range(2, bands), 1]
    received = []
    for message in (send, part):
        for step in steps:
            received.append(exchange(message, "rows", step))
    project = call(
        functools.partial(project_kernel, block, parts, total_rows),
        [((3 * block, rows), f32), ((block, block), f32)],
        "v" * (5 + len(received)),
    )
    removed, diagonal = project(total, corr, high, low, near, *received)
    images, full, part = call(
        gram_kernel,
        [(half, f32), ((block // 2, 2 * block), f32), ((block // 4, 2 * block), f32)],
        "vvvv",
    )(removed, lax.ppermute(removed, "sub", swap), y, late)
    for distance in distances:
        full = full + exchange(full, "cols", distance)
        middle = part.shape[0]
        part = jnp.where(lax.axis_index("sub") == 0, full[:middle], full[middle:])
    following, coupling, diagonal = call(
        functools.partial(factor_kernel, pairs, total_rows),
        [(half, f32), ((block, block), f32), ((block, block), f32)],
        "v" * (3 + 2 * len(pairs)),
    )(full, images, diagonal, *serve([full] * (len(pairs) - 1) + [part]))
    return following.T[None], diagonal[None], coupling[None]


def solution(mesh):
    return jax.shard_map(
        local,
        mesh=mesh,
        in_specs=(
            P(("groups", "rows", "cols", "sub"), None),
            P(("groups", "rows", "cols", "sub"), None, None),
            P(("groups", "rows", "cols")),
            P(("groups", "rows", "cols"), None),
            P(("groups", "rows", "cols"), None),
            P("groups", None),
            P("sub", ("groups", "rows", "cols"), None),
        ),
        out_specs=(
            P(None, ("groups", "rows", "cols"), None),
            P(None, "groups", None),
            P(None, "groups", None),
        ),
        check_vma=False,
    )
```

```python
import functools

import jax
import jax.numpy as jnp
from jax import lax
from jax.experimental import pallas as pl
from jax.experimental.pallas import tpu as pltpu
from jax.sharding import PartitionSpec as P

f32 = jnp.float32
bf16 = jnp.bfloat16
GROUP = 16
GRANT = 16 * 1024 * 1024
NN = (((1,), (0,)), ((), ()))
NT = (((1,), (1,)), ((), ()))


def split(x):
    high = x.astype(bf16)
    return high, (x - high.astype(f32)).astype(bf16)


def dot_bf16(a, b, dims):
    return lax.dot_general(a, b, dims, preferred_element_type=f32)


def dot_split(a, b, dims):
    (ah, al), (bh, bl) = a, b
    return dot_bf16(ah, bh, dims) + dot_bf16(ah, bl, dims) + dot_bf16(al, bh, dims)


def dot_stacked(a, b, dims):
    (ah, al), (bh, bl) = a, b
    rows = ah.shape[0]
    both = dot_bf16(jnp.concatenate([ah, al], axis=0), bh, dims)
    return both[:rows] + both[rows:] + dot_bf16(ah, bl, dims)


def fold(x, parts):
    rows = x.shape[0] // parts
    return jnp.concatenate([x[i * rows : (i + 1) * rows] for i in range(parts)], axis=1)


def unfold(x, parts):
    lanes = x.shape[1] // parts
    return jnp.concatenate([x[:, i * lanes : (i + 1) * lanes] for i in range(parts)], axis=0)


def call(kernel, outs, ins, scratch=(), work=40000000):
    spaces = {"v": pltpu.VMEM, "h": pltpu.HBM}
    return pl.pallas_call(
        kernel,
        out_shape=[jax.ShapeDtypeStruct(s, d) for s, d in outs],
        in_specs=[pl.BlockSpec(memory_space=spaces[c]) for c in ins],
        out_specs=[pl.BlockSpec(memory_space=pltpu.VMEM)] * len(outs),
        scratch_shapes=list(scratch),
        cost_estimate=pl.CostEstimate(flops=work, bytes_accessed=1000000, transcendentals=0),
        compiler_params=pltpu.CompilerParams(vmem_limit_bytes=GRANT),
    )


def prepare_kernel(
    x_hbm, e_hbm, p_hbm, c_hbm, s_hbm, t_hbm, i_hbm,
    base_ref, corr_ref, high_ref, low_ref, t_ref, i_ref,
    x_ref, e_ref, p_ref, c_ref, s_ref, sems,
):
    pairs = (
        (s_hbm, s_ref), (x_hbm, x_ref), (p_hbm, p_ref), (c_hbm, c_ref),
        (e_hbm, e_ref), (t_hbm, t_ref), (i_hbm, i_ref),
    )
    copies = [pltpu.make_async_copy(a, b, sems.at[k]) for k, (a, b) in enumerate(pairs)]
    for copy in copies:
        copy.start()
    for copy in copies[:5]:
        copy.wait()
    block = x_ref.shape[0]
    row = lax.broadcasted_iota(jnp.int32, (block, block), 0)
    column = lax.broadcasted_iota(jnp.int32, (block, block), 1)
    coupling = jnp.where(row <= column, c_ref[...], 0.0)
    x = x_ref[...]
    xs = split(x)
    ss = split(s_ref[...])
    for k, ref in enumerate((high_ref, low_ref)):
        ref[...] = jnp.concatenate([ss[k], xs[k]], axis=0)
    base_ref[...] = e_ref[...] * x - dot_stacked(split(coupling), split(p_ref[...]), NN)
    corr = dot_stacked(xs, ss, NT)
    chunk = corr_ref.shape[1]
    for band in range(corr_ref.shape[0]):
        corr_ref[band] = corr[band * chunk : (band + 1) * chunk]
    for copy in copies[5:]:
        copy.wait()


def tile_columns(index_refs, shape):
    found = []
    for ref in index_refs:
        index = ref[...]
        for k in range(ref.shape[0]):
            found.append(jnp.broadcast_to(index[k : k + 1, 1:2], shape))
    return found


def target_band(me, core, pair):
    return jnp.bitwise_xor(me, jnp.where(core == 0, pair[0], pair[1]))


def push_kernel(pairs, columns, i_ref, j_ref, high_ref, corr_ref, t_ref, u_ref, *outs):
    width, rows = corr_ref.shape[2], high_ref.shape[1]
    block = high_ref.shape[0] - width
    x = high_ref[width:]
    me, core = lax.axis_index("rows"), lax.axis_index("sub")
    targets = tile_columns((i_ref, j_ref), (block, rows))
    products = [dot_bf16(x, ref[k], NN) for ref in (t_ref, u_ref) for k in range(ref.shape[0])]

    def pushed(band):
        first = band * columns
        total = jnp.zeros((block, rows), f32)
        for target, product in zip(targets, products):
            inside = (target >= first) & (target < first + columns)
            total = total + jnp.where(inside, product, 0.0)
        return total

    parity = jnp.bitwise_and(me, 1)
    outs[0][...] = jnp.concatenate([pushed(me), corr_ref[parity]], axis=0)
    for ref, pair in zip(outs[1:], pairs):
        products_of = split(pushed(target_band(me, core, pair)))
        message = jnp.concatenate([h.astype(f32) for h in (x, *products_of)], axis=0)
        if pair[0] != pair[1]:
            ref[...] = message.astype(bf16)
        else:
            message = jnp.where(core == 0, message[:, : rows // 2], message[:, rows // 2 :])
            halves = [unfold(h.astype(f32), 2) for h in split(corr_ref[1 - parity])]
            ref[...] = jnp.concatenate([message, *halves], axis=0).astype(bf16)


def image_kernel(pairs, columns, parts, i_ref, j_ref, base_ref, high_ref, low_ref, t_ref, u_ref, own_ref, *refs):
    received, (y_ref, send_ref) = refs[:-2], refs[-2:]
    block, rows = base_ref.shape
    width = high_ref.shape[0] - block
    me, core = lax.axis_index("rows"), lax.axis_index("sub")
    y = base_ref[...] + own_ref[0:block]
    corr = own_ref[block:]
    blocks = [(me, high_ref[width:].astype(f32))]
    for k, pair in enumerate(pairs):
        mine, other = received[2 * k][...].astype(f32), received[2 * k + 1][...].astype(f32)
        if pair[0] != pair[1]:
            found = [(target_band(me, core, pair), mine), (target_band(me, core, pair[::-1]), other)]
        else:
            parts_of = mine[3 * block :]
            count = parts_of.shape[0] // 2
            corr = corr + fold(parts_of[:count] + parts_of[count:], 2)
            mine, other = mine[: 3 * block], other[: 3 * block]
            first, second = jnp.where(core == 0, mine, other), jnp.where(core == 0, other, mine)
            found = [(jnp.bitwise_xor(me, pair[0]), jnp.concatenate([first, second], axis=1))]
        for band, message in found:
            blocks.append((band, message[0:block]))
            y = y + (message[block : 2 * block] + message[2 * block :])
    tiles = [ref[k] for ref in (t_ref, u_ref) for k in range(ref.shape[0])]
    for target, tile in zip(tile_columns((i_ref, j_ref), (block, rows)), tiles):
        source = jnp.zeros((block, rows), f32)
        for band, held in blocks:
            first = band * columns
            inside = (target >= first) & (target < first + columns)
            source = jnp.where(inside, held, source)
        source = source.astype(bf16)
        halves = [dot_bf16(source, tile[k * rows // 2 : (k + 1) * rows // 2], NT) for k in range(2)]
        y = y + jnp.concatenate(halves, axis=1)
    y_ref[...] = y
    halves = split(y)
    diagonal = fold(dot_split(halves, (high_ref[width:], low_ref[width:]), NT), parts)
    stored = dot_split(halves, (high_ref[:width], low_ref[:width]), NT)
    send_ref[...] = jnp.concatenate([stored, diagonal, corr], axis=0)


def pack(total, block, small):
    high, low = split(total[block : block + small])
    message = [total[0:block], high.astype(f32), low.astype(f32), total[block + small :]]
    return jnp.concatenate(message, axis=0).astype(bf16)


def combine_kernel(block, small, mine_ref, other_ref, total_ref, *send_refs):
    total = mine_ref[...] + other_ref[...]
    total_ref[...] = total
    for ref in send_refs:
        ref[...] = pack(total, block, small)


def project_kernel(steps, block, parts, total_rows, total_ref, high_ref, low_ref, near_ref, *refs):
    received, (out_ref, diagonal_ref) = refs[:-2], refs[-2:]
    me, core = lax.axis_index("rows"), lax.axis_index("sub")
    small = block // parts
    total = total_ref[...]
    stored, diagonal = total[0:block], total[block : block + small]
    same, other = total[block + small :], jnp.zeros((block // 2, total.shape[1]), f32)
    for step, ref in zip(steps, received):
        message = ref[...].astype(f32)
        stored = stored + message[0:block]
        diagonal = diagonal + message[block : block + small]
        diagonal = diagonal + message[block + small : block + 2 * small]
        part = message[block + 2 * small :]
        if step % 2:
            other = other + part
        else:
            same = same + part
    even = jnp.bitwise_and(me, 1) == 0
    corr = jnp.concatenate([jnp.where(even, same, other), jnp.where(even, other, same)], axis=0)
    scale = 1.0 / total_rows
    diagonal = diagonal * scale
    lane = lax.broadcasted_iota(jnp.int32, diagonal.shape, 1)
    inside = [(lane >= k * block) & (lane < (k + 1) * block) for k in range(parts)]
    spread = jnp.concatenate([jnp.where(k, diagonal, 0.0) for k in inside], axis=0)
    many = [jnp.concatenate([h] * parts, axis=0) for h in split(corr * scale)]
    projection = stored * scale - dot_split(split(spread), many, NN)
    diagonal = unfold(diagonal, parts)
    diagonal_ref[...] = diagonal
    weights = split(jnp.concatenate([projection, jnp.where(core == 0, diagonal, 0.0)], axis=1))
    for k, ref in enumerate((high_ref, near_ref)):
        rounded = dot_bf16(weights[0], ref[...], NN) + dot_bf16(weights[1], ref[...], NN)
        out_ref[k * block : (k + 1) * block, :] = rounded
    out_ref[2 * block :, :] = dot_bf16(weights[0], low_ref[...], NN)


def gram_kernel(mine_ref, other_ref, y_ref, z_ref, images_ref, full_ref, half_ref):
    block = images_ref.shape[0]
    removed = mine_ref[...] + other_ref[...]
    images = y_ref[...] - removed[0:block]
    images_ref[...] = images - removed[2 * block :]
    gram = 0.0
    for x in (images, z_ref[...] - removed[block : 2 * block]):
        halves = split(x)
        twice = [jnp.concatenate([h, h], axis=0) for h in halves]
        gram = gram + dot_stacked(halves, twice, NT)
    left = lax.broadcasted_iota(jnp.int32, full_ref.shape, 1) < block
    gram = jnp.where(left, gram[: block // 2], gram[block // 2 :])
    full_ref[...] = gram
    middle = half_ref.shape[0]
    half_ref[...] = jnp.where(lax.axis_index("sub") == 0, gram[:middle], gram[middle:])


def factor_kernel(pairs, total_rows, own_ref, images_ref, d_ref, *refs):
    received, (following_ref, coupling_ref, diagonal_ref) = refs[:-3], refs[-3:]
    block = images_ref.shape[0]
    lanes = 2 * block
    core = lax.axis_index("sub")
    gram = own_ref[...]
    for k, pair in enumerate(pairs):
        mine, other = received[2 * k][...], received[2 * k + 1][...]
        if pair[0] != pair[1]:
            gram = gram + (mine + other)
        else:
            first, second = jnp.where(core == 0, mine, other), jnp.where(core == 0, other, mine)
            gram = gram + jnp.concatenate([first, second], axis=0)
    gram = gram * (1.0 / total_rows)
    row = lax.broadcasted_iota(jnp.int32, (block, lanes), 0)
    column = lax.broadcasted_iota(jnp.int32, (block, lanes), 1)
    left = column < block
    m = jnp.concatenate([gram, pltpu.roll(gram, block, 1)], axis=0)
    m = jnp.where(left, m, jnp.where(column == row + block, 1.0, 0.0))
    finished = []
    for start in range(0, block, GROUP):
        spread = [
            jnp.broadcast_to(m[:, start + p : start + p + 1], m.shape) for p in range(GROUP)
        ]
        for p in range(GROUP):
            at = p % 8
            root = lax.rsqrt(spread[p][at : at + 1])
            lower = spread[p] * root
            done = m[at : at + 1] * root
            finished.append(done)
            for q in range(p + 1, GROUP):
                pivot = q - p + at
                spread[q] = spread[q] - lower * lower[pivot : pivot + 1]
            m = m - lower * done
            if at == 7:
                m = m[8:]
                spread = [column[8:] for column in spread]
    done = jnp.concatenate(finished, axis=0)
    coupling_ref[...] = jnp.where((row <= column) & left, done, 0.0)[:, 0:block]
    inverse = jnp.where((row + block >= column) & ~left, done, 0.0)
    images = images_ref[...]
    images = jnp.concatenate([images, images], axis=0)
    following_ref[...] = dot_split(split(inverse), split(images), NN)
    diagonal_ref[...] = d_ref[...].T


def exchange(x, axis, distance):
    return lax.ppermute(x, axis, [(i, i ^ distance) for i in range(lax.axis_size(axis))])


def local(
    tile_index,
    tile_values,
    onsite_energy,
    start_block,
    previous_block,
    previous_coupling,
    stored_basis,
):
    rows, block = start_block.shape
    bands, columns = lax.axis_size("rows"), lax.axis_size("cols")
    cores = lax.axis_size("sub")
    stored = stored_basis.shape[0]
    width = stored * block
    total_rows = rows * bands * columns
    parts = width // block
    chunk = block // 2
    assert rows == tile_values.shape[1] and cores == 2 and width == rows
    assert bands > 1 and columns > 1 and bands & (bands - 1) == 0 and columns & (columns - 1) == 0
    half = (block, rows)
    swap = [(0, 1), (1, 0)]
    other_tiles = lax.ppermute(tile_values, "sub", swap)
    other_index = lax.ppermute(tile_index, "sub", swap)
    prepare = call(
        prepare_kernel,
        [
            (half, f32), ((2, chunk, width), f32), *[((width + block, rows), bf16)] * 2,
            (tile_values.shape, bf16), (tile_index.shape, jnp.int32),
        ],
        "hhhhhhh",
        [
            pltpu.VMEM(half, f32), pltpu.VMEM((1, rows), f32), pltpu.VMEM(half, f32),
            pltpu.VMEM((block, block), f32), pltpu.VMEM((width, rows), f32),
            pltpu.SemaphoreType.DMA((7,)),
        ],
    )
    sources = (
        start_block.T, onsite_energy.reshape(1, rows), previous_block.T, previous_coupling,
        stored_basis.transpose(0, 2, 1).reshape(width, rows), tile_values, tile_index,
    )
    base, corr, high, low, tiles, index = prepare(
        *(pltpu.with_memory_space_constraint(a, pltpu.HBM) for a in sources)
    )
    pairs = [(step - 1, step) for step in range(bands - 1, 1, -2)] + [(1, 1)]

    def serve(sends):
        received = []
        for send, pair in zip(sends, pairs):
            moves = [(2 * r + c, 2 * (r ^ pair[c]) + c) for r in range(bands) for c in range(2)]
            received.append(lax.ppermute(send, ("rows", "sub"), moves))
        swapped = []
        for x, pair in zip(received, pairs):
            swapped += [x, lax.ppermute(x, "sub", swap)]
        return swapped

    sends = call(
        functools.partial(push_kernel, pairs, columns),
        [((block + chunk, rows), f32)]
        + [((3 * block, rows) if a != b else (5 * block, rows // 2), bf16) for a, b in pairs],
        "vvvvvv",
    )(index, other_index, high, corr, tiles, other_tiles)
    near = exchange(high, "cols", 1)
    received = serve(sends[1:])
    small = block // parts
    y, mine = call(
        functools.partial(image_kernel, pairs, columns, parts),
        [(half, f32), ((block + small + chunk, rows), f32)],
        "v" * (8 + len(received)),
    )(index, other_index, base, high, low, tiles, other_tiles, sends[0], *received)
    other = exchange(mine, "cols", 1)
    late = exchange(y, "cols", 1)
    distances = [2**k for k in range(1, columns.bit_length() - 1)]
    total, *send = call(
        functools.partial(combine_kernel, block, small),
        [((block + small + chunk, rows), f32)]
        + [((block + 2 * small + chunk, rows), bf16)] * (not distances),
        "vv",
    )(mine, other)
    for distance in distances:
        total = total + exchange(total, "cols", distance)
    send = send[0] if send else pack(total, block, small)
    steps = [*range(2, bands), 1]
    received = []
    for step in steps:
        received.append(exchange(send, "rows", step))
    project = call(
        functools.partial(project_kernel, steps, block, parts, total_rows),
        [((3 * block, rows), f32), ((block, block), f32)],
        "v" * (3 + bands),
    )
    removed, diagonal = project(total, high, low, near, *received)
    images, full, part = call(
        gram_kernel,
        [(half, f32), ((block // 2, 2 * block), f32), ((block // 4, 2 * block), f32)],
        "vvvv",
    )(removed, lax.ppermute(removed, "sub", swap), y, late)
    for distance in distances:
        full = full + exchange(full, "cols", distance)
        middle = part.shape[0]
        part = jnp.where(lax.axis_index("sub") == 0, full[:middle], full[middle:])
    following, coupling, diagonal = call(
        functools.partial(factor_kernel, pairs, total_rows),
        [(half, f32), ((block, block), f32), ((block, block), f32)],
        "v" * (3 + 2 * len(pairs)),
    )(full, images, diagonal, *serve([full] * (len(pairs) - 1) + [part]))
    return following.T[None], diagonal[None], coupling[None]


def solution(mesh):
    return jax.shard_map(
        local,
        mesh=mesh,
        in_specs=(
            P(("groups", "rows", "cols", "sub"), None),
            P(("groups", "rows", "cols", "sub"), None, None),
            P(("groups", "rows", "cols")),
            P(("groups", "rows", "cols"), None),
            P(("groups", "rows", "cols"), None),
            P("groups", None),
            P("sub", ("groups", "rows", "cols"), None),
        ),
        out_specs=(
            P(None, ("groups", "rows", "cols"), None),
            P(None, "groups", None),
            P(None, "groups", None),
        ),
        check_vma=False,
    )
```
